256 devices in a mesh: chain: 32 (over z_lo, x, core), dp: 8 (over z_hi, y).
Axes of the slice: x: 4, y: 4, z: 8 (z_hi: 2, z_lo: 4; z = z_hi * 4 + z_lo), core: 2. Of those that a mesh axis runs over, the one named last changes fastest.
Arguments:
- segments: bfloat16 [8, 32, 128, 1024], P('dp', 'chain'), may hold values from -6 to 6
- lengths: int32 [8, 32], P('dp', 'chain'), may hold values from 64 to 128, as said below
- query_weight: bfloat16 [1024, 1024], replicated, may hold values from -0.1875 to 0.1875
- key_weight: bfloat16 [1024, 256], replicated, may hold values from -0.1875 to 0.1875
- value_weight: bfloat16 [1024, 256], replicated, may hold values from -0.1875 to 0.1875
- out_weight: bfloat16 [1024, 1024], replicated, may hold values from -0.1875 to 0.1875
- norm_gain: float32 [1024], replicated, may hold values from 0.5 to 1.5
- gate_vector: float32 [1024], replicated, may hold values from -0.6 to 0.6
- gate_bias: float32 [128], replicated, may hold values from -2 to 5
- memory_init: bfloat16 [128, 1024], replicated, may hold values from -6 to 6
- cotangent: bfloat16 [8, 32, 128, 1024], P('dp', 'chain'), may hold values from -6 to 6
Outputs:
- layer_output: bfloat16 [8, 32, 128, 1024], P('dp', 'chain')
- grad_query: float32 [1024, 1024], P(('chain', 'dp'))
- grad_key: float32 [1024, 256], P(('chain', 'dp'))
- grad_value: float32 [1024, 256], P(('chain', 'dp'))
- grad_out: float32 [1024, 1024], P(('chain', 'dp'))
- grad_gain: float32 [1024], P(('chain', 'dp'))
- grad_gate: float32 [1024], P(('chain', 'dp'))
- grad_memory: float32 [128, 1024], P(None, ('chain', 'dp'))
The draws below stay inside these ranges and needn't reach their ends.
Inputs may be any that keep to these rules, and one draw needn't show every extreme that they name: `lengths`: in every document one segment is full.
All inputs are finite; a program needn't handle non-finite values.
Results may differ from the reference program's by a relative error of at most 0.02.
Values sent between devices are 32-bit elements; how exact they have to be, the bound alone decides.
A program may use at most 128 MiB of HBM per device.

```python
import jax
import jax.numpy as jnp
from jax import lax

D = 1024
HEAD = 64
QHEADS = 16
KVHEADS = 4
MEM = 128
SEG = 128
DOCS = 8
SEGS = 32


def draw_lengths(key, part):
    base = jax.random.randint(key, (DOCS, SEGS), SEG // 2, SEG + 1)
    chosen = jax.random.randint(jax.random.fold_in(key, 7), (DOCS, 1), 0, SEGS)
    return jnp.where(jnp.arange(SEGS)[None, :] == chosen, SEG, base).astype(jnp.int32)


def spiked(entries, key, source, target, shards_of, factor):
    def block_of(position):
        return (jnp.arange(entries.shape[position]) // (entries.shape[position] // shards_of)).reshape((-1,) + (1,) * (entries.ndim - 1 - position))

    one_side = jax.random.permutation(key, shards_of)[block_of(target)]
    second = (block_of(target) + shards_of // 2) % shards_of
    return jnp.where((block_of(source) == one_side) | (block_of(source) == second), factor * entries, entries)


def steps_of(rng, dims, split, least, largest):
    gain = 1.0
    for axis_at, blocks in split:
        heights = jax.random.uniform(jax.random.fold_in(jax.random.fold_in(rng, 6), axis_at), (blocks,), jnp.float32, least / len(split), largest / len(split))
        gain = gain * jnp.repeat(jnp.exp(heights), dims[axis_at] // blocks).reshape((-1,) + (1,) * (len(dims) - 1 - axis_at))
    return gain


def noise(key, shape, scale, most, split=(), kind=jnp.bfloat16):
    gain = steps_of(key, shape, split, -0.22, 0.18) if split else 1.0
    array = jax.random.normal(key, shape, jnp.float32) * scale * gain
    return jnp.minimum(jnp.maximum(array, -most), most).astype(kind)


def noise_with(key, shape, scale, reach, split, heavy, held_as=jnp.bfloat16):
    drawn = scale * jax.random.normal(key, shape, jnp.float32)
    if split:
        drawn = drawn * steps_of(key, shape, split, -0.22, 0.18)
    return jnp.clip(spiked(drawn, jax.random.fold_in(key, 3), *heavy), -reach, reach).astype(held_as)


def setup_inputs(seed: int = 0) -> dict:
    streams_of = jax.random.split(jax.random.key(seed), 12)
    return {
        "segments": noise_with(streams_of[0], (DOCS, SEGS, SEG, D), 1.0, 6.0, ((0, 8), (1, 32)), (1, 3, 32, 2.75)),
        "lengths": draw_lengths(jax.random.fold_in(streams_of[11], 71), 0),
        "query_weight": noise(streams_of[2], (D, QHEADS * HEAD), D ** -0.5, 0.1875),
        "key_weight": noise(streams_of[3], (D, KVHEADS * HEAD), D ** -0.5, 0.1875),
        "value_weight": noise(streams_of[4], (D, KVHEADS * HEAD), D ** -0.5, 0.1875),
        "out_weight": noise(streams_of[5], (QHEADS * HEAD, D), (QHEADS * HEAD) ** -0.5, 0.1875),
        "norm_gain": jnp.clip(1.0 + 0.1 * jax.random.normal(streams_of[6], (D,), jnp.float32), 0.5, 1.5),
        "gate_vector": noise(streams_of[7], (D,), 0.1, 0.6, (), jnp.float32),
        "gate_bias": jnp.clip(jax.random.uniform(streams_of[8], (MEM,), jnp.float32, -2.0, 5.0), -2.0, 5.0),
        "memory_init": noise(streams_of[9], (MEM, D), 1.0, 6.0),
        "cotangent": noise_with(streams_of[10], (DOCS, SEGS, SEG, D), 1.0, 6.0, ((0, 8), (1, 32)), (1, 3, 32, 2.75)),
    }


epsilon = 1e-05
score_scale = 0.125

def normalize(activations, norm_gain):
    inverse = lax.rsqrt(lax.optimization_barrier(jnp.mean(activations * activations, axis=-1, keepdims=True)) + epsilon)
    return (activations * inverse * norm_gain).astype(jnp.bfloat16)

def prepare(query_weight, key_weight, value_weight, norm_gain, segment):
    normed_rows = normalize(segment.astype(jnp.float32), norm_gain)
    queries = (jnp.dot(normed_rows, query_weight, preferred_element_type=jnp.float32) * score_scale).astype(jnp.bfloat16)
    key_rows = jnp.dot(normed_rows, key_weight, preferred_element_type=jnp.float32).astype(jnp.bfloat16)
    value_rows = jnp.dot(normed_rows, value_weight, preferred_element_type=jnp.float32).astype(jnp.bfloat16)
    return (queries, key_rows, value_rows)

def attend(queries, key_rows, value_rows, allowed):
    count = queries.shape[0]
    width = key_rows.shape[0]
    groups = key_rows.shape[1] // HEAD
    shared = queries.shape[1] // key_rows.shape[1]
    grouped = queries.reshape(count, groups, shared, HEAD)
    keyed = key_rows.reshape(width, groups, HEAD)
    valued = value_rows.reshape(width, groups, HEAD)
    scores = jnp.einsum('rgsh,kgh->gsrk', grouped, keyed, preferred_element_type=jnp.float32)
    scores = jnp.where(allowed, scores, -1e+30)
    weights = jax.nn.softmax(scores, axis=-1).astype(jnp.bfloat16)
    context = jnp.einsum('gsrk,kgh->rgsh', weights, valued, preferred_element_type=jnp.float32)
    return context.reshape(count, groups * shared * HEAD).astype(jnp.bfloat16)

def read_part(queries, seg_keys, seg_values, key_weight, value_weight, out_weight, norm_gain, memory_in, segment, seg_length):
    memory_rows = normalize(memory_in, norm_gain)
    memory_keys = jnp.dot(memory_rows, key_weight, preferred_element_type=jnp.float32).astype(jnp.bfloat16)
    memory_values = jnp.dot(memory_rows, value_weight, preferred_element_type=jnp.float32).astype(jnp.bfloat16)
    key_rows = jnp.concatenate([memory_keys, seg_keys], axis=0)
    value_rows = jnp.concatenate([memory_values, seg_values], axis=0)
    count = segment.shape[0]
    places = jnp.arange(count)
    causal = (places[None, :] <= places[:, None]) & (places[None, :] < seg_length)
    allowed = jnp.concatenate([jnp.ones((count, memory_in.shape[0]), dtype=bool), causal], axis=1)
    context = attend(queries, key_rows, value_rows, allowed)
    return segment.astype(jnp.float32) + jnp.dot(context, out_weight, preferred_element_type=jnp.float32)

def write_part(seg_keys, seg_values, query_weight, out_weight, norm_gain, gate_vector, memory_start, gate_bias, seg_length):
    start_rows = normalize(memory_start, norm_gain)
    slot_queries = (jnp.dot(start_rows, query_weight, preferred_element_type=jnp.float32) * score_scale).astype(jnp.bfloat16)
    places = jnp.arange(seg_keys.shape[0])
    allowed = jnp.broadcast_to(places[None, :] < seg_length, (memory_start.shape[0], seg_keys.shape[0]))
    context = attend(slot_queries, seg_keys, seg_values, allowed)
    written = jnp.dot(context, out_weight, preferred_element_type=jnp.float32)
    retain = jax.nn.sigmoid(gate_bias + jnp.dot(written, gate_vector, precision=lax.Precision.HIGHEST))
    return (retain, written)

def reference(segments, lengths, query_weight, key_weight, value_weight, out_weight, norm_gain, gate_vector, gate_bias, memory_init, cotangent):
    memory_start = memory_init.astype(jnp.float32)

    def document(bundle):
        seg_rows, seg_lengths, seg_cotangents = bundle

        def forward_write(paired):
            segment, seg_length = paired
            queries, seg_keys, seg_values = prepare(query_weight, key_weight, value_weight, norm_gain, segment)
            return write_part(seg_keys, seg_values, query_weight, out_weight, norm_gain, gate_vector, memory_start, gate_bias, seg_length)
        retain_all, written_all = lax.map(forward_write, (seg_rows, seg_lengths))

        def advance(memory, paired):
            retain, written = paired
            return (retain[:, None] * memory + (1.0 - retain)[:, None] * written, memory)
        unused, memory_all = lax.scan(advance, memory_start, (retain_all, written_all))

        def backward_read(bundle_in):
            segment, seg_length, memory_in, seg_cot = bundle_in
            queries, seg_keys, seg_values = prepare(query_weight, key_weight, value_weight, norm_gain, segment)

            def reading(queries_in, keys_in, values_in, key_part, value_part, out_part, gain_part, memory_part):
                return read_part(queries_in, keys_in, values_in, key_part, value_part, out_part, gain_part, memory_part, segment, seg_length)
            result, read_back = jax.vjp(reading, queries, seg_keys, seg_values, key_weight, value_weight, out_weight, norm_gain, memory_in)
            valid_rows = (jnp.arange(segment.shape[0]) < seg_length)[:, None]
            gradients = read_back(seg_cot.astype(jnp.float32) * valid_rows)
            return (result.astype(jnp.bfloat16),) + tuple(gradients)
        read_out = lax.map(backward_read, (seg_rows, seg_lengths, memory_all, seg_cotangents))
        layer_out, d_queries, d_keys_read, d_values_read, key_read, value_read, out_read, gain_read, d_memory = read_out

        def upstream(later_grad, paired):
            retain, local_grad = paired
            return (local_grad + retain[:, None] * later_grad, later_grad)
        anchor_grad, later_all = lax.scan(upstream, jnp.zeros_like(memory_start), (retain_all, d_memory), reverse=True)

        def backward_write(totals, bundle_in):
            segment, seg_length, memory_in, retain, written, later_grad, dq_in, dk_in, dv_in = bundle_in

            def prepared(query_part, key_part, value_part, gain_part):
                return prepare(query_part, key_part, value_part, gain_part, segment)
            (queries, seg_keys, seg_values), prep_back = jax.vjp(prepared, query_weight, key_weight, value_weight, norm_gain)

            def writing(keys_in, values_in, query_part, out_part, gain_part, vector_part, start_part):
                return write_part(keys_in, values_in, query_part, out_part, gain_part, vector_part, start_part, gate_bias, seg_length)
            unused_pair, write_back = jax.vjp(writing, seg_keys, seg_values, query_weight, out_weight, norm_gain, gate_vector, memory_start)
            d_retain = lax.optimization_barrier(jnp.sum(later_grad * (memory_in - written), axis=1))
            d_written = (1.0 - retain)[:, None] * later_grad
            d_keys_write, d_values_write, query_write, out_write, gain_write, gate_grad, start_grad = write_back((d_retain, d_written))
            d_keys = (dk_in.astype(jnp.float32) + d_keys_write.astype(jnp.float32)).astype(jnp.bfloat16)
            d_values = (dv_in.astype(jnp.float32) + d_values_write.astype(jnp.float32)).astype(jnp.bfloat16)
            query_prep, key_prep, value_prep, gain_prep = prep_back((dq_in, d_keys, d_values))
            updates = (query_write.astype(jnp.float32) + query_prep.astype(jnp.float32), key_prep.astype(jnp.float32), value_prep.astype(jnp.float32), out_write.astype(jnp.float32), gain_write + gain_prep, gate_grad, start_grad)
            return (tuple((total + update for total, update in zip(totals, updates))), None)
        zeros_init = (jnp.zeros(query_weight.shape, jnp.float32), jnp.zeros(key_weight.shape, jnp.float32), jnp.zeros(value_weight.shape, jnp.float32), jnp.zeros(out_weight.shape, jnp.float32), jnp.zeros(norm_gain.shape, jnp.float32), jnp.zeros(gate_vector.shape, jnp.float32), jnp.zeros(memory_start.shape, jnp.float32))
        totals, unused_rows = lax.scan(backward_write, zeros_init, (seg_rows, seg_lengths, memory_all, retain_all, written_all, later_all, d_queries, d_keys_read, d_values_read))
        grads = (totals[0], totals[1] + lax.optimization_barrier(jnp.sum(key_read.astype(jnp.float32), axis=0)), totals[2] + lax.optimization_barrier(jnp.sum(value_read.astype(jnp.float32), axis=0)), totals[3] + lax.optimization_barrier(jnp.sum(out_read.astype(jnp.float32), axis=0)), totals[4] + lax.optimization_barrier(jnp.sum(gain_read, axis=0)), totals[5], totals[6] + anchor_grad)
        return (layer_out,) + grads
    results = lax.map(document, (segments, lengths, cotangent))
    sums = tuple((lax.optimization_barrier(jnp.sum(item, axis=0)) for item in results[1:]))
    return (results[0], sums[0], sums[1], sums[2], sums[3], sums[4], sums[5], sums[6])
```

```python
import functools

import jax
import jax.numpy as jnp
from jax import lax
from jax.experimental import pallas as pl
from jax.experimental.pallas import tpu as pltpu
from jax.sharding import Mesh
from jax.sharding import PartitionSpec as P

HEAD = 64
AXES = ("zl", "x", "c", "zh", "y")
MESH = pl.DeviceIdType.MESH
VMEM_SPEC = pl.BlockSpec(memory_space=pltpu.VMEM)


def z_shift(step):
    place = lax.rem(lax.axis_index("zh") * 4 + lax.axis_index("zl") + step, 8)
    return {"zh": lax.div(place, 4), "zl": lax.rem(place, 4)}


def shift(axis, step):
    if axis == "z":
        return z_shift(step % 8)
    return {axis: lax.rem(lax.axis_index(axis) + step % 4, 4)}


def place_of(axis):
    return lax.axis_index("zl" if axis == "z" else axis)


def remote(source, target, send, receive, device):
    return pltpu.make_async_remote_copy(
        src_ref=source,
        dst_ref=target,
        send_sem=send,
        recv_sem=receive,
        device_id=device,
        device_id_type=MESH,
    )


def greet(devices):
    barrier = pltpu.get_barrier_semaphore()
    for device in devices:
        pl.semaphore_signal(barrier, inc=1, device_id=device, device_id_type=MESH)
    pl.semaphore_wait(barrier, len(devices))


class Ring:
    def __init__(self, axis, work, landing, out, send, receive):
        self.work, self.landing, self.out = work, landing, out
        self.send, self.receive = send, receive
        self.me = place_of(axis)
        self.up, self.down = shift(axis, 1), shift(axis, -1)
        self.copies = []

    def at(self, step):
        return lax.rem(self.me + step, 4)

    def push(self, half, step, device):
        slot = len(self.copies)
        copy = remote(
            self.work.at[half, self.at(step)],
            self.landing.at[slot],
            self.send.at[slot],
            self.receive.at[slot],
            device,
        )
        copy.start()
        self.copies.append(copy)

    def first(self):
        self.push(0, 2, self.up)
        self.push(1, 2, self.down)
        self.push(1, 1, self.up)
        self.push(0, 3, self.down)

    def second(self):
        for half, step, device in ((0, 1, self.up), (1, 3, self.down)):
            self.copies[half].wait_recv()
            self.work[half, self.at(step)] += self.landing[half]
            self.push(half, step, device)

    def finish(self):
        for slot in range(2, 6):
            self.copies[slot].wait_recv()
        self.out[0] = self.work[0, self.me] + self.landing[3] + self.landing[4]
        self.out[1] = self.work[1, self.me] + self.landing[2] + self.landing[5]

    def drain(self):
        for copy in self.copies:
            copy.wait_send()


ORDERS = (("x", "y", "z"), ("y", "z", "x"), ("z", "x", "y"))
WIDTHS = ((1024,), (1024,), (256, 256, 256))
TOTAL = 2816


def sum_kernel(*refs):
    inputs, refs = refs[:5], refs[5:]
    out_ref, refs = refs[0], refs[1:]
    landed, refs = refs[:5], refs[5:]
    works, refs = refs[:3], refs[3:]
    rings_of, refs = refs[:18], refs[18:]
    sent, mate, fold_in, core_send, core_receive, ring_send, ring_receive, fold_sems = refs
    core = lax.axis_index("c")
    other = {"c": 1 - core}
    far = z_shift(4)
    greet(
        [other, far]
        + [shift(axis, step) for axis in ("x", "y", "z") for step in (1, -1)]
    )
    core_copies = []
    for k in range(5):
        copy = remote(
            inputs[k].at[:, 1 - core], landed[k], core_send.at[k], core_receive.at[k], other
        )
        copy.start()
        core_copies.append(copy)
    rings = []
    k = 0
    for part in range(3):
        order = ORDERS[part]
        work = works[part]
        half_width = sum(WIDTHS[part]) // 2
        members = []
        start = 0
        for width in WIDTHS[part]:
            members.append((k, width, start))
            core_copies[k].wait_recv()
            k += 1
            start += width

        def build(zl, carry, members=members, order=order, work=work, half_width=half_width):
            for x in range(4):
                block = zl * 4 + x
                for member, width, start in members:
                    for col in range(0, width, 128):
                        cols = pl.ds(col, 128)
                        half = (start + col) // half_width
                        to = pl.ds((start + col) % half_width, 128)
                        rows = (
                            inputs[member][block, core, :, cols] + landed[member][block, :, cols]
                        )
                        low = lax.broadcasted_iota(jnp.int32, (8, 128), 0) < 4
                        for pair in range(2):
                            a = rows[pair * 8 : pair * 8 + 8]
                            b = rows[16 + pair * 8 : 24 + pair * 8]
                            tiles = (
                                jnp.where(low, a, pltpu.roll(b, 4, 0)),
                                jnp.where(low, pltpu.roll(a, 4, 0), b),
                            )
                            for bit in range(2):
                                where = {"z": zl, "x": x, "y": pair * 2 + bit}
                                index = (half,) + tuple(where[axis] for axis in order)
                                work[index + (slice(None), to)] = tiles[bit]
            return carry

        lax.fori_loop(0, 4, build, 0)
        stages = []
        for stage in range(3):
            n = part * 3 + stage
            stages.append(
                Ring(
                    order[stage],
                    work if stage == 0 else rings_of[2 * (n - 1) + 1],
                    rings_of[2 * n],
                    rings_of[2 * n + 1],
                    ring_send.at[n],
                    ring_receive.at[n],
                )
            )
        rings.append(stages)
        stages[0].first()
    for stage in range(3):
        for part in range(3):
            rings[part][stage].second()
        for part in range(3):
            rings[part][stage].finish()
            if stage < 2:
                rings[part][stage + 1].first()
    total = jnp.concatenate(
        [rings_of[2 * (part * 3 + 2) + 1][half] for part in range(3) for half in range(2)], axis=1
    )
    turned = pltpu.roll(total, 4, 0)
    high = lax.axis_index("zh")
    fold = lax.broadcasted_iota(jnp.int32, (8, TOTAL // 2), 0) < 4

    def folded(upright, upside):
        return jnp.where(fold, upright[:, : TOTAL // 2], upside[:, TOTAL // 2 :])

    straight, crossed = folded(total, turned), folded(turned, total)
    sent[...] = jnp.where(high == 1, straight, crossed)
    mate[...] = jnp.where(high == 0, straight, crossed)
    last = remote(sent, fold_in, fold_sems.at[0], fold_sems.at[1], far)
    last.start()
    for copy in core_copies:
        copy.wait_send()
    for stages in rings:
        for ring in stages:
            ring.drain()
    last.wait()
    out_ref[...] = mate[...] + fold_in[...]


def sum_over_devices(*arrays):
    f32 = jnp.float32
    scratch = [pltpu.VMEM((16, 32, a.shape[1]), f32) for a in arrays]
    halves = [sum(widths) // 2 for widths in WIDTHS]
    scratch += [pltpu.VMEM((2, 4, 4, 4, 8, n), f32) for n in halves]
    for n in halves:
        for stage in range(3):
            rest = (4,) * (2 - stage) + (8, n)
            scratch += [pltpu.VMEM((6,) + rest, f32), pltpu.VMEM((2,) + rest, f32)]
    scratch += [pltpu.VMEM((8, TOTAL // 2), f32)] * 3
    scratch += [
        pltpu.SemaphoreType.DMA((5,)),
        pltpu.SemaphoreType.DMA((5,)),
        pltpu.SemaphoreType.DMA((9, 6)),
        pltpu.SemaphoreType.DMA((9, 6)),
        pltpu.SemaphoreType.DMA((2,)),
    ]
    out = pl.pallas_call(
        sum_kernel,
        out_shape=jax.ShapeDtypeStruct((8, TOTAL // 2), f32),
        in_specs=[VMEM_SPEC] * 5,
        out_specs=VMEM_SPEC,
        scratch_shapes=scratch,
        compiler_params=pltpu.CompilerParams(
            collective_id=2, has_side_effects=True, vmem_limit_bytes=60 << 20
        ),
        name="sum_over_devices",
    )(*[a.reshape(16, 2, 32, a.shape[1]) for a in arrays])
    return jnp.concatenate([out[:4], out[4:]], axis=1)


WIDE = 1152


def joined(earlier, later):
    keep = later[:, 1024:]
    gain = jnp.concatenate([keep] * 9, axis=1)
    added = jnp.concatenate([later[:, :1024], jnp.zeros_like(keep)], axis=1)
    return gain * earlier + added


def identity_rows(rows):
    return jnp.concatenate(
        [jnp.zeros((rows, 1024), jnp.float32), jnp.ones((rows, 128), jnp.float32)], axis=1
    )


def scan_kernel(reverse, add_ref, keep_ref, out_ref, own, mate, pair, xs, zs, backs, down, up, far, send, receive):
    core, x, zl = lax.axis_index("c"), lax.axis_index("x"), lax.axis_index("zl")
    other = {"c": 1 - core}
    x_peers = [{"x": lax.rem(x + k, 4)} for k in (1, 2, 3)]
    z_peers = [{"zl": lax.rem(zl + k, 4)} for k in (1, 2, 3)]
    own[:, :1024] = add_ref[...]
    own[:, 1024:] = keep_ref[...]
    greet([other] + x_peers + z_peers)

    def rows_of(start, count):
        return pl.ds(pl.multiple_of(start, count), count)

    mine = rows_of(core * 64, 64)
    theirs = rows_of((1 - core) * 64, 64)
    copies = []

    def push(source, target, device):
        n = len(copies)
        copy = remote(source, target, send.at[n], receive.at[n], device)
        copy.start()
        copies.append(copy)
        return copy

    push(own.at[theirs], mate, other).wait_recv()
    leads = core == (1 if reverse else 0)
    kept, got = own[mine], mate[...]
    earlier = jnp.where(leads, kept, got)
    pair[...] = joined(earlier, jnp.where(leads, got, kept))
    started = [
        push(pair.at[rows_of(lax.rem(x + k, 4) * 16, 16)], xs.at[x], x_peers[k - 1])
        for k in (1, 2, 3)
    ]
    xs[x] = pair[rows_of(x * 16, 16)]
    for copy in started:
        copy.wait_recv()
    order = (3, 2, 1, 0) if reverse else (0, 1, 2, 3)
    inside = {}
    running = None
    for k in order:
        inside[k] = running
        running = xs[k] if running is None else joined(running, xs[k])
    zs[zl] = running
    started = [push(zs.at[zl], zs.at[zl], z_peers[k - 1]) for k in (1, 2, 3)]
    for copy in started:
        copy.wait_recv()
    before = identity_rows(16)
    for k in order[:3]:
        passed = k > zl if reverse else k < zl
        before = jnp.where(passed, joined(before, zs[k]), before)
    for k in order:
        backs[k] = before if inside[k] is None else joined(before, inside[k])
    started = [
        push(backs.at[lax.rem(x + k, 4)], down.at[rows_of(x * 16, 16)], x_peers[k - 1])
        for k in (1, 2, 3)
    ]
    down[rows_of(x * 16, 16)] = backs[x]
    for copy in started:
        copy.wait_recv()
    lead = down[...]
    follow = joined(lead, earlier)
    up[...] = jnp.where(leads, follow, lead)
    last = push(up, far, other)
    out_ref[mine] = jnp.where(leads, lead, follow)
    last.wait_recv()
    out_ref[theirs] = far[...]
    for copy in copies:
        copy.wait_send()


def entering(keep, added, reverse):
    f32 = jnp.float32
    out = pl.pallas_call(
        functools.partial(scan_kernel, reverse),
        out_shape=jax.ShapeDtypeStruct((128, WIDE), f32),
        in_specs=[VMEM_SPEC] * 2,
        out_specs=VMEM_SPEC,
        scratch_shapes=[
            pltpu.VMEM((128, WIDE), f32),
            pltpu.VMEM((64, WIDE), f32),
            pltpu.VMEM((64, WIDE), f32),
            pltpu.VMEM((4, 16, WIDE), f32),
            pltpu.VMEM((4, 16, WIDE), f32),
            pltpu.VMEM((4, 16, WIDE), f32),
            pltpu.VMEM((64, WIDE), f32),
            pltpu.VMEM((64, WIDE), f32),
            pltpu.VMEM((64, WIDE), f32),
            pltpu.SemaphoreType.DMA((11,)),
            pltpu.SemaphoreType.DMA((11,)),
        ],
        compiler_params=pltpu.CompilerParams(
            collective_id=1 if reverse else 0, has_side_effects=True
        ),
        name="suffix" if reverse else "prefix",
    )(added, jnp.broadcast_to(keep[:, None], (128, 128)))
    return out[:, 1024], out[:, :1024]


epsilon = 1e-05
score_scale = 0.125


def normalize(activations, norm_gain):
    inverse = lax.rsqrt(jnp.mean(activations * activations, axis=-1, keepdims=True) + epsilon)
    return (activations * inverse * norm_gain).astype(jnp.bfloat16)


def prepare(query_weight, key_weight, value_weight, norm_gain, segment):
    normed_rows = normalize(segment.astype(jnp.float32), norm_gain)
    queries = (
        jnp.dot(normed_rows, query_weight, preferred_element_type=jnp.float32) * score_scale
    ).astype(jnp.bfloat16)
    key_rows = jnp.dot(normed_rows, key_weight, preferred_element_type=jnp.float32).astype(
        jnp.bfloat16
    )
    value_rows = jnp.dot(normed_rows, value_weight, preferred_element_type=jnp.float32).astype(
        jnp.bfloat16
    )
    return (queries, key_rows, value_rows)


def attend(queries, key_rows, value_rows, allowed):
    count = queries.shape[0]
    width = key_rows.shape[0]
    groups = key_rows.shape[1] // HEAD
    shared = queries.shape[1] // key_rows.shape[1]
    grouped = queries.reshape(count, groups, shared, HEAD)
    keyed = key_rows.reshape(width, groups, HEAD)
    valued = value_rows.reshape(width, groups, HEAD)
    scores = jnp.einsum("rgsh,kgh->gsrk", grouped, keyed, preferred_element_type=jnp.float32)
    scores = jnp.where(allowed, scores, -1e30)
    weights = jax.nn.softmax(scores, axis=-1).astype(jnp.bfloat16)
    context = jnp.einsum("gsrk,kgh->rgsh", weights, valued, preferred_element_type=jnp.float32)
    return context.reshape(count, groups * shared * HEAD).astype(jnp.bfloat16)


def read_part(
    queries,
    seg_keys,
    seg_values,
    key_weight,
    value_weight,
    out_weight,
    norm_gain,
    memory_in,
    segment,
    seg_length,
):
    memory_rows = normalize(memory_in, norm_gain)
    memory_keys = jnp.dot(memory_rows, key_weight, preferred_element_type=jnp.float32).astype(
        jnp.bfloat16
    )
    memory_values = jnp.dot(memory_rows, value_weight, preferred_element_type=jnp.float32).astype(
        jnp.bfloat16
    )
    key_rows = jnp.concatenate([memory_keys, seg_keys], axis=0)
    value_rows = jnp.concatenate([memory_values, seg_values], axis=0)
    count = segment.shape[0]
    places = jnp.arange(count)
    causal = (places[None, :] <= places[:, None]) & (places[None, :] < seg_length)
    allowed = jnp.concatenate([jnp.ones((count, memory_in.shape[0]), dtype=bool), causal], axis=1)
    context = attend(queries, key_rows, value_rows, allowed)
    return segment.astype(jnp.float32) + jnp.dot(
        context, out_weight, preferred_element_type=jnp.float32
    )


def write_part(
    seg_keys,
    seg_values,
    query_weight,
    out_weight,
    norm_gain,
    gate_vector,
    memory_start,
    gate_bias,
    seg_length,
):
    start_rows = normalize(memory_start, norm_gain)
    slot_queries = (
        jnp.dot(start_rows, query_weight, preferred_element_type=jnp.float32) * score_scale
    ).astype(jnp.bfloat16)
    places = jnp.arange(seg_keys.shape[0])
    allowed = jnp.broadcast_to(
        places[None, :] < seg_length, (memory_start.shape[0], seg_keys.shape[0])
    )
    context = attend(slot_queries, seg_keys, seg_values, allowed)
    written = jnp.dot(context, out_weight, preferred_element_type=jnp.float32)
    retain = jax.nn.sigmoid(
        gate_bias + jnp.dot(written, gate_vector, precision=lax.Precision.HIGHEST)
    )
    return (retain, written)


def per_device(
    segments,
    lengths,
    query_weight,
    key_weight,
    value_weight,
    out_weight,
    norm_gain,
    gate_vector,
    gate_bias,
    memory_init,
    cotangent,
):
    segment = segments[0, 0]
    seg_length = lengths[0, 0]
    memory_start = memory_init.astype(jnp.float32)

    def prepared(query_part, key_part, value_part, gain_part):
        return prepare(query_part, key_part, value_part, gain_part, segment)

    (queries, seg_keys, seg_values), prep_back = jax.vjp(
        prepared, query_weight, key_weight, value_weight, norm_gain
    )

    def writing(keys_in, values_in, query_part, out_part, gain_part, vector_part, start_part):
        return write_part(
            keys_in,
            values_in,
            query_part,
            out_part,
            gain_part,
            vector_part,
            start_part,
            gate_bias,
            seg_length,
        )

    (retain, written), write_back = jax.vjp(
        writing,
        seg_keys,
        seg_values,
        query_weight,
        out_weight,
        norm_gain,
        gate_vector,
        memory_start,
    )
    prefix_keep, prefix_add = entering(retain, (1.0 - retain)[:, None] * written, False)
    memory_in = prefix_keep[:, None] * memory_start + prefix_add

    def reading(
        queries_in, keys_in, values_in, key_part, value_part, out_part, gain_part, memory_part
    ):
        return read_part(
            queries_in,
            keys_in,
            values_in,
            key_part,
            value_part,
            out_part,
            gain_part,
            memory_part,
            segment,
            seg_length,
        )

    result, read_back = jax.vjp(
        reading,
        queries,
        seg_keys,
        seg_values,
        key_weight,
        value_weight,
        out_weight,
        norm_gain,
        memory_in,
    )
    valid_rows = (jnp.arange(segment.shape[0]) < seg_length)[:, None]
    d_result = cotangent[0, 0].astype(jnp.float32) * valid_rows
    d_queries, d_keys_read, d_values_read, key_read, value_read, out_read, gain_read, d_memory = (
        read_back(d_result)
    )
    later_keep, later_grad = entering(retain, d_memory, True)
    d_retain = jnp.sum(later_grad * (memory_in - written), axis=1)
    d_written = (1.0 - retain)[:, None] * later_grad
    d_keys_write, d_values_write, query_write, out_write, gain_write, gate_grad, start_grad = (
        write_back((d_retain, d_written))
    )
    d_keys = (d_keys_read.astype(jnp.float32) + d_keys_write.astype(jnp.float32)).astype(
        jnp.bfloat16
    )
    d_values = (d_values_read.astype(jnp.float32) + d_values_write.astype(jnp.float32)).astype(
        jnp.bfloat16
    )
    query_prep, key_prep, value_prep, gain_prep = prep_back((d_queries, d_keys, d_values))
    query_total = query_write.astype(jnp.float32) + query_prep.astype(jnp.float32)
    gain_total = gain_read + gain_write + gain_prep
    start_total = start_grad + prefix_keep[:, None] * d_memory
    key_total = key_read.astype(jnp.float32) + key_prep.astype(jnp.float32)
    value_total = value_read.astype(jnp.float32) + value_prep.astype(jnp.float32)
    out_total = out_read.astype(jnp.float32) + out_write.astype(jnp.float32)
    rest = jnp.concatenate(
        [start_total.T, gain_total[:, None], gate_grad[:, None], jnp.zeros((1024, 126))], axis=1
    )
    summed = sum_over_devices(query_total, out_total, key_total, value_total, rest)
    grad_query, grad_out = summed[:, :1024], summed[:, 1024:2048]
    grad_key, grad_value = summed[:, 2048:2304], summed[:, 2304:2560]
    grad_memory = summed[:, 2560:2688].T
    grad_gain, grad_gate = summed[:, 2688], summed[:, 2689]
    layer_output = result.astype(jnp.bfloat16)[None, None]
    return (
        layer_output,
        grad_query,
        grad_key,
        grad_value,
        grad_out,
        grad_gain,
        grad_gate,
        grad_memory,
    )


def solution(mesh):
    split = Mesh(mesh.devices.reshape(4, 4, 2, 2, 4), AXES)
    rows = P(("zh", "y"), ("zl", "x", "c"), None, None)
    return jax.shard_map(
        per_device,
        mesh=split,
        in_specs=(rows, P(("zh", "y"), ("zl", "x", "c"))) + (P(),) * 8 + (rows,),
        out_specs=(
            rows,
            P(AXES, None),
            P(AXES, None),
            P(AXES, None),
            P(AXES, None),
            P(AXES),
            P(AXES),
            P(None, AXES),
        ),
        check_vma=False,
    )
```

```python
import functools

import jax
import jax.numpy as jnp
from jax import lax
from jax.experimental import pallas as pl
from jax.experimental.pallas import tpu as pltpu
from jax.sharding import Mesh
from jax.sharding import PartitionSpec as P

HEAD = 64
AXES = ("zl", "x", "c", "zh", "y")
MESH = pl.DeviceIdType.MESH
VMEM_SPEC = pl.BlockSpec(memory_space=pltpu.VMEM)


def z_shift(step):
    place = lax.rem(lax.axis_index("zh") * 4 + lax.axis_index("zl") + step, 8)
    return {"zh": lax.div(place, 4), "zl": lax.rem(place, 4)}


def shift(axis, step):
    if axis == "z":
        return z_shift(step % 8)
    return {axis: lax.rem(lax.axis_index(axis) + step % 4, 4)}


def place_of(axis):
    return lax.axis_index("zl" if axis == "z" else axis)


def remote(source, target, send, receive, device):
    return pltpu.make_async_remote_copy(
        src_ref=source,
        dst_ref=target,
        send_sem=send,
        recv_sem=receive,
        device_id=device,
        device_id_type=MESH,
    )


def greet(devices):
    barrier = pltpu.get_barrier_semaphore()
    for device in devices:
        pl.semaphore_signal(barrier, inc=1, device_id=device, device_id_type=MESH)
    pl.semaphore_wait(barrier, len(devices))


class Ring:
    def __init__(self, axis, work, landing, out, send, receive):
        self.work, self.landing, self.out = work, landing, out
        self.send, self.receive = send, receive
        self.me = place_of(axis)
        self.up, self.down = shift(axis, 1), shift(axis, -1)
        self.copies = []

    def at(self, step):
        return lax.rem(self.me + step, 4)

    def push(self, half, step, device):
        slot = len(self.copies)
        copy = remote(
            self.work.at[half, self.at(step)],
            self.landing.at[slot],
            self.send.at[slot],
            self.receive.at[slot],
            device,
        )
        copy.start()
        self.copies.append(copy)

    def first(self):
        self.push(0, 2, self.up)
        self.push(1, 2, self.down)
        self.push(1, 1, self.up)
        self.push(0, 3, self.down)

    def second(self):
        for half, step, device in ((0, 1, self.up), (1, 3, self.down)):
            self.copies[half].wait_recv()
            self.work[half, self.at(step)] += self.landing[half]
            self.push(half, step, device)

    def finish(self):
        for slot in range(2, 6):
            self.copies[slot].wait_recv()
        self.out[0] = self.work[0, self.me] + self.landing[3] + self.landing[4]
        self.out[1] = self.work[1, self.me] + self.landing[2] + self.landing[5]

    def drain(self):
        for copy in self.copies:
            copy.wait_send()


ORDERS = (("x", "y", "z"), ("y", "z", "x"), ("z", "x", "y"))
WIDTHS = ((1024,), (1024,), (256, 256, 256))
TOTAL = 2816


def sum_kernel(*refs):
    inputs, refs = refs[:5], refs[5:]
    out_ref, refs = refs[0], refs[1:]
    landed, refs = refs[:5], refs[5:]
    works, refs = refs[:3], refs[3:]
    rings_of, refs = refs[:18], refs[18:]
    sent, mate, fold_in, core_send, core_receive, ring_send, ring_receive, fold_sems = refs
    core = lax.axis_index("c")
    other = {"c": 1 - core}
    far = z_shift(4)
    greet(
        [other, far]
        + [shift(axis, step) for axis in ("x", "y", "z") for step in (1, -1)]
    )
    core_copies = []
    for k in range(5):
        copy = remote(
            inputs[k].at[:, 1 - core], landed[k], core_send.at[k], core_receive.at[k], other
        )
        copy.start()
        core_copies.append(copy)
    rings = []
    k = 0
    for part in range(3):
        order = ORDERS[part]
        work = works[part]
        half_width = sum(WIDTHS[part]) // 2
        members = []
        start = 0
        for width in WIDTHS[part]:
            members.append((k, width, start))
            core_copies[k].wait_recv()
            k += 1
            start += width

        def build(zl, carry, members=members, order=order, work=work, half_width=half_width):
            for x in range(4):
                block = zl * 4 + x
                for member, width, start in members:
                    for col in range(0, width, 128):
                        cols = pl.ds(col, 128)
                        half = (start + col) // half_width
                        to = pl.ds((start + col) % half_width, 128)
                        rows = (
                            inputs[member][block, core, :, cols] + landed[member][block, :, cols]
                        )
                        low = lax.broadcasted_iota(jnp.int32, (8, 128), 0) < 4
                        for pair in range(2):
                            a = rows[pair * 8 : pair * 8 + 8]
                            b = rows[16 + pair * 8 : 24 + pair * 8]
                            tiles = (
                                jnp.where(low, a, pltpu.roll(b, 4, 0)),
                                jnp.where(low, pltpu.roll(a, 4, 0), b),
                            )
                            for bit in range(2):
                                where = {"z": zl, "x": x, "y": pair * 2 + bit}
                                index = (half,) + tuple(where[axis] for axis in order)
                                work[index + (slice(None), to)] = tiles[bit]
            return carry

        lax.fori_loop(0, 4, build, 0)
        stages = []
        for stage in range(3):
            n = part * 3 + stage
            stages.append(
                Ring(
                    order[stage],
                    work if stage == 0 else rings_of[2 * (n - 1) + 1],
                    rings_of[2 * n],
                    rings_of[2 * n + 1],
                    ring_send.at[n],
                    ring_receive.at[n],
                )
            )
        rings.append(stages)
        stages[0].first()
    for stage in range(3):
        for part in range(3):
            rings[part][stage].second()
        for part in range(3):
            rings[part][stage].finish()
            if stage < 2:
                rings[part][stage + 1].first()
    total = jnp.concatenate(
        [rings_of[2 * (part * 3 + 2) + 1][half] for part in range(3) for half in range(2)], axis=1
    )
    turned = pltpu.roll(total, 4, 0)
    high = lax.axis_index("zh")
    fold = lax.broadcasted_iota(jnp.int32, (8, TOTAL // 2), 0) < 4

    def folded(upright, upside):
        return jnp.where(fold, upright[:, : TOTAL // 2], upside[:, TOTAL // 2 :])

    straight, crossed = folded(total, turned), folded(turned, total)
    sent[...] = jnp.where(high == 1, straight, crossed)
    mate[...] = jnp.where(high == 0, straight, crossed)
    last = remote(sent, fold_in, fold_sems.at[0], fold_sems.at[1], far)
    last.start()
    for copy in core_copies:
        copy.wait_send()
    for stages in rings:
        for ring in stages:
            ring.drain()
    last.wait()
    out_ref[...] = mate[...] + fold_in[...]


def sum_over_devices(*arrays):
    f32 = jnp.float32
    scratch = [pltpu.VMEM((16, 32, a.shape[1]), f32) for a in arrays]
    halves = [sum(widths) // 2 for widths in WIDTHS]
    scratch += [pltpu.VMEM((2, 4, 4, 4, 8, n), f32) for n in halves]
    for n in halves:
        for stage in range(3):
            rest = (4,) * (2 - stage) + (8, n)
            scratch += [pltpu.VMEM((6,) + rest, f32), pltpu.VMEM((2,) + rest, f32)]
    scratch += [pltpu.VMEM((8, TOTAL // 2), f32)] * 3
    scratch += [
        pltpu.SemaphoreType.DMA((5,)),
        pltpu.SemaphoreType.DMA((5,)),
        pltpu.SemaphoreType.DMA((9, 6)),
        pltpu.SemaphoreType.DMA((9, 6)),
        pltpu.SemaphoreType.DMA((2,)),
    ]
    out = pl.pallas_call(
        sum_kernel,
        out_shape=jax.ShapeDtypeStruct((8, TOTAL // 2), f32),
        in_specs=[VMEM_SPEC] * 5,
        out_specs=VMEM_SPEC,
        scratch_shapes=scratch,
        compiler_params=pltpu.CompilerParams(
            collective_id=2, has_side_effects=True, vmem_limit_bytes=60 << 20
        ),
        name="sum_over_devices",
    )(*[a.reshape(16, 2, 32, a.shape[1]) for a in arrays])
    return jnp.concatenate([out[:4], out[4:]], axis=1)


WIDE = 1152


def joined(earlier, later):
    keep = later[:, 1024:]
    gain = jnp.concatenate([keep] * 9, axis=1)
    added = jnp.concatenate([later[:, :1024], jnp.zeros_like(keep)], axis=1)
    return gain * earlier + added


def identity_rows(rows):
    return jnp.concatenate(
        [jnp.zeros((rows, 1024), jnp.float32), jnp.ones((rows, 128), jnp.float32)], axis=1
    )


def scan_kernel(reverse, add_ref, keep_ref, out_ref, own, mate, pair, xs, zs, backs, down, up, far, send, receive):
    core, x, zl = lax.axis_index("c"), lax.axis_index("x"), lax.axis_index("zl")
    other = {"c": 1 - core}
    x_peers = [{"x": lax.rem(x + k, 4)} for k in (1, 2, 3)]
    z_peers = [{"zl": lax.rem(zl + k, 4)} for k in (1, 2, 3)]
    own[:, :1024] = add_ref[...]
    own[:, 1024:] = keep_ref[...]
    greet([other] + x_peers + z_peers)

    def rows_of(start, count):
        return pl.ds(pl.multiple_of(start, count), count)

    mine = rows_of(core * 64, 64)
    theirs = rows_of((1 - core) * 64, 64)
    copies = []

    def push(source, target, device):
        n = len(copies)
        copy = remote(source, target, send.at[n], receive.at[n], device)
        copy.start()
        copies.append(copy)
        return copy

    push(own.at[theirs], mate, other).wait_recv()
    leads = core == (1 if reverse else 0)
    kept, got = own[mine], mate[...]
    earlier = jnp.where(leads, kept, got)
    pair[...] = joined(earlier, jnp.where(leads, got, kept))
    started = [
        push(pair.at[rows_of(lax.rem(x + k, 4) * 16, 16)], xs.at[x], x_peers[k - 1])
        for k in (1, 2, 3)
    ]
    xs[x] = pair[rows_of(x * 16, 16)]
    for copy in started:
        copy.wait_recv()
    order = (3, 2, 1, 0) if reverse else (0, 1, 2, 3)
    inside = {}
    running = None
    for k in order:
        inside[k] = running
        running = xs[k] if running is None else joined(running, xs[k])
    zs[zl] = running
    started = [push(zs.at[zl], zs.at[zl], z_peers[k - 1]) for k in (1, 2, 3)]
    for copy in started:
        copy.wait_recv()
    before = identity_rows(16)
    for k in order[:3]:
        passed = k > zl if reverse else k < zl
        before = jnp.where(passed, joined(before, zs[k]), before)
    for k in order:
        backs[k] = before if inside[k] is None else joined(before, inside[k])
    started = [
        push(backs.at[lax.rem(x + k, 4)], down.at[rows_of(x * 16, 16)], x_peers[k - 1])
        for k in (1, 2, 3)
    ]
    down[rows_of(x * 16, 16)] = backs[x]
    for copy in started:
        copy.wait_recv()
    lead = down[...]
    follow = joined(lead, earlier)
    up[...] = jnp.where(leads, follow, lead)
    last = push(up, far, other)
    out_ref[mine] = jnp.where(leads, lead, follow)
    last.wait_recv()
    out_ref[theirs] = far[...]
    for copy in copies:
        copy.wait_send()


def entering(keep, added, reverse):
    f32 = jnp.float32
    out = pl.pallas_call(
        functools.partial(scan_kernel, reverse),
        out_shape=jax.ShapeDtypeStruct((128, WIDE), f32),
        in_specs=[VMEM_SPEC] * 2,
        out_specs=VMEM_SPEC,
        scratch_shapes=[
            pltpu.VMEM((128, WIDE), f32),
            pltpu.VMEM((64, WIDE), f32),
            pltpu.VMEM((64, WIDE), f32),
            pltpu.VMEM((4, 16, WIDE), f32),
            pltpu.VMEM((4, 16, WIDE), f32),
            pltpu.VMEM((4, 16, WIDE), f32),
            pltpu.VMEM((64, WIDE), f32),
            pltpu.VMEM((64, WIDE), f32),
            pltpu.VMEM((64, WIDE), f32),
            pltpu.SemaphoreType.DMA((11,)),
            pltpu.SemaphoreType.DMA((11,)),
        ],
        compiler_params=pltpu.CompilerParams(
            collective_id=1 if reverse else 0, has_side_effects=True
        ),
        name="suffix" if reverse else "prefix",
    )(added, keep)
    return out


epsilon = 1e-05
score_scale = 0.125
F32, BF16 = jnp.float32, jnp.bfloat16
GROUPS, SHARED, SEG = 4, 4, 128


def mul(a, b):
    return lax.dot_general(a, b, (((1,), (0,)), ((), ())), preferred_element_type=F32)


def mul_nt(a, b):
    return lax.dot_general(a, b, (((1,), (1,)), ((), ())), preferred_element_type=F32)


def mul_tn(a, b):
    return lax.dot_general(a, b, (((0,), (0,)), ((), ())), preferred_element_type=F32)


def inverse_of(rows):
    return lax.rsqrt(jnp.mean(rows * rows, axis=-1, keepdims=True) + epsilon)


def normalize(rows, gain):
    return (rows * inverse_of(rows) * gain).astype(BF16)


def normalize_back(rows, gain, d_normed):
    inverse = inverse_of(rows)
    scaled = d_normed * gain
    shared = jnp.mean(scaled * rows, axis=-1, keepdims=True)
    return inverse * scaled - rows * (inverse * inverse * inverse * shared)


def stacked(rows, group):
    start = group * SHARED * HEAD
    return jnp.concatenate(
        [rows[:, start + k * HEAD : start + (k + 1) * HEAD] for k in range(SHARED)], axis=0
    )


def side_by_side(rows):
    return jnp.concatenate([rows[k * SEG : (k + 1) * SEG] for k in range(SHARED)], axis=1)


def of_group(rows, group):
    return rows[:, group * HEAD : (group + 1) * HEAD]


def weights_of(queries, keys, allowed):
    scores = jnp.where(allowed, mul_nt(queries, keys), -1e30)
    raised = jnp.exp(scores - jnp.max(scores, axis=-1, keepdims=True))
    return raised / jnp.sum(raised, axis=-1, keepdims=True)


def attend_back(weights, rounded, queries, keys, values, d_context):
    d_values = mul_tn(rounded, d_context)
    d_weights = mul_nt(d_context, values).astype(BF16).astype(F32)
    pulled = jnp.sum(d_weights * weights, axis=-1, keepdims=True)
    d_scores = (weights * (d_weights - pulled)).astype(BF16)
    return mul(d_scores, keys).astype(BF16), mul_tn(d_scores, queries), d_values


def write_kernel(
    length_ref, x_ref, wq_ref, wk_ref, wv_ref, wo_ref, gain_ref, vector_ref, bias_ref, start_ref,
    q_ref, k_ref, v_ref, xn_ref, sn_ref, sq_ref, p_ref, context_ref, written_ref, retain_ref,
    added_ref,
):
    length = length_ref[0, 0]
    gain = gain_ref[...]
    xn = normalize(x_ref[...].astype(F32), gain)
    sn = normalize(start_ref[...].astype(F32), gain)
    xn_ref[...] = xn
    sn_ref[...] = sn
    both = (mul(jnp.concatenate([xn, sn], axis=0), wq_ref[...]) * score_scale).astype(BF16)
    q_ref[...] = both[:SEG]
    sq = both[SEG:]
    sq_ref[...] = sq
    keys = mul(xn, wk_ref[...]).astype(BF16)
    values = mul(xn, wv_ref[...]).astype(BF16)
    k_ref[...] = keys
    v_ref[...] = values
    allowed = lax.broadcasted_iota(jnp.int32, (SHARED * SEG, SEG), 1) < length
    contexts = []
    for group in range(GROUPS):
        weights = weights_of(stacked(sq, group), of_group(keys, group), allowed).astype(BF16)
        p_ref[group] = weights
        contexts.append(side_by_side(mul(weights, of_group(values, group)).astype(BF16)))
    context = jnp.concatenate(contexts, axis=1)
    context_ref[...] = context
    written = mul(context, wo_ref[...])
    written_ref[...] = written
    logits = jnp.sum(written * vector_ref[...], axis=-1, keepdims=True) + bias_ref[...]
    retain = jax.nn.sigmoid(logits)
    retain_ref[...] = jnp.broadcast_to(retain, (SEG, 128))
    added_ref[...] = (1.0 - retain) * written


def read_kernel(
    length_ref, x_ref, cot_ref, wk_ref, wv_ref, wo_ref, gain_ref, start_ref, scan_ref,
    q_ref, k_ref, v_ref,
    out_ref, memory_ref, mn_ref, context_ref, dr_ref, dq_ref, dk_ref, dv_ref, dmk_ref, dmv_ref,
    r_ref,
):
    length = length_ref[0, 0]
    gain = gain_ref[...]
    memory = scan_ref[:, 1024:1025] * start_ref[...].astype(F32) + scan_ref[:, :1024]
    memory_ref[...] = memory
    mn = normalize(memory, gain)
    mn_ref[...] = mn
    keys = jnp.concatenate([mul(mn, wk_ref[...]).astype(BF16), k_ref[...]], axis=0)
    values = jnp.concatenate([mul(mn, wv_ref[...]).astype(BF16), v_ref[...]], axis=0)
    valid = lax.broadcasted_iota(jnp.int32, (SEG, 1024), 0) < length
    d_result = jnp.where(valid, cot_ref[...].astype(F32), 0.0).astype(BF16)
    dr_ref[...] = d_result
    d_context = mul_nt(d_result, wo_ref[...]).astype(BF16)
    shape = (SHARED * SEG, 2 * SEG)
    place = lax.broadcasted_iota(jnp.int32, shape, 1) - SEG
    row = lax.rem(lax.broadcasted_iota(jnp.int32, shape, 0), SEG)
    allowed = (place < 0) | ((place <= row) & (place < length))
    queries = q_ref[...]
    contexts, d_queries, d_keys, d_values = [], [], [], []
    for group in range(GROUPS):
        q, k, v = stacked(queries, group), of_group(keys, group), of_group(values, group)
        weights = weights_of(q, k, allowed)
        rounded = weights.astype(BF16)
        contexts.append(side_by_side(mul(rounded, v).astype(BF16)))
        dq, dk, dv = attend_back(weights, rounded, q, k, v, stacked(d_context, group))
        d_queries.append(side_by_side(dq))
        d_keys.append(dk.astype(BF16))
        d_values.append(dv.astype(BF16))
    context = jnp.concatenate(contexts, axis=1)
    context_ref[...] = context
    out_ref[...] = (x_ref[...].astype(F32) + mul(context, wo_ref[...])).astype(BF16)
    dq_ref[...] = jnp.concatenate(d_queries, axis=1)
    d_key = jnp.concatenate(d_keys, axis=1)
    d_value = jnp.concatenate(d_values, axis=1)
    dmk_ref[...] = d_key[:SEG]
    dmv_ref[...] = d_value[:SEG]
    dk_ref[...] = d_key[SEG:]
    dv_ref[...] = d_value[SEG:]
    d_mn = mul_nt(d_key[:SEG], wk_ref[...]) + mul_nt(d_value[:SEG], wv_ref[...])
    r_ref[...] = normalize_back(memory, gain, d_mn.astype(BF16).astype(F32))


def grads_kernel(
    later_ref, memory_ref, written_ref, retain_ref, vector_ref, wq_ref, wo_ref, gain_ref,
    start_ref, scan_ref, r_ref, p_ref, q_ref, sq_ref, k_ref, v_ref, xn_ref, sn_ref, mn_ref,
    cr_ref, cw_ref, dr_ref, dq_ref, dk_ref, dv_ref, dmk_ref, dmv_ref,
    gq_ref, go_ref, gk_ref, gv_ref, rest_ref,
):
    later = later_ref[:, :1024]
    written = written_ref[...]
    retain = retain_ref[:, :1]
    d_retain = jnp.sum(later * (memory_ref[...] - written), axis=-1, keepdims=True)
    d_logit = d_retain * retain * (1.0 - retain)
    gate = jnp.sum(written * d_logit, axis=0, keepdims=True)
    d_written = ((1.0 - retain) * later + d_logit * vector_ref[...]).astype(BF16)
    d_context = mul_nt(d_written, wo_ref[...]).astype(BF16)
    slots, keys, values = sq_ref[...], k_ref[...], v_ref[...]
    d_slots, d_keys, d_values = [], [], []
    for group in range(GROUPS):
        rounded = p_ref[group]
        dq, dk, dv = attend_back(
            rounded.astype(F32), rounded, stacked(slots, group), of_group(keys, group),
            of_group(values, group), stacked(d_context, group),
        )
        d_slots.append(side_by_side(dq))
        d_keys.append(dk.astype(BF16))
        d_values.append(dv.astype(BF16))

    def added(first, second):
        return (first.astype(F32) + second.astype(F32)).astype(BF16)

    scale = jnp.asarray(score_scale, BF16)
    d_slot = jnp.concatenate(d_slots, axis=1) * scale
    d_key = added(dk_ref[...], jnp.concatenate(d_keys, axis=1))
    d_value = added(dv_ref[...], jnp.concatenate(d_values, axis=1))
    left = jnp.concatenate([xn_ref[...], sn_ref[...]], axis=0)
    right = jnp.concatenate([dq_ref[...] * scale, d_slot], axis=0)
    normed = jnp.concatenate([xn_ref[...], mn_ref[...]], axis=0)
    right_key = jnp.concatenate([d_key, dmk_ref[...]], axis=0)
    right_value = jnp.concatenate([d_value, dmv_ref[...]], axis=0)
    context = jnp.concatenate([cr_ref[...], cw_ref[...]], axis=0)
    d_out = jnp.concatenate([dr_ref[...], d_written], axis=0)
    for block in range(4):
        rows = slice(block * 256, block * 256 + 256)
        gq_ref[rows] = mul_tn(left[:, rows], right)
        go_ref[rows] = mul_tn(context[:, rows], d_out)
        gk_ref[rows] = mul_tn(normed[:, rows], right_key)
        gv_ref[rows] = mul_tn(normed[:, rows], right_value)
    d_sn = mul_nt(d_slot, wq_ref[...]).astype(BF16).astype(F32)
    start = start_ref[...].astype(F32)
    total = normalize_back(start, gain_ref[...], d_sn) + scan_ref[:, 1024:1025] * r_ref[...]
    gates = jnp.broadcast_to(gate, (128, 1024))
    for block in range(8):
        rows = slice(block * 128, block * 128 + 128)
        rest_ref[rows, :128] = jnp.transpose(total[:, rows])
        rest_ref[rows, 128:] = jnp.transpose(gates[:, rows])


def local_kernel(kernel, shapes, operands, name):
    smem = pl.BlockSpec(memory_space=pltpu.SMEM)
    return pl.pallas_call(
        kernel,
        out_shape=[jax.ShapeDtypeStruct(shape, dtype) for shape, dtype in shapes],
        in_specs=[smem if a.dtype == jnp.int32 else VMEM_SPEC for a in operands],
        out_specs=[VMEM_SPEC] * len(shapes),
        compiler_params=pltpu.CompilerParams(vmem_limit_bytes=60 << 20),
        name=name,
    )(*operands)


def per_device(
    segments,
    lengths,
    query_weight,
    key_weight,
    value_weight,
    out_weight,
    norm_gain,
    gate_vector,
    gate_bias,
    memory_init,
    cotangent,
):
    segment, cot = segments[0, 0], cotangent[0, 0]
    gain, vector, bias = norm_gain[None], gate_vector[None], gate_bias[:, None]
    wide, narrow = ((SEG, 1024), BF16), ((SEG, 256), BF16)
    full = ((SEG, 1024), F32)
    q, k, v, xn, sn, sq, p, cw, written, retain, added = local_kernel(
        write_kernel,
        [wide, narrow, narrow, wide, wide, wide, ((GROUPS, SHARED * SEG, SEG), BF16), wide, full,
         ((SEG, 128), F32), full],
        (lengths, segment, query_weight, key_weight, value_weight, out_weight, gain, vector, bias,
         memory_init),
        "write_forward",
    )
    scan = entering(retain, added, False)
    output, memory, mn, cr, dr, dq, dk, dv, dmk, dmv, r = local_kernel(
        read_kernel,
        [wide, full, wide, wide, wide, wide, narrow, narrow, narrow, narrow, full],
        (lengths, segment, cot, key_weight, value_weight, out_weight, gain, memory_init, scan, q,
         k, v),
        "read_both",
    )
    later = entering(retain, r, True)
    sums = local_kernel(
        grads_kernel,
        [((1024, n), F32) for n in (1024, 1024, 256, 256, 256)],
        (later, memory, written, retain, vector, query_weight, out_weight, gain, memory_init, scan,
         r, p, q, sq, k, v, xn, sn, mn, cr, cw, dr, dq, dk, dv, dmk, dmv),
        "gradients",
    )
    summed = sum_over_devices(*sums)
    grad_query, grad_out = summed[:, :1024], summed[:, 1024:2048]
    grad_key, grad_value = summed[:, 2048:2304], summed[:, 2304:2560]
    grad_memory = summed[:, 2560:2688].T
    grad_gate = summed[:, 2688]
    place = lax.axis_index(AXES)

    def mine(array):
        return lax.dynamic_slice_in_dim(array, place * 4, 4, 0).astype(F32)

    grad_gain = (
        jnp.sum(mine(query_weight) * grad_query, axis=1)
        + jnp.sum(mine(key_weight) * grad_key, axis=1)
        + jnp.sum(mine(value_weight) * grad_value, axis=1)
    ) / mine(norm_gain)
    return (
        output[None, None],
        grad_query,
        grad_key,
        grad_value,
        grad_out,
        grad_gain,
        grad_gate,
        grad_memory,
    )


def solution(mesh):
    split = Mesh(mesh.devices.reshape(4, 4, 2, 2, 4), AXES)
    rows = P(("zh", "y"), ("zl", "x", "c"), None, None)
    return jax.shard_map(
        per_device,
        mesh=split,
        in_specs=(rows, P(("zh", "y"), ("zl", "x", "c"))) + (P(),) * 8 + (rows,),
        out_specs=(
            rows,
            P(AXES, None),
            P(AXES, None),
            P(AXES, None),
            P(AXES, None),
            P(AXES),
            P(AXES),
            P(None, AXES),
        ),
        check_vma=False,
    )
```

```python
import functools

import jax
import jax.numpy as jnp
from jax import lax
from jax.experimental import pallas as pl
from jax.experimental.pallas import tpu as pltpu
from jax.sharding import Mesh
from jax.sharding import PartitionSpec as P

HEAD = 64
F32, BF16 = jnp.float32, jnp.bfloat16
AXES = ("zl", "x", "c", "zh", "y")
MESH = pl.DeviceIdType.MESH
VMEM_SPEC = pl.BlockSpec(memory_space=pltpu.VMEM)


def z_shift(step):
    place = lax.rem(lax.axis_index("zh") * 4 + lax.axis_index("zl") + step, 8)
    return {"zh": lax.div(place, 4), "zl": lax.rem(place, 4)}


def shift(axis, step):
    if axis == "z":
        return z_shift(step % 8)
    return {axis: lax.rem(lax.axis_index(axis) + step % 4, 4)}


def place_of(axis):
    return lax.axis_index("zl" if axis == "z" else axis)


def remote(source, target, send, receive, device):
    return pltpu.make_async_remote_copy(
        src_ref=source,
        dst_ref=target,
        send_sem=send,
        recv_sem=receive,
        device_id=device,
        device_id_type=MESH,
    )


def greet(devices):
    barrier = pltpu.get_barrier_semaphore()
    for device in devices:
        pl.semaphore_signal(barrier, inc=1, device_id=device, device_id_type=MESH)
    pl.semaphore_wait(barrier, len(devices))


class Ring:
    def __init__(self, axis, work, landing, out, send, receive):
        self.work, self.landing, self.out = work, landing, out
        self.send, self.receive = send, receive
        self.me = place_of(axis)
        self.up, self.down = shift(axis, 1), shift(axis, -1)
        self.copies = []

    def at(self, step):
        return lax.rem(self.me + step, 4)

    def push(self, half, step, device):
        slot = len(self.copies)
        copy = remote(
            self.work.at[half, self.at(step)],
            self.landing.at[slot],
            self.send.at[slot],
            self.receive.at[slot],
            device,
        )
        copy.start()
        self.copies.append(copy)

    def first(self):
        self.push(0, 2, self.up)
        self.push(1, 2, self.down)
        self.push(1, 1, self.up)
        self.push(0, 3, self.down)

    def second(self):
        for half, step, device in ((0, 1, self.up), (1, 3, self.down)):
            self.copies[half].wait_recv()
            self.work[half, self.at(step)] += self.landing[half]
            self.push(half, step, device)

    def finish(self):
        for slot in range(2, 6):
            self.copies[slot].wait_recv()
        self.out[0] = self.work[0, self.me] + self.landing[3] + self.landing[4]
        self.out[1] = self.work[1, self.me] + self.landing[2] + self.landing[5]

    def drain(self):
        for copy in self.copies:
            copy.wait_send()


ORDERS = (("x", "y", "z"), ("y", "z", "x"), ("z", "x", "y"))
WIDTHS = ((1024,), (1024,), (512, 256))
TOTAL = 2816


def sum_kernel(*refs):
    left, right, context, d_out, normed, pair, rest, gain, wq, wk, wv = refs[:11]
    out_ref, refs = refs[11], refs[12:]
    products, refs = refs[:3], refs[3:]
    landed, refs = refs[:4], refs[4:]
    works, refs = refs[:3], refs[3:]
    rings_of, refs = refs[:18], refs[18:]
    rows_of, refs = refs[:3], refs[3:]
    sent, mate, fold_in, core_send, core_receive, ring_send, ring_receive, fold_sems, row_sems = refs
    core = lax.axis_index("c")
    other = {"c": 1 - core}
    far = z_shift(4)
    place = lax.axis_index(AXES)
    base = pl.ds(pl.multiple_of(lax.div(place, 4) * 16, 16), 16)
    row_copies = [
        pltpu.make_async_copy(w.at[base], rows, row_sems.at[k])
        for k, (w, rows) in enumerate(zip((wq, wk, wv), rows_of))
    ]
    for copy in row_copies:
        copy.start()
    peers = [other, far] + [shift(axis, step) for axis in ("x", "y", "z") for step in (1, -1)]
    barrier = pltpu.get_barrier_semaphore()
    for device in peers:
        pl.semaphore_signal(barrier, inc=1, device_id=device, device_id_type=MESH)
    core_copies = []

    def push_core(source, target):
        n = len(core_copies)
        copy = remote(source, target, core_send.at[n], core_receive.at[n], other)
        copy.start()
        core_copies.append(copy)

    def product(member, block, factor, other_factor):
        value = mul_tn(factor[:, block * 256 : block * 256 + 256], other_factor[...])
        products[member][block * 4 : block * 4 + 4] = value.reshape(4, 2, 32, value.shape[1])

    def product_and_push(member, factor, other_factor):
        for block in range(4):
            product(member, block, factor, other_factor)
            if member == 0 and block == 0:
                pl.semaphore_wait(barrier, len(peers))
                push_core(rest.at[:, 1 - core], landed[3])
            blocks = pl.ds(block * 4, 4)
            push_core(products[member].at[blocks, 1 - core], landed[member].at[blocks])

    members = [((0, 0),), ((1, 0),), ((2, 0), (3, 512))]
    sources = tuple(products) + (rest,)

    def build_part(part):
        order, work = ORDERS[part], works[part]
        half_width = sum(WIDTHS[part]) // 2

        def build(zl, carry):
            for x in range(4):
                block = zl * 4 + x
                for member, start in members[part]:
                    for col in range(0, sources[member].shape[3], 128):
                        cols = pl.ds(col, 128)
                        half = (start + col) // half_width
                        to = pl.ds((start + col) % half_width, 128)
                        rows = (
                            sources[member][block, core, :, cols] + landed[member][block, :, cols]
                        )
                        low = lax.broadcasted_iota(jnp.int32, (8, 128), 0) < 4
                        for pair_at in range(2):
                            a = rows[pair_at * 8 : pair_at * 8 + 8]
                            b = rows[16 + pair_at * 8 : 24 + pair_at * 8]
                            tiles = (
                                jnp.where(low, a, pltpu.roll(b, 4, 0)),
                                jnp.where(low, pltpu.roll(a, 4, 0), b),
                            )
                            for bit in range(2):
                                where = {"z": zl, "x": x, "y": pair_at * 2 + bit}
                                index = (half,) + tuple(where[axis] for axis in order)
                                work[index + (slice(None), to)] = tiles[bit]
            return carry

        lax.fori_loop(0, 4, build, 0)

    rings = []

    def begin(part, waited):
        for n in waited:
            core_copies[n].wait_recv()
        build_part(part)
        stages = []
        for stage in range(3):
            n = part * 3 + stage
            stages.append(
                Ring(
                    ORDERS[part][stage],
                    works[part] if stage == 0 else rings_of[2 * (n - 1) + 1],
                    rings_of[2 * n],
                    rings_of[2 * n + 1],
                    ring_send.at[n],
                    ring_receive.at[n],
                )
            )
        rings.append(stages)
        stages[0].first()

    product_and_push(0, left, right)
    product_and_push(1, context, d_out)
    begin(0, (1, 2, 3, 4))
    product_and_push(2, normed, pair)
    begin(1, (5, 6, 7, 8))
    begin(2, (0, 9, 10, 11, 12))
    for stage in range(3):
        for part in range(3):
            rings[part][stage].second()
        for part in range(3):
            rings[part][stage].finish()
            if stage < 2:
                rings[part][stage + 1].first()
    total = jnp.concatenate(
        [rings_of[2 * (part * 3 + 2) + 1][half] for part in range(3) for half in range(2)], axis=1
    )
    turned = pltpu.roll(total, 4, 0)
    high = lax.axis_index("zh")
    fold = lax.broadcasted_iota(jnp.int32, (8, TOTAL // 2), 0) < 4

    def folded(upright, upside):
        return jnp.where(fold, upright[:, : TOTAL // 2], upside[:, TOTAL // 2 :])

    straight, crossed = folded(total, turned), folded(turned, total)
    sent[...] = jnp.where(high == 1, straight, crossed)
    mate[...] = jnp.where(high == 0, straight, crossed)
    last = remote(sent, fold_in, fold_sems.at[0], fold_sems.at[1], far)
    last.start()
    for copy in core_copies:
        copy.wait_send()
    for stages in rings:
        for ring in stages:
            ring.drain()
    for copy in row_copies:
        copy.wait()
    part_of_16 = lax.rem(place, 4)
    weights = []
    for rows in rows_of:
        loaded = rows[...].astype(F32)
        tile = jnp.where(part_of_16 >= 2, loaded[8:], loaded[:8])
        weights.append(jnp.where(lax.rem(place, 2) == 1, pltpu.roll(tile, 4, 0), tile))
    spot = place * 4 + lax.broadcasted_iota(jnp.int32, (8, 1024), 0)
    here = lax.broadcasted_iota(jnp.int32, (8, 1024), 1) == spot
    low = lax.broadcasted_iota(jnp.int32, (8, 1), 0) < 4
    gains = jnp.sum(jnp.where(here, gain[...], 0.0), axis=1, keepdims=True)
    gains = jnp.where(low, gains, 1.0)
    last.wait()
    short = mate[...] + fold_in[...]
    full = jnp.concatenate([short, pltpu.roll(short, 4, 0)], axis=1)
    of_gain = (
        jnp.sum(weights[0] * full[:, :1024], axis=1, keepdims=True)
        + jnp.sum(weights[1] * full[:, 2048:2304], axis=1, keepdims=True)
        + jnp.sum(weights[2] * full[:, 2304:2560], axis=1, keepdims=True)
    ) / gains
    out_ref[:, :TOTAL] = full
    out_ref[:, TOTAL:] = jnp.broadcast_to(of_gain, (8, 128))


def sum_over_devices(left, right, context, d_out, normed, pair, rest, gain, wq, wk, wv):
    widths = (1024, 1024, 512, 256)
    scratch = [pltpu.VMEM((16, 2, 32, n), F32) for n in widths[:3]]
    scratch += [pltpu.VMEM((16, 32, n), F32) for n in widths]
    halves = [sum(w) // 2 for w in WIDTHS]
    scratch += [pltpu.VMEM((2, 4, 4, 4, 8, n), F32) for n in halves]
    for n in halves:
        for stage in range(3):
            tail = (4,) * (2 - stage) + (8, n)
            scratch += [pltpu.VMEM((6,) + tail, F32), pltpu.VMEM((2,) + tail, F32)]
    scratch += [pltpu.VMEM((16, n), BF16) for n in (1024, 256, 256)]
    scratch += [pltpu.VMEM((8, TOTAL // 2), F32)] * 3
    scratch += [
        pltpu.SemaphoreType.DMA((13,)),
        pltpu.SemaphoreType.DMA((13,)),
        pltpu.SemaphoreType.DMA((9, 6)),
        pltpu.SemaphoreType.DMA((9, 6)),
        pltpu.SemaphoreType.DMA((2,)),
        pltpu.SemaphoreType.DMA((3,)),
    ]
    return pl.pallas_call(
        sum_kernel,
        out_shape=jax.ShapeDtypeStruct((8, TOTAL + 128), F32),
        in_specs=[VMEM_SPEC] * 8 + [pl.BlockSpec(memory_space=pl.ANY)] * 3,
        out_specs=VMEM_SPEC,
        scratch_shapes=scratch,
        compiler_params=pltpu.CompilerParams(
            collective_id=2, has_side_effects=True, vmem_limit_bytes=60 << 20
        ),
        name="sum_over_devices",
    )(left, right, context, d_out, normed, pair, rest.reshape(16, 2, 32, 256), gain, wq, wk, wv)


def finish_kernel(full, gq, go, gk, gv, gain, gate, memory):
    gq[...] = full[:4, :1024]
    go[...] = full[:4, 1024:2048]
    gk[...] = full[:4, 2048:2304]
    gv[...] = full[:4, 2304:2560]
    rows = jnp.concatenate([full[:, 2560:2688]] + [jnp.zeros((120, 128), F32)], axis=0)
    memory[...] = jnp.transpose(rows)[:, :4]
    for ref, start in ((gate, 2688), (gain, TOTAL)):
        rows = jnp.concatenate([full[:, start : start + 128], jnp.zeros((120, 128), F32)], axis=0)
        ref[...] = jnp.transpose(rows)[:1, :4]


WIDE = 1152


def joined(earlier, later):
    keep = later[:, 1024:]
    gain = jnp.concatenate([keep] * 9, axis=1)
    added = jnp.concatenate([later[:, :1024], jnp.zeros_like(keep)], axis=1)
    return gain * earlier + added


def identity_rows(rows):
    return jnp.concatenate(
        [jnp.zeros((rows, 1024), jnp.float32), jnp.ones((rows, 128), jnp.float32)], axis=1
    )


def scan_kernel(reverse, add_ref, keep_ref, out_ref, own, mate, pair, xs, zs, backs, down, up, far, send, receive):
    core, x, zl = lax.axis_index("c"), lax.axis_index("x"), lax.axis_index("zl")
    other = {"c": 1 - core}
    x_peers = [{"x": lax.rem(x + k, 4)} for k in (1, 2, 3)]
    z_peers = [{"zl": lax.rem(zl + k, 4)} for k in (1, 2, 3)]
    own[:, :1024] = add_ref[...]
    own[:, 1024:] = keep_ref[...]
    greet([other] + x_peers + z_peers)

    def rows_of(start, count):
        return pl.ds(pl.multiple_of(start, count), count)

    mine = rows_of(core * 64, 64)
    theirs = rows_of((1 - core) * 64, 64)
    copies = []

    def push(source, target, device):
        n = len(copies)
        copy = remote(source, target, send.at[n], receive.at[n], device)
        copy.start()
        copies.append(copy)
        return copy

    push(own.at[theirs], mate, other).wait_recv()
    leads = core == (1 if reverse else 0)
    kept, got = own[mine], mate[...]
    earlier = jnp.where(leads, kept, got)
    pair[...] = joined(earlier, jnp.where(leads, got, kept))
    started = [
        push(pair.at[rows_of(lax.rem(x + k, 4) * 16, 16)], xs.at[x], x_peers[k - 1])
        for k in (1, 2, 3)
    ]
    xs[x] = pair[rows_of(x * 16, 16)]
    for copy in started:
        copy.wait_recv()
    order = (3, 2, 1, 0) if reverse else (0, 1, 2, 3)
    inside = {}
    running = None
    for k in order:
        inside[k] = running
        running = xs[k] if running is None else joined(running, xs[k])
    zs[zl] = running
    started = [push(zs.at[zl], zs.at[zl], z_peers[k - 1]) for k in (1, 2, 3)]
    for copy in started:
        copy.wait_recv()
    before = identity_rows(16)
    for k in order[:3]:
        passed = k > zl if reverse else k < zl
        before = jnp.where(passed, joined(before, zs[k]), before)
    for k in order:
        backs[k] = before if inside[k] is None else joined(before, inside[k])
    started = [
        push(backs.at[lax.rem(x + k, 4)], down.at[rows_of(x * 16, 16)], x_peers[k - 1])
        for k in (1, 2, 3)
    ]
    down[rows_of(x * 16, 16)] = backs[x]
    for copy in started:
        copy.wait_recv()
    lead = down[...]
    follow = joined(lead, earlier)
    up[...] = jnp.where(leads, follow, lead)
    last = push(up, far, other)
    out_ref[mine] = jnp.where(leads, lead, follow)
    last.wait_recv()
    out_ref[theirs] = far[...]
    for copy in copies:
        copy.wait_send()


def entering(keep, added, reverse):
    f32 = jnp.float32
    out = pl.pallas_call(
        functools.partial(scan_kernel, reverse),
        out_shape=jax.ShapeDtypeStruct((128, WIDE), f32),
        in_specs=[VMEM_SPEC] * 2,
        out_specs=VMEM_SPEC,
        scratch_shapes=[
            pltpu.VMEM((128, WIDE), f32),
            pltpu.VMEM((64, WIDE), f32),
            pltpu.VMEM((64, WIDE), f32),
            pltpu.VMEM((4, 16, WIDE), f32),
            pltpu.VMEM((4, 16, WIDE), f32),
            pltpu.VMEM((4, 16, WIDE), f32),
            pltpu.VMEM((64, WIDE), f32),
            pltpu.VMEM((64, WIDE), f32),
            pltpu.VMEM((64, WIDE), f32),
            pltpu.SemaphoreType.DMA((11,)),
            pltpu.SemaphoreType.DMA((11,)),
        ],
        compiler_params=pltpu.CompilerParams(
            collective_id=1 if reverse else 0, has_side_effects=True
        ),
        name="suffix" if reverse else "prefix",
    )(added, keep)
    return out


epsilon = 1e-05
score_scale = 0.125
GROUPS, SHARED, SEG = 4, 4, 128


def mul(a, b):
    return lax.dot_general(a, b, (((1,), (0,)), ((), ())), preferred_element_type=F32)


def mul_nt(a, b):
    return lax.dot_general(a, b, (((1,), (1,)), ((), ())), preferred_element_type=F32)


def mul_tn(a, b):
    return lax.dot_general(a, b, (((0,), (0,)), ((), ())), preferred_element_type=F32)


def inverse_of(rows):
    return lax.rsqrt(jnp.mean(rows * rows, axis=-1, keepdims=True) + epsilon)


def normalize(rows, gain):
    return (rows * inverse_of(rows) * gain).astype(BF16)


def normalize_back(rows, gain, d_normed):
    inverse = inverse_of(rows)
    scaled = d_normed * gain
    shared = jnp.mean(scaled * rows, axis=-1, keepdims=True)
    return inverse * scaled - rows * (inverse * inverse * inverse * shared)


def stacked(rows, group):
    start = group * SHARED * HEAD
    return jnp.concatenate(
        [rows[:, start + k * HEAD : start + (k + 1) * HEAD] for k in range(SHARED)], axis=0
    )


def side_by_side(rows):
    return jnp.concatenate([rows[k * SEG : (k + 1) * SEG] for k in range(SHARED)], axis=1)


def of_group(rows, group):
    return rows[:, group * HEAD : (group + 1) * HEAD]


def weights_of(queries, keys, allowed):
    scores = jnp.where(allowed, mul_nt(queries, keys), -1e30)
    raised = jnp.exp(scores - jnp.max(scores, axis=-1, keepdims=True))
    return raised / jnp.sum(raised, axis=-1, keepdims=True)


def attend_back(weights, rounded, queries, keys, values, d_context):
    d_values = mul_tn(rounded, d_context)
    d_weights = mul_nt(d_context, values).astype(BF16).astype(F32)
    pulled = jnp.sum(d_weights * weights, axis=-1, keepdims=True)
    d_scores = (weights * (d_weights - pulled)).astype(BF16)
    return mul(d_scores, keys).astype(BF16), mul_tn(d_scores, queries), d_values


def write_kernel(
    length_ref, x_ref, wq_ref, wk_ref, wv_ref, wo_ref, gain_ref, vector_ref, bias_ref, start_ref,
    q_ref, k_ref, v_ref, left_ref, sq_ref, p_ref, context_ref, written_ref, retain_ref,
    added_ref,
):
    length = length_ref[0, 0]
    gain = gain_ref[...]
    xn = normalize(x_ref[...].astype(F32), gain)
    sn = normalize(start_ref[...].astype(F32), gain)
    left = jnp.concatenate([xn, sn], axis=0)
    left_ref[...] = left
    both = (mul(left, wq_ref[...]) * score_scale).astype(BF16)
    q_ref[...] = both[:SEG]
    sq = both[SEG:]
    sq_ref[...] = sq
    keys = mul(xn, wk_ref[...]).astype(BF16)
    values = mul(xn, wv_ref[...]).astype(BF16)
    k_ref[...] = keys
    v_ref[...] = values
    allowed = lax.broadcasted_iota(jnp.int32, (SHARED * SEG, SEG), 1) < length
    contexts = []
    for group in range(GROUPS):
        weights = weights_of(stacked(sq, group), of_group(keys, group), allowed).astype(BF16)
        p_ref[group] = weights
        contexts.append(side_by_side(mul(weights, of_group(values, group)).astype(BF16)))
    context = jnp.concatenate(contexts, axis=1)
    context_ref[...] = context
    written = mul(context, wo_ref[...])
    written_ref[...] = written
    bias = jnp.transpose(jnp.broadcast_to(bias_ref[...], (128, 128)))[:, :1]
    logits = jnp.sum(written * vector_ref[...], axis=-1, keepdims=True) + bias
    retain = jax.nn.sigmoid(logits)
    retain_ref[...] = jnp.broadcast_to(retain, (SEG, 128))
    added_ref[...] = (1.0 - retain) * written


def read_kernel(
    length_ref, x_ref, cot_ref, wk_ref, wv_ref, wo_ref, gain_ref, start_ref, scan_ref,
    q_ref, k_ref, v_ref,
    out_ref, memory_ref, mn_ref, context_ref, dr_ref, dq_ref, dk_ref, dv_ref, dmk_ref, dmv_ref,
    r_ref,
):
    length = length_ref[0, 0]
    gain = gain_ref[...]
    memory = scan_ref[:, 1024:1025] * start_ref[...].astype(F32) + scan_ref[:, :1024]
    memory_ref[...] = memory
    mn = normalize(memory, gain)
    mn_ref[...] = mn
    keys = jnp.concatenate([mul(mn, wk_ref[...]).astype(BF16), k_ref[...]], axis=0)
    values = jnp.concatenate([mul(mn, wv_ref[...]).astype(BF16), v_ref[...]], axis=0)
    valid = lax.broadcasted_iota(jnp.int32, (SEG, 1024), 0) < length
    d_result = jnp.where(valid, cot_ref[...].astype(F32), 0.0).astype(BF16)
    dr_ref[...] = d_result
    d_context = mul_nt(d_result, wo_ref[...]).astype(BF16)
    shape = (SHARED * SEG, 2 * SEG)
    place = lax.broadcasted_iota(jnp.int32, shape, 1) - SEG
    row = lax.rem(lax.broadcasted_iota(jnp.int32, shape, 0), SEG)
    allowed = (place < 0) | ((place <= row) & (place < length))
    queries = q_ref[...]
    contexts, d_queries, d_keys, d_values = [], [], [], []
    for group in range(GROUPS):
        q, k, v = stacked(queries, group), of_group(keys, group), of_group(values, group)
        weights = weights_of(q, k, allowed)
        rounded = weights.astype(BF16)
        contexts.append(side_by_side(mul(rounded, v).astype(BF16)))
        dq, dk, dv = attend_back(weights, rounded, q, k, v, stacked(d_context, group))
        d_queries.append(side_by_side(dq))
        d_keys.append(dk.astype(BF16))
        d_values.append(dv.astype(BF16))
    context = jnp.concatenate(contexts, axis=1)
    context_ref[...] = context
    out_ref[...] = (x_ref[...].astype(F32) + mul(context, wo_ref[...])).astype(BF16)
    dq_ref[...] = jnp.concatenate(d_queries, axis=1)
    d_key = jnp.concatenate(d_keys, axis=1)
    d_value = jnp.concatenate(d_values, axis=1)
    dmk_ref[...] = d_key[:SEG]
    dmv_ref[...] = d_value[:SEG]
    dk_ref[...] = d_key[SEG:]
    dv_ref[...] = d_value[SEG:]
    d_mn = mul_nt(d_key[:SEG], wk_ref[...]) + mul_nt(d_value[:SEG], wv_ref[...])
    r_ref[...] = normalize_back(memory, gain, d_mn.astype(BF16).astype(F32))


def back_kernel(
    later_ref, memory_ref, written_ref, retain_ref, vector_ref, wq_ref, wo_ref, gain_ref,
    start_ref, scan_ref, r_ref, p_ref, sq_ref, k_ref, v_ref, left_ref, mn_ref,
    cr_ref, cw_ref, dr_ref, dq_ref, dk_ref, dv_ref, dmk_ref, dmv_ref,
    right_ref, context_ref, dout_ref, normed_ref, pair_ref, rest_ref,
):
    later = later_ref[:, :1024]
    written = written_ref[...]
    retain = retain_ref[:, :1]
    d_retain = jnp.sum(later * (memory_ref[...] - written), axis=-1, keepdims=True)
    d_logit = d_retain * retain * (1.0 - retain)
    gate = jnp.sum(written * d_logit, axis=0, keepdims=True)
    d_written = ((1.0 - retain) * later + d_logit * vector_ref[...]).astype(BF16)
    d_context = mul_nt(d_written, wo_ref[...]).astype(BF16)
    slots, keys, values = sq_ref[...], k_ref[...], v_ref[...]
    d_slots, d_keys, d_values = [], [], []
    for group in range(GROUPS):
        rounded = p_ref[group]
        dq, dk, dv = attend_back(
            rounded.astype(F32), rounded, stacked(slots, group), of_group(keys, group),
            of_group(values, group), stacked(d_context, group),
        )
        d_slots.append(side_by_side(dq))
        d_keys.append(dk.astype(BF16))
        d_values.append(dv.astype(BF16))

    def added(first, second):
        return (first.astype(F32) + second.astype(F32)).astype(BF16)

    scale = jnp.asarray(score_scale, BF16)
    d_slot = jnp.concatenate(d_slots, axis=1) * scale
    right_ref[:SEG] = dq_ref[...] * scale
    right_ref[SEG:] = d_slot
    pair_ref[:SEG, :256] = added(dk_ref[...], jnp.concatenate(d_keys, axis=1))
    pair_ref[:SEG, 256:] = added(dv_ref[...], jnp.concatenate(d_values, axis=1))
    pair_ref[SEG:, :256] = dmk_ref[...]
    pair_ref[SEG:, 256:] = dmv_ref[...]
    normed_ref[:SEG] = left_ref[:SEG]
    normed_ref[SEG:] = mn_ref[...]
    context_ref[:SEG] = cr_ref[...]
    context_ref[SEG:] = cw_ref[...]
    dout_ref[:SEG] = dr_ref[...]
    dout_ref[SEG:] = d_written
    d_sn = mul_nt(d_slot, wq_ref[...]).astype(BF16).astype(F32)
    start = start_ref[...].astype(F32)
    total = normalize_back(start, gain_ref[...], d_sn) + scan_ref[:, 1024:1025] * r_ref[...]
    gates = jnp.broadcast_to(gate, (128, 1024))
    for block in range(8):
        rows = slice(block * 128, block * 128 + 128)
        rest_ref[rows, :128] = jnp.transpose(total[:, rows])
        rest_ref[rows, 128:] = jnp.transpose(gates[:, rows])


def local_kernel(kernel, shapes, operands, name):
    smem = pl.BlockSpec(memory_space=pltpu.SMEM)
    return pl.pallas_call(
        kernel,
        out_shape=[jax.ShapeDtypeStruct(shape, dtype) for shape, dtype in shapes],
        in_specs=[smem if a.dtype == jnp.int32 else VMEM_SPEC for a in operands],
        out_specs=[VMEM_SPEC] * len(shapes),
        compiler_params=pltpu.CompilerParams(vmem_limit_bytes=60 << 20),
        name=name,
    )(*operands)


def per_device(
    segments,
    lengths,
    query_weight,
    key_weight,
    value_weight,
    out_weight,
    norm_gain,
    gate_vector,
    gate_bias,
    memory_init,
    cotangent,
):
    segment, cot = segments[0, 0], cotangent[0, 0]
    gain, vector, bias = norm_gain[None], gate_vector[None], gate_bias[None]
    wide, narrow = ((SEG, 1024), BF16), ((SEG, 256), BF16)
    full, double = ((SEG, 1024), F32), ((2 * SEG, 1024), BF16)
    q, k, v, left, sq, p, cw, written, retain, added = local_kernel(
        write_kernel,
        [wide, narrow, narrow, double, wide, ((GROUPS, SHARED * SEG, SEG), BF16), wide, full,
         ((SEG, 128), F32), full],
        (lengths, segment, query_weight, key_weight, value_weight, out_weight, gain, vector, bias,
         memory_init),
        "write_forward",
    )
    scan = entering(retain, added, False)
    output, memory, mn, cr, dr, dq, dk, dv, dmk, dmv, r = local_kernel(
        read_kernel,
        [wide, full, wide, wide, wide, wide, narrow, narrow, narrow, narrow, full],
        (lengths, segment, cot, key_weight, value_weight, out_weight, gain, memory_init, scan, q,
         k, v),
        "read_both",
    )
    later = entering(retain, r, True)
    right, context, d_out, normed, pair, rest = local_kernel(
        back_kernel,
        [double, double, double, double, ((2 * SEG, 512), BF16), ((1024, 256), F32)],
        (later, memory, written, retain, vector, query_weight, out_weight, gain, memory_init, scan,
         r, p, sq, k, v, left, mn, cr, cw, dr, dq, dk, dv, dmk, dmv),
        "write_backward",
    )
    summed = sum_over_devices(
        left, right, context, d_out, normed, pair, rest, gain, query_weight, key_weight,
        value_weight,
    )
    grad_query, grad_out, grad_key, grad_value, grad_gain, grad_gate, grad_memory = local_kernel(
        finish_kernel,
        [((4, n), F32) for n in (1024, 1024, 256, 256)]
        + [((1, 4), F32), ((1, 4), F32), ((128, 4), F32)],
        (summed,),
        "finish",
    )
    grad_gain, grad_gate = grad_gain[0], grad_gate[0]
    return (
        output[None, None],
        grad_query,
        grad_key,
        grad_value,
        grad_out,
        grad_gain,
        grad_gate,
        grad_memory,
    )


def solution(mesh):
    split = Mesh(mesh.devices.reshape(4, 4, 2, 2, 4), AXES)
    rows = P(("zh", "y"), ("zl", "x", "c"), None, None)
    return jax.shard_map(
        per_device,
        mesh=split,
        in_specs=(rows, P(("zh", "y"), ("zl", "x", "c"))) + (P(),) * 8 + (rows,),
        out_specs=(
            rows,
            P(AXES, None),
            P(AXES, None),
            P(AXES, None),
            P(AXES, None),
            P(AXES),
            P(AXES),
            P(None, AXES),
        ),
        check_vma=False,
    )
```

```python
import functools

import jax
import jax.numpy as jnp
from jax import lax
from jax.experimental import pallas as pl
from jax.experimental.pallas import tpu as pltpu
from jax.sharding import Mesh
from jax.sharding import PartitionSpec as P

HEAD = 64
F32, BF16 = jnp.float32, jnp.bfloat16
AXES = ("zl", "x", "c", "zh", "y")
MESH = pl.DeviceIdType.MESH
VMEM_SPEC = pl.BlockSpec(memory_space=pltpu.VMEM)


def z_shift(step):
    place = lax.rem(lax.axis_index("zh") * 4 + lax.axis_index("zl") + step, 8)
    return {"zh": lax.div(place, 4), "zl": lax.rem(place, 4)}


def shift(axis, step):
    if axis == "z":
        return z_shift(step % 8)
    return {axis: lax.rem(lax.axis_index(axis) + step % 4, 4)}


def place_of(axis):
    return lax.axis_index("zl" if axis == "z" else axis)


def remote(source, target, send, receive, device):
    return pltpu.make_async_remote_copy(
        src_ref=source,
        dst_ref=target,
        send_sem=send,
        recv_sem=receive,
        device_id=device,
        device_id_type=MESH,
    )


class Ring:
    def __init__(self, axis, work, landing, out, send, receive):
        self.work, self.landing, self.out = work, landing, out
        self.send, self.receive = send, receive
        self.me = place_of(axis)
        self.up, self.down = shift(axis, 1), shift(axis, -1)
        self.copies = []

    def at(self, step):
        return lax.rem(self.me + step, 4)

    def push(self, half, step, device):
        slot = len(self.copies)
        copy = remote(
            self.work.at[half, self.at(step)],
            self.landing.at[slot],
            self.send.at[slot],
            self.receive.at[slot],
            device,
        )
        copy.start()
        self.copies.append(copy)

    def first(self):
        self.push(0, 2, self.up)
        self.push(1, 2, self.down)
        self.push(1, 1, self.up)
        self.push(0, 3, self.down)

    def second(self):
        for half, step, device in ((0, 1, self.up), (1, 3, self.down)):
            self.copies[half].wait_recv()
            self.work[half, self.at(step)] += self.landing[half]
            self.push(half, step, device)

    def finish(self):
        for slot in range(2, 6):
            self.copies[slot].wait_recv()
        self.out[0] = self.work[0, self.me] + self.landing[3] + self.landing[4]
        self.out[1] = self.work[1, self.me] + self.landing[2] + self.landing[5]

    def drain(self):
        for copy in self.copies:
            copy.wait_send()


class Direct:
    def __init__(self, axis, work, landing, out, send, receive):
        self.work, self.landing, self.out = work, landing, out
        self.send, self.receive = send, receive
        self.me = place_of(axis)
        self.steps = ((2, shift(axis, 2)), (1, shift(axis, 1)), (3, shift(axis, -1)))
        self.copies = []

    def first(self):
        for slot, (step, device) in enumerate(self.steps):
            copy = remote(
                self.work.at[:, lax.rem(self.me + step, 4)],
                self.landing.at[slot],
                self.send.at[slot],
                self.receive.at[slot],
                device,
            )
            copy.start()
            self.copies.append(copy)

    def second(self):
        pass

    def finish(self):
        for copy in self.copies:
            copy.wait_recv()
        self.out[...] = (
            self.work[:, self.me] + self.landing[0] + self.landing[1] + self.landing[2]
        )

    def drain(self):
        for copy in self.copies:
            copy.wait_send()


ORDERS = (("x", "y", "z"), ("y", "z", "x"), ("z", "x", "y"))
PARTS = 6
WIDTHS = (512, 512, 512, 512, 512, 256)
TOTAL = 2816


def sum_kernel(*refs):
    left, right, context, d_out, normed, pair, rest, gain, wq, wk, wv = refs[:11]
    out_ref, refs = refs[11], refs[12:]
    products, refs = refs[:5], refs[5:]
    landed, refs = refs[:6], refs[6:]
    works, refs = refs[:6], refs[6:]
    rings_of, refs = refs[:36], refs[36:]
    rows_of, refs = refs[:3], refs[3:]
    sent, mate, fold_in, refs = refs[:2], refs[2:4], refs[4:6], refs[6:]
    core_send, core_receive, ring_send, ring_receive, fold_sems, row_sems = refs
    core = lax.axis_index("c")
    other = {"c": 1 - core}
    far = z_shift(4)
    place = lax.axis_index(AXES)
    base = pl.ds(pl.multiple_of(lax.div(place, 4) * 16, 16), 16)
    row_copies = [
        pltpu.make_async_copy(w.at[base], rows, row_sems.at[k])
        for k, (w, rows) in enumerate(zip((wq, wk, wv), rows_of))
    ]
    for copy in row_copies:
        copy.start()
    peers = [other, far, shift("x", 2), shift("y", 2), shift("z", 2), shift("z", -2)]
    peers += [shift(axis, step) for axis in ("x", "y", "z") for step in (1, -1)]
    barrier = pltpu.get_barrier_semaphore()
    for device in peers:
        pl.semaphore_signal(barrier, inc=1, device_id=device, device_id_type=MESH)
    core_copies = []

    def push_core(source, target):
        n = len(core_copies)
        copy = remote(source, target, core_send.at[n], core_receive.at[n], other)
        copy.start()
        core_copies.append(copy)

    def product_and_push(part):
        factor, other_factor, start = (
            (left, right, 0),
            (context, d_out, 0),
            (normed, pair, 0),
            (left, right, 512),
            (context, d_out, 512),
        )[part]
        for block in range(4):
            value = mul_tn(
                factor[:, block * 256 : block * 256 + 256], other_factor[:, start : start + 512]
            )
            products[part][block * 4 : block * 4 + 4] = value.reshape(4, 2, 32, 512)
            if part == 0 and block == 0:
                pl.semaphore_wait(barrier, len(peers))
            if block % 2 == 1:
                blocks = pl.ds((block - 1) * 4, 8)
                push_core(products[part].at[blocks, 1 - core], landed[part].at[blocks])

    sources = tuple(products) + (rest,)

    def build_part(part):
        order, work = ORDERS[part % 3], works[part]
        half_width = WIDTHS[part] // 2

        def build(zl, carry):
            for x in range(4):
                block = zl * 4 + x
                for col in range(0, WIDTHS[part], 128):
                    cols = pl.ds(col, 128)
                    half = col // half_width
                    to = pl.ds(col % half_width, 128)
                    rows = sources[part][block, core, :, cols] + landed[part][block, :, cols]
                    low = lax.broadcasted_iota(jnp.int32, (8, 128), 0) < 4
                    for pair_at in range(2):
                        a = rows[pair_at * 8 : pair_at * 8 + 8]
                        b = rows[16 + pair_at * 8 : 24 + pair_at * 8]
                        tiles = (
                            jnp.where(low, a, pltpu.roll(b, 4, 0)),
                            jnp.where(low, pltpu.roll(a, 4, 0), b),
                        )
                        for bit in range(2):
                            where = {"z": zl, "x": x, "y": pair_at * 2 + bit}
                            index = (half,) + tuple(where[axis] for axis in order)
                            work[index + (slice(None), to)] = tiles[bit]
            return carry

        lax.fori_loop(0, 4, build, 0)

    rings = []

    def begin(part, waited):
        for n in waited:
            core_copies[n].wait_recv()
        build_part(part)
        stages = []
        for stage in range(3):
            n = part * 3 + stage
            stages.append(
                (Direct if stage else Ring)(
                    ORDERS[part % 3][stage],
                    works[part] if stage == 0 else rings_of[2 * (n - 1) + 1],
                    rings_of[2 * n],
                    rings_of[2 * n + 1],
                    ring_send.at[n],
                    ring_receive.at[n],
                )
            )
        rings.append(stages)
        stages[0].first()

    early, late = (0, 1, 2), (3, 4, 5)

    def second(parts, stage):
        for part in parts:
            rings[part][stage].second()

    def finish(parts, stage):
        for part in parts:
            rings[part][stage].finish()
            if stage < 2:
                rings[part][stage + 1].first()

    high = lax.axis_index("zh")
    folds = []

    def fold(parts, which):
        total = jnp.concatenate(
            [rings_of[2 * (part * 3 + 2) + 1][half] for part in parts for half in range(2)],
            axis=1,
        )
        turned = pltpu.roll(total, 4, 0)
        middle = total.shape[1] // 2
        top = lax.broadcasted_iota(jnp.int32, (8, middle), 0) < 4
        straight = jnp.where(top, total[:, :middle], turned[:, middle:])
        crossed = jnp.where(top, turned[:, :middle], total[:, middle:])
        sent[which][...] = jnp.where(high == 1, straight, crossed)
        mate[which][...] = jnp.where(high == 0, straight, crossed)
        copy = remote(
            sent[which], fold_in[which], fold_sems.at[which, 0], fold_sems.at[which, 1], far
        )
        copy.start()
        folds.append(copy)

    product_and_push(0)
    product_and_push(1)
    product_and_push(2)
    begin(0, (0, 1))
    product_and_push(3)
    begin(1, (2, 3))
    product_and_push(4)
    begin(2, (4, 5))
    push_core(rest.at[:, 1 - core], landed[5])
    begin(3, (6, 7))
    second(early, 0)
    begin(4, (8, 9))
    begin(5, (10,))
    finish(early, 0)
    second(late, 0)
    finish(early, 1)
    finish(late, 0)
    finish(early, 2)
    fold(early, 0)
    finish(late, 1)
    finish(late, 2)
    fold(late, 1)
    for copy in core_copies:
        copy.wait_send()
    for stages in rings:
        for ring in stages:
            ring.drain()
    for copy in row_copies:
        copy.wait()
    part_of_16 = lax.rem(place, 4)
    weights = []
    for rows in rows_of:
        loaded = rows[...].astype(F32)
        tile = jnp.where(part_of_16 >= 2, loaded[8:], loaded[:8])
        weights.append(jnp.where(lax.rem(place, 2) == 1, pltpu.roll(tile, 4, 0), tile))
    spot = place * 4 + lax.broadcasted_iota(jnp.int32, (8, 1024), 0)
    here = lax.broadcasted_iota(jnp.int32, (8, 1024), 1) == spot
    low = lax.broadcasted_iota(jnp.int32, (8, 1), 0) < 4
    gains = jnp.sum(jnp.where(here, gain[...], 0.0), axis=1, keepdims=True)
    gains = jnp.where(low, gains, 1.0)
    pieces = []
    for which in range(2):
        folds[which].wait()
        short = mate[which][...] + fold_in[which][...]
        pieces += [short, pltpu.roll(short, 4, 0)]
    full = jnp.concatenate(pieces, axis=1)
    of_gain = (
        jnp.sum(weights[0][:, :512] * full[:, :512], axis=1, keepdims=True)
        + jnp.sum(weights[0][:, 512:] * full[:, 1536:2048], axis=1, keepdims=True)
        + jnp.sum(weights[1] * full[:, 1024:1280], axis=1, keepdims=True)
        + jnp.sum(weights[2] * full[:, 1280:1536], axis=1, keepdims=True)
    ) / gains
    out_ref[:, :TOTAL] = full
    out_ref[:, TOTAL:] = jnp.broadcast_to(of_gain, (8, 128))


def sum_over_devices(left, right, context, d_out, normed, pair, rest, gain, wq, wk, wv):
    scratch = [pltpu.VMEM((16, 2, 32, n), F32) for n in WIDTHS[:5]]
    scratch += [pltpu.VMEM((16, 32, n), F32) for n in WIDTHS]
    scratch += [pltpu.VMEM((2, 4, 4, 4, 8, n // 2), F32) for n in WIDTHS]
    for n in WIDTHS:
        for stage in range(3):
            tail = (4,) * (2 - stage) + (8, n // 2)
            lands = (3, 2) if stage else (6,)
            scratch += [pltpu.VMEM(lands + tail, F32), pltpu.VMEM((2,) + tail, F32)]
    scratch += [pltpu.VMEM((16, n), BF16) for n in (1024, 256, 256)]
    scratch += [pltpu.VMEM((8, n), F32) for n in (768, 640)] * 3
    scratch += [
        pltpu.SemaphoreType.DMA((11,)),
        pltpu.SemaphoreType.DMA((11,)),
        pltpu.SemaphoreType.DMA((18, 6)),
        pltpu.SemaphoreType.DMA((18, 6)),
        pltpu.SemaphoreType.DMA((2, 2)),
        pltpu.SemaphoreType.DMA((3,)),
    ]
    return pl.pallas_call(
        sum_kernel,
        out_shape=jax.ShapeDtypeStruct((8, TOTAL + 128), F32),
        in_specs=[VMEM_SPEC] * 8 + [pl.BlockSpec(memory_space=pl.ANY)] * 3,
        out_specs=VMEM_SPEC,
        scratch_shapes=scratch,
        compiler_params=pltpu.CompilerParams(
            collective_id=2, has_side_effects=True, vmem_limit_bytes=60 << 20
        ),
        name="sum_over_devices",
    )(left, right, context, d_out, normed, pair, rest.reshape(16, 2, 32, 256), gain, wq, wk, wv)


def finish_kernel(full, gq, go, gk, gv, gain, gate, memory):
    gq[:, :512] = full[:4, :512]
    gq[:, 512:] = full[:4, 1536:2048]
    go[:, :512] = full[:4, 512:1024]
    go[:, 512:] = full[:4, 2048:2560]
    gk[...] = full[:4, 1024:1280]
    gv[...] = full[:4, 1280:1536]
    memory[...] = full[:4, 2560:2688]
    for ref, start in ((gate, 2688), (gain, TOTAL)):
        rows = jnp.concatenate([full[:, start : start + 128], jnp.zeros((120, 128), F32)], axis=0)
        ref[...] = jnp.transpose(rows)[:1, :4]


WIDE = 1152


def joined(earlier, later):
    keep = later[:, 1024:]
    gain = jnp.concatenate([keep] * 9, axis=1)
    added = jnp.concatenate([later[:, :1024], jnp.zeros_like(keep)], axis=1)
    return gain * earlier + added


def identity_rows(rows):
    return jnp.concatenate(
        [jnp.zeros((rows, 1024), jnp.float32), jnp.ones((rows, 128), jnp.float32)], axis=1
    )


CHUNKS = 2
CORE_ROWS, X_ROWS = 32, 8


def scan_kernel(
    reverse, add_ref, keep_ref, out_ref, own, mate, pair, xs, zs, backs, down, up, far, send,
    receive,
):
    core, x, zl = lax.axis_index("c"), lax.axis_index("x"), lax.axis_index("zl")
    other = {"c": 1 - core}
    x_peers = [{"x": lax.rem(x + k, 4)} for k in (1, 2, 3)]
    z_peers = [{"zl": lax.rem(zl + k, 4)} for k in (1, 2, 3)]
    peers = [other] + x_peers + z_peers
    barrier = pltpu.get_barrier_semaphore()
    for device in peers:
        pl.semaphore_signal(barrier, inc=1, device_id=device, device_id_type=MESH)
    own[:, :1024] = add_ref[...]
    own[:, 1024:] = keep_ref[...]
    pl.semaphore_wait(barrier, len(peers))
    order = (3, 2, 1, 0) if reverse else (0, 1, 2, 3)
    leads = core == (1 if reverse else 0)
    all_copies = []

    def chunk_of(chunk):
        copies = []

        def push(source, target, device):
            n = len(copies)
            copy = remote(source, target, send.at[chunk, n], receive.at[chunk, n], device)
            copy.start()
            copies.append(copy)
            all_copies.append(copy)
            return copy

        def rows_of(start, count):
            return pl.ds(pl.multiple_of(start, count), count)

        mine = rows_of(chunk * 2 * CORE_ROWS + core * CORE_ROWS, CORE_ROWS)
        theirs = rows_of(chunk * 2 * CORE_ROWS + (1 - core) * CORE_ROWS, CORE_ROWS)
        at_x = [rows_of(lax.rem(x + k, 4) * X_ROWS, X_ROWS) for k in range(4)]
        started = push(own.at[theirs], mate.at[chunk], other)
        yield
        started.wait_recv()
        kept, got = own[mine], mate[chunk]
        earlier = jnp.where(leads, kept, got)
        pair[chunk] = joined(earlier, jnp.where(leads, got, kept))
        started = [
            push(pair.at[chunk, at_x[k]], xs.at[chunk, x], x_peers[k - 1]) for k in (2, 1, 3)
        ]
        xs[chunk, x] = pair[chunk, at_x[0]]
        yield
        for copy in started:
            copy.wait_recv()
        inside = {}
        running = None
        for k in order:
            inside[k] = running
            running = xs[chunk, k] if running is None else joined(running, xs[chunk, k])
        zs[chunk, zl] = running
        started = [
            push(zs.at[chunk, zl], zs.at[chunk, zl], z_peers[k - 1])
            for k in ((1, 2, 3) if reverse else (3, 2, 1))
        ]
        yield
        for copy in started:
            copy.wait_recv()
        before = identity_rows(X_ROWS)
        for k in order[:3]:
            passed = k > zl if reverse else k < zl
            before = jnp.where(passed, joined(before, zs[chunk, k]), before)
        for k in order:
            backs[chunk, k] = before if inside[k] is None else joined(before, inside[k])
        started = [
            push(backs.at[chunk, lax.rem(x + k, 4)], down.at[chunk, at_x[0]], x_peers[k - 1])
            for k in (2, 1, 3)
        ]
        down[chunk, at_x[0]] = backs[chunk, x]
        yield
        for copy in started:
            copy.wait_recv()
        lead = down[chunk]
        follow = joined(lead, earlier)
        up[chunk] = jnp.where(leads, follow, lead)
        started = push(up.at[chunk], far.at[chunk], other)
        out_ref[mine] = jnp.where(leads, lead, follow)
        yield
        started.wait_recv()
        out_ref[theirs] = far[chunk]

    running = [chunk_of(chunk) for chunk in range(CHUNKS)]
    for step in range(6):
        for steps in running:
            next(steps, None)
    for copy in all_copies:
        copy.wait_send()


def entering(keep, added, reverse):
    f32 = jnp.float32
    out = pl.pallas_call(
        functools.partial(scan_kernel, reverse),
        out_shape=jax.ShapeDtypeStruct((128, WIDE), f32),
        in_specs=[VMEM_SPEC] * 2,
        out_specs=VMEM_SPEC,
        scratch_shapes=[
            pltpu.VMEM((128, WIDE), f32),
            pltpu.VMEM((CHUNKS, CORE_ROWS, WIDE), f32),
            pltpu.VMEM((CHUNKS, CORE_ROWS, WIDE), f32),
            pltpu.VMEM((CHUNKS, 4, X_ROWS, WIDE), f32),
            pltpu.VMEM((CHUNKS, 4, X_ROWS, WIDE), f32),
            pltpu.VMEM((CHUNKS, 4, X_ROWS, WIDE), f32),
            pltpu.VMEM((CHUNKS, CORE_ROWS, WIDE), f32),
            pltpu.VMEM((CHUNKS, CORE_ROWS, WIDE), f32),
            pltpu.VMEM((CHUNKS, CORE_ROWS, WIDE), f32),
            pltpu.SemaphoreType.DMA((CHUNKS, 11)),
            pltpu.SemaphoreType.DMA((CHUNKS, 11)),
        ],
        compiler_params=pltpu.CompilerParams(
            collective_id=1 if reverse else 0, has_side_effects=True
        ),
        name="suffix" if reverse else "prefix",
    )(added, keep)
    return out


epsilon = 1e-05
score_scale = 0.125
GROUPS, SHARED, SEG = 4, 4, 128


def mul(a, b):
    return lax.dot_general(a, b, (((1,), (0,)), ((), ())), preferred_element_type=F32)


def mul_nt(a, b):
    return lax.dot_general(a, b, (((1,), (1,)), ((), ())), preferred_element_type=F32)


def mul_tn(a, b):
    return lax.dot_general(a, b, (((0,), (0,)), ((), ())), preferred_element_type=F32)


def inverse_of(rows):
    return lax.rsqrt(jnp.mean(rows * rows, axis=-1, keepdims=True) + epsilon)


def normalize(rows, gain):
    return (rows * inverse_of(rows) * gain).astype(BF16)


def normalize_back(rows, gain, d_normed):
    inverse = inverse_of(rows)
    scaled = d_normed * gain
    shared = jnp.mean(scaled * rows, axis=-1, keepdims=True)
    return inverse * scaled - rows * (inverse * inverse * inverse * shared)


def stacked(rows, group):
    start = group * SHARED * HEAD
    return jnp.concatenate(
        [rows[:, start + k * HEAD : start + (k + 1) * HEAD] for k in range(SHARED)], axis=0
    )


def side_by_side(rows):
    return jnp.concatenate([rows[k * SEG : (k + 1) * SEG] for k in range(SHARED)], axis=1)


def of_group(rows, group):
    return rows[:, group * HEAD : (group + 1) * HEAD]


def weights_of(queries, keys, allowed):
    scores = jnp.where(allowed, mul_nt(queries, keys), -1e30)
    raised = jnp.exp(scores - jnp.max(scores, axis=-1, keepdims=True))
    return raised / jnp.sum(raised, axis=-1, keepdims=True)


def attend_back(weights, rounded, queries, keys, values, d_context):
    d_values = mul_tn(rounded, d_context)
    d_weights = mul_nt(d_context, values).astype(BF16).astype(F32)
    pulled = jnp.sum(d_weights * weights, axis=-1, keepdims=True)
    d_scores = (weights * (d_weights - pulled)).astype(BF16)
    return mul(d_scores, keys).astype(BF16), mul_tn(d_scores, queries), d_values


def write_kernel(
    length_ref, x_ref, wq_ref, wk_ref, wv_ref, wo_ref, gain_ref, vector_ref, bias_ref, start_ref,
    q_ref, k_ref, v_ref, left_ref, sq_ref, p_ref, context_ref, written_ref, retain_ref,
    added_ref,
):
    length = length_ref[0, 0]
    gain = gain_ref[...]
    xn = normalize(x_ref[...].astype(F32), gain)
    sn = normalize(start_ref[...].astype(F32), gain)
    left = jnp.concatenate([xn, sn], axis=0)
    left_ref[...] = left
    both = (mul(left, wq_ref[...]) * score_scale).astype(BF16)
    q_ref[...] = both[:SEG]
    sq = both[SEG:]
    sq_ref[...] = sq
    keys = mul(xn, wk_ref[...]).astype(BF16)
    values = mul(xn, wv_ref[...]).astype(BF16)
    k_ref[...] = keys
    v_ref[...] = values
    allowed = lax.broadcasted_iota(jnp.int32, (SHARED * SEG, SEG), 1) < length
    contexts = []
    for group in range(GROUPS):
        weights = weights_of(stacked(sq, group), of_group(keys, group), allowed).astype(BF16)
        p_ref[group] = weights
        contexts.append(side_by_side(mul(weights, of_group(values, group)).astype(BF16)))
    context = jnp.concatenate(contexts, axis=1)
    context_ref[...] = context
    written = mul(context, wo_ref[...])
    written_ref[...] = written
    bias = jnp.transpose(jnp.broadcast_to(bias_ref[...], (128, 128)))[:, :1]
    logits = jnp.sum(written * vector_ref[...], axis=-1, keepdims=True) + bias
    retain = jax.nn.sigmoid(logits)
    retain_ref[...] = jnp.broadcast_to(retain, (SEG, 128))
    added_ref[...] = (1.0 - retain) * written


def read_kernel(
    length_ref, x_ref, cot_ref, wk_ref, wv_ref, wo_ref, gain_ref, start_ref, scan_ref,
    q_ref, k_ref, v_ref,
    out_ref, memory_ref, mn_ref, context_ref, dr_ref, dq_ref, dk_ref, dv_ref, dmk_ref, dmv_ref,
    r_ref,
):
    length = length_ref[0, 0]
    gain = gain_ref[...]
    memory = scan_ref[:, 1024:1025] * start_ref[...].astype(F32) + scan_ref[:, :1024]
    memory_ref[...] = memory
    mn = normalize(memory, gain)
    mn_ref[...] = mn
    keys = jnp.concatenate([mul(mn, wk_ref[...]).astype(BF16), k_ref[...]], axis=0)
    values = jnp.concatenate([mul(mn, wv_ref[...]).astype(BF16), v_ref[...]], axis=0)
    valid = lax.broadcasted_iota(jnp.int32, (SEG, 1024), 0) < length
    d_result = jnp.where(valid, cot_ref[...].astype(F32), 0.0).astype(BF16)
    dr_ref[...] = d_result
    d_context = mul_nt(d_result, wo_ref[...]).astype(BF16)
    shape = (SHARED * SEG, 2 * SEG)
    place = lax.broadcasted_iota(jnp.int32, shape, 1) - SEG
    row = lax.rem(lax.broadcasted_iota(jnp.int32, shape, 0), SEG)
    allowed = (place < 0) | ((place <= row) & (place < length))
    queries = q_ref[...]
    contexts, d_queries, d_keys, d_values = [], [], [], []
    for group in range(GROUPS):
        q, k, v = stacked(queries, group), of_group(keys, group), of_group(values, group)
        weights = weights_of(q, k, allowed)
        rounded = weights.astype(BF16)
        contexts.append(side_by_side(mul(rounded, v).astype(BF16)))
        dq, dk, dv = attend_back(weights, rounded, q, k, v, stacked(d_context, group))
        d_queries.append(side_by_side(dq))
        d_keys.append(dk.astype(BF16))
        d_values.append(dv.astype(BF16))
    context = jnp.concatenate(contexts, axis=1)
    context_ref[...] = context
    out_ref[...] = (x_ref[...].astype(F32) + mul(context, wo_ref[...])).astype(BF16)
    dq_ref[...] = jnp.concatenate(d_queries, axis=1)
    d_key = jnp.concatenate(d_keys, axis=1)
    d_value = jnp.concatenate(d_values, axis=1)
    dmk_ref[...] = d_key[:SEG]
    dmv_ref[...] = d_value[:SEG]
    dk_ref[...] = d_key[SEG:]
    dv_ref[...] = d_value[SEG:]
    d_mn = mul_nt(d_key[:SEG], wk_ref[...]) + mul_nt(d_value[:SEG], wv_ref[...])
    r_ref[...] = normalize_back(memory, gain, d_mn.astype(BF16).astype(F32))


def back_kernel(
    later_ref, memory_ref, written_ref, retain_ref, vector_ref, wq_ref, wo_ref, gain_ref,
    start_ref, scan_ref, r_ref, p_ref, sq_ref, k_ref, v_ref, left_ref, mn_ref,
    cr_ref, cw_ref, dr_ref, dq_ref, dk_ref, dv_ref, dmk_ref, dmv_ref,
    right_ref, context_ref, dout_ref, normed_ref, pair_ref, rest_ref,
):
    later = later_ref[:, :1024]
    written = written_ref[...]
    retain = retain_ref[:, :1]
    d_retain = jnp.sum(later * (memory_ref[...] - written), axis=-1, keepdims=True)
    d_logit = d_retain * retain * (1.0 - retain)
    gate = jnp.sum(written * d_logit, axis=0, keepdims=True)
    d_written = ((1.0 - retain) * later + d_logit * vector_ref[...]).astype(BF16)
    d_context = mul_nt(d_written, wo_ref[...]).astype(BF16)
    slots, keys, values = sq_ref[...], k_ref[...], v_ref[...]
    d_slots, d_keys, d_values = [], [], []
    for group in range(GROUPS):
        rounded = p_ref[group]
        dq, dk, dv = attend_back(
            rounded.astype(F32), rounded, stacked(slots, group), of_group(keys, group),
            of_group(values, group), stacked(d_context, group),
        )
        d_slots.append(side_by_side(dq))
        d_keys.append(dk.astype(BF16))
        d_values.append(dv.astype(BF16))

    def added(first, second):
        return (first.astype(F32) + second.astype(F32)).astype(BF16)

    scale = jnp.asarray(score_scale, BF16)
    d_slot = jnp.concatenate(d_slots, axis=1) * scale
    right_ref[:SEG] = dq_ref[...] * scale
    right_ref[SEG:] = d_slot
    pair_ref[:SEG, :256] = added(dk_ref[...], jnp.concatenate(d_keys, axis=1))
    pair_ref[:SEG, 256:] = added(dv_ref[...], jnp.concatenate(d_values, axis=1))
    pair_ref[SEG:, :256] = dmk_ref[...]
    pair_ref[SEG:, 256:] = dmv_ref[...]
    normed_ref[:SEG] = left_ref[:SEG]
    normed_ref[SEG:] = mn_ref[...]
    context_ref[:SEG] = cr_ref[...]
    context_ref[SEG:] = cw_ref[...]
    dout_ref[:SEG] = dr_ref[...]
    dout_ref[SEG:] = d_written
    d_sn = mul_nt(d_slot, wq_ref[...]).astype(BF16).astype(F32)
    start = start_ref[...].astype(F32)
    total = normalize_back(start, gain_ref[...], d_sn) + scan_ref[:, 1024:1025] * r_ref[...]
    gates = jnp.broadcast_to(gate, (128, 1024))
    for block in range(8):
        rows = slice(block * 128, block * 128 + 128)
        rest_ref[rows, :128] = jnp.transpose(total[:, rows])
        rest_ref[rows, 128:] = jnp.transpose(gates[:, rows])


def local_kernel(kernel, shapes, operands, name):
    smem = pl.BlockSpec(memory_space=pltpu.SMEM)
    return pl.pallas_call(
        kernel,
        out_shape=[jax.ShapeDtypeStruct(shape, dtype) for shape, dtype in shapes],
        in_specs=[smem if a.dtype == jnp.int32 else VMEM_SPEC for a in operands],
        out_specs=[VMEM_SPEC] * len(shapes),
        compiler_params=pltpu.CompilerParams(vmem_limit_bytes=60 << 20),
        name=name,
    )(*operands)


def per_device(
    segments,
    lengths,
    query_weight,
    key_weight,
    value_weight,
    out_weight,
    norm_gain,
    gate_vector,
    gate_bias,
    memory_init,
    cotangent,
):
    segment, cot = segments[0, 0], cotangent[0, 0]
    gain, vector, bias = norm_gain[None], gate_vector[None], gate_bias[None]
    wide, narrow = ((SEG, 1024), BF16), ((SEG, 256), BF16)
    full, double = ((SEG, 1024), F32), ((2 * SEG, 1024), BF16)
    q, k, v, left, sq, p, cw, written, retain, added = local_kernel(
        write_kernel,
        [wide, narrow, narrow, double, wide, ((GROUPS, SHARED * SEG, SEG), BF16), wide, full,
         ((SEG, 128), F32), full],
        (lengths, segment, query_weight, key_weight, value_weight, out_weight, gain, vector, bias,
         memory_init),
        "write_forward",
    )
    scan = entering(retain, added, False)
    output, memory, mn, cr, dr, dq, dk, dv, dmk, dmv, r = local_kernel(
        read_kernel,
        [wide, full, wide, wide, wide, wide, narrow, narrow, narrow, narrow, full],
        (lengths, segment, cot, key_weight, value_weight, out_weight, gain, memory_init, scan, q,
         k, v),
        "read_both",
    )
    later = entering(retain, r, True)
    right, context, d_out, normed, pair, rest = local_kernel(
        back_kernel,
        [double, double, double, double, ((2 * SEG, 512), BF16), ((1024, 256), F32)],
        (later, memory, written, retain, vector, query_weight, out_weight, gain, memory_init, scan,
         r, p, sq, k, v, left, mn, cr, cw, dr, dq, dk, dv, dmk, dmv),
        "write_backward",
    )
    summed = sum_over_devices(
        left, right, context, d_out, normed, pair, rest, gain, query_weight, key_weight,
        value_weight,
    )
    grad_query, grad_out, grad_key, grad_value, grad_gain, grad_gate, grad_memory = local_kernel(
        finish_kernel,
        [((4, n), F32) for n in (1024, 1024, 256, 256)]
        + [((1, 4), F32), ((1, 4), F32), ((4, 128), F32)],
        (summed,),
        "finish",
    )
    grad_gain, grad_gate, grad_memory = grad_gain[0], grad_gate[0], grad_memory.T
    return (
        output[None, None],
        grad_query,
        grad_key,
        grad_value,
        grad_out,
        grad_gain,
        grad_gate,
        grad_memory,
    )


def solution(mesh):
    split = Mesh(mesh.devices.reshape(4, 4, 2, 2, 4), AXES)
    rows = P(("zh", "y"), ("zl", "x", "c"), None, None)
    return jax.shard_map(
        per_device,
        mesh=split,
        in_specs=(rows, P(("zh", "y"), ("zl", "x", "c"))) + (P(),) * 8 + (rows,),
        out_specs=(
            rows,
            P(AXES, None),
            P(AXES, None),
            P(AXES, None),
            P(AXES, None),
            P(AXES),
            P(AXES),
            P(None, AXES),
        ),
        check_vma=False,
    )
```

```python
import functools

import jax
import jax.numpy as jnp
from jax import lax
from jax.experimental import pallas as pl
from jax.experimental.pallas import tpu as pltpu
from jax.sharding import Mesh
from jax.sharding import PartitionSpec as P

HEAD = 64
F32, BF16 = jnp.float32, jnp.bfloat16
AXES = ("zl", "x", "c", "zh", "y")
MESH = pl.DeviceIdType.MESH
VMEM_SPEC = pl.BlockSpec(memory_space=pltpu.VMEM)


def z_shift(step):
    place = lax.rem(lax.axis_index("zh") * 4 + lax.axis_index("zl") + step, 8)
    return {"zh": lax.div(place, 4), "zl": lax.rem(place, 4)}


def shift(axis, step):
    if axis == "z":
        return z_shift(step % 8)
    return {axis: lax.rem(lax.axis_index(axis) + step % 4, 4)}


def place_of(axis):
    return lax.axis_index("zl" if axis == "z" else axis)


def remote(source, target, send, receive, device):
    return pltpu.make_async_remote_copy(
        src_ref=source,
        dst_ref=target,
        send_sem=send,
        recv_sem=receive,
        device_id=device,
        device_id_type=MESH,
    )


class Ring:
    def __init__(self, axis, work, landing, out, send, receive):
        self.work, self.landing, self.out = work, landing, out
        self.send, self.receive = send, receive
        self.me = place_of(axis)
        self.up, self.down = shift(axis, 1), shift(axis, -1)
        self.copies = []

    def at(self, step):
        return lax.rem(self.me + step, 4)

    def push(self, half, step, device):
        slot = len(self.copies)
        copy = remote(
            self.work.at[half, self.at(step)],
            self.landing.at[slot],
            self.send.at[slot],
            self.receive.at[slot],
            device,
        )
        copy.start()
        self.copies.append(copy)

    def first(self):
        self.push(0, 2, self.up)
        self.push(1, 2, self.down)
        self.push(1, 1, self.up)
        self.push(0, 3, self.down)

    def second(self):
        for half, step, device in ((0, 1, self.up), (1, 3, self.down)):
            self.copies[half].wait_recv()
            self.work[half, self.at(step)] += self.landing[half]
            self.push(half, step, device)

    def finish(self):
        for slot in range(2, 6):
            self.copies[slot].wait_recv()
        self.out[0] = self.work[0, self.me] + self.landing[3] + self.landing[4]
        self.out[1] = self.work[1, self.me] + self.landing[2] + self.landing[5]

    def drain(self):
        for copy in self.copies:
            copy.wait_send()


class Direct:
    def __init__(self, axis, work, landing, out, send, receive):
        self.work, self.landing, self.out = work, landing, out
        self.send, self.receive = send, receive
        self.me = place_of(axis)
        self.steps = ((2, shift(axis, 2)), (1, shift(axis, 1)), (3, shift(axis, -1)))
        self.copies = []

    def first(self):
        for slot, (step, device) in enumerate(self.steps):
            copy = remote(
                self.work.at[:, lax.rem(self.me + step, 4)],
                self.landing.at[slot],
                self.send.at[slot],
                self.receive.at[slot],
                device,
            )
            copy.start()
            self.copies.append(copy)

    def second(self):
        pass

    def finish(self):
        for copy in self.copies:
            copy.wait_recv()
        self.out[...] = (
            self.work[:, self.me] + self.landing[0] + self.landing[1] + self.landing[2]
        )

    def drain(self):
        for copy in self.copies:
            copy.wait_send()


ORDERS = (("x", "y", "z"), ("y", "z", "x"), ("z", "x", "y"))
PARTS = 6
WIDTHS = (512, 512, 512, 512, 512, 256)
TOTAL = 2816


def sum_kernel(*refs):
    (
        later_ref, memory_ref, written_ref, retain_ref, vector_ref, wq_ref, wo_ref, gain,
        start_ref, scan_ref, r_ref, p_ref, sq_ref, k_ref, v_ref, left, mn_ref,
        cr_ref, cw_ref, dr_ref, dq_ref, dk_ref, dv_ref, dmk_ref, dmv_ref, wk, wv,
    ) = refs[:27]
    out_ref, refs = refs[27], refs[28:]
    right, context, d_out, normed, pair, rest, *refs = refs
    products, refs = refs[:5], refs[5:]
    landed, refs = refs[:6], refs[6:]
    works, refs = refs[:6], refs[6:]
    rings_of, refs = refs[:36], refs[36:]
    rows_of, refs = refs[:2], refs[2:]
    sent, mate, fold_in, refs = refs[:2], refs[2:4], refs[4:6], refs[6:]
    core_send, core_receive, ring_send, ring_receive, fold_sems, row_sems = refs
    core = lax.axis_index("c")
    other = {"c": 1 - core}
    far = z_shift(4)
    place = lax.axis_index(AXES)
    base = pl.ds(pl.multiple_of(lax.div(place, 4) * 16, 16), 16)
    row_copies = [
        pltpu.make_async_copy(w.at[base], rows, row_sems.at[k])
        for k, (w, rows) in enumerate(zip((wk, wv), rows_of))
    ]
    for copy in row_copies:
        copy.start()
    peers = [other, far, shift("x", 2), shift("y", 2), shift("z", 2), shift("z", -2)]
    peers += [shift(axis, step) for axis in ("x", "y", "z") for step in (1, -1)]
    barrier = pltpu.get_barrier_semaphore()
    for device in peers:
        pl.semaphore_signal(barrier, inc=1, device_id=device, device_id_type=MESH)
    core_copies = []
    core_of = {}

    def push_core(part, source, target):
        n = len(core_copies)
        copy = remote(source, target, core_send.at[n], core_receive.at[n], other)
        copy.start()
        core_copies.append(copy)
        core_of.setdefault(part, []).append(copy)

    def product_and_push(part):
        factor, other_factor, start = (
            (left, right, 0),
            (context, d_out, 0),
            (normed, pair, 0),
            (left, right, 512),
            (context, d_out, 512),
        )[part]
        for block in range(4):
            value = mul_tn(
                factor[:, block * 256 : block * 256 + 256], other_factor[:, start : start + 512]
            )
            products[part][block * 4 : block * 4 + 4] = value.reshape(4, 2, 32, 512)
            if not core_copies and block == 0:
                pl.semaphore_wait(barrier, len(peers))
            if block % 2 == 1:
                blocks = pl.ds((block - 1) * 4, 8)
                push_core(part, products[part].at[blocks, 1 - core], landed[part].at[blocks])

    sources = tuple(products) + (rest,)

    def build_part(part):
        order, work = ORDERS[part % 3], works[part]
        half_width = WIDTHS[part] // 2

        def build(zl, carry):
            for x in range(4):
                block = zl * 4 + x
                for col in range(0, WIDTHS[part], 128):
                    cols = pl.ds(col, 128)
                    half = col // half_width
                    to = pl.ds(col % half_width, 128)
                    rows = sources[part][block, core, :, cols] + landed[part][block, :, cols]
                    low = lax.broadcasted_iota(jnp.int32, (8, 128), 0) < 4
                    for pair_at in range(2):
                        a = rows[pair_at * 8 : pair_at * 8 + 8]
                        b = rows[16 + pair_at * 8 : 24 + pair_at * 8]
                        tiles = (
                            jnp.where(low, a, pltpu.roll(b, 4, 0)),
                            jnp.where(low, pltpu.roll(a, 4, 0), b),
                        )
                        for bit in range(2):
                            where = {"z": zl, "x": x, "y": pair_at * 2 + bit}
                            index = (half,) + tuple(where[axis] for axis in order)
                            work[index + (slice(None), to)] = tiles[bit]
            return carry

        lax.fori_loop(0, 4, build, 0)

    rings = {}

    def begin(part):
        for copy in core_of[part]:
            copy.wait_recv()
        build_part(part)
        stages = []
        for stage in range(3):
            n = part * 3 + stage
            stages.append(
                (Direct if stage else Ring)(
                    ORDERS[part % 3][stage],
                    works[part] if stage == 0 else rings_of[2 * (n - 1) + 1],
                    rings_of[2 * n],
                    rings_of[2 * n + 1],
                    ring_send.at[n],
                    ring_receive.at[n],
                )
            )
        rings[part] = stages
        stages[0].first()

    early, late = (0, 1, 2), (3, 4, 5)

    def second(parts, stage):
        for part in parts:
            rings[part][stage].second()

    def finish(parts, stage):
        for part in parts:
            rings[part][stage].finish()
            if stage < 2:
                rings[part][stage + 1].first()

    high = lax.axis_index("zh")
    folds = []

    def fold(parts, which):
        total = jnp.concatenate(
            [rings_of[2 * (part * 3 + 2) + 1][half] for part in parts for half in range(2)],
            axis=1,
        )
        turned = pltpu.roll(total, 4, 0)
        middle = total.shape[1] // 2
        top = lax.broadcasted_iota(jnp.int32, (8, middle), 0) < 4
        straight = jnp.where(top, total[:, :middle], turned[:, middle:])
        crossed = jnp.where(top, turned[:, :middle], total[:, middle:])
        sent[which][...] = jnp.where(high == 1, straight, crossed)
        mate[which][...] = jnp.where(high == 0, straight, crossed)
        copy = remote(
            sent[which], fold_in[which], fold_sems.at[which, 0], fold_sems.at[which, 1], far
        )
        copy.start()
        folds.append(copy)

    later = later_ref[:, :1024]
    written = written_ref[...]
    retain = retain_ref[:, :1]
    d_retain = jnp.sum(later * (memory_ref[...] - written), axis=-1, keepdims=True)
    d_logit = d_retain * retain * (1.0 - retain)
    gate = jnp.sum(written * d_logit, axis=0, keepdims=True)
    d_written = ((1.0 - retain) * later + d_logit * vector_ref[...]).astype(BF16)
    context[:SEG] = cr_ref[...]
    context[SEG:] = cw_ref[...]
    d_out[:SEG] = dr_ref[...]
    d_out[SEG:] = d_written
    product_and_push(1)
    product_and_push(4)
    begin(1)
    begin(4)
    d_context = mul_nt(d_written, wo_ref[...]).astype(BF16)
    slots, keys, values = sq_ref[...], k_ref[...], v_ref[...]
    d_slots, d_keys, d_values = [], [], []
    for group in range(GROUPS):
        rounded = p_ref[group]
        dq, dk, dv = attend_back(
            rounded.astype(F32), rounded, stacked(slots, group), of_group(keys, group),
            of_group(values, group), stacked(d_context, group),
        )
        d_slots.append(side_by_side(dq))
        d_keys.append(dk.astype(BF16))
        d_values.append(dv.astype(BF16))

    def added(one, two):
        return (one.astype(F32) + two.astype(F32)).astype(BF16)

    scale = jnp.asarray(score_scale, BF16)
    d_slot = jnp.concatenate(d_slots, axis=1) * scale
    right[:SEG] = dq_ref[...] * scale
    right[SEG:] = d_slot
    product_and_push(0)
    product_and_push(3)
    second((1,), 0)
    begin(0)
    pair[:SEG, :256] = added(dk_ref[...], jnp.concatenate(d_keys, axis=1))
    pair[:SEG, 256:] = added(dv_ref[...], jnp.concatenate(d_values, axis=1))
    pair[SEG:, :256] = dmk_ref[...]
    pair[SEG:, 256:] = dmv_ref[...]
    normed[:SEG] = left[:SEG]
    normed[SEG:] = mn_ref[...]
    product_and_push(2)
    begin(3)
    begin(2)
    second((4, 0), 0)
    d_sn = mul_nt(d_slot, wq_ref[...]).astype(BF16).astype(F32)
    start = start_ref[...].astype(F32)
    total = normalize_back(start, gain[...], d_sn) + scan_ref[:, 1024:1025] * r_ref[...]
    gates = jnp.broadcast_to(gate, (128, 1024))
    for block in range(8):
        rows = slice(block * 128, block * 128 + 128)
        blocks = slice(block * 2, block * 2 + 2)
        rest[blocks, :, :, :128] = jnp.transpose(total[:, rows]).reshape(2, 2, 32, 128)
        rest[blocks, :, :, 128:] = jnp.transpose(gates[:, rows]).reshape(2, 2, 32, 128)
    push_core(5, rest.at[:, 1 - core], landed[5])
    second((2,), 0)
    begin(5)
    finish((1,), 0)
    second((3,), 0)
    finish((0, 2), 0)
    second((5,), 0)
    finish((4,), 0)
    finish((1, 0, 2), 1)
    finish((3, 5), 0)
    finish((1, 0, 2), 2)
    fold(early, 0)
    finish((4, 5, 3), 1)
    finish((4, 5, 3), 2)
    fold(late, 1)
    for copy in core_copies:
        copy.wait_send()
    for stages in rings.values():
        for ring in stages:
            ring.drain()
    for copy in row_copies:
        copy.wait()
    part_of_16 = lax.rem(place, 4)
    weights = []
    for loaded in (wq_ref[base], rows_of[0][...], rows_of[1][...]):
        loaded = loaded.astype(F32)
        tile = jnp.where(part_of_16 >= 2, loaded[8:], loaded[:8])
        weights.append(jnp.where(lax.rem(place, 2) == 1, pltpu.roll(tile, 4, 0), tile))
    spot = place * 4 + lax.broadcasted_iota(jnp.int32, (8, 1024), 0)
    here = lax.broadcasted_iota(jnp.int32, (8, 1024), 1) == spot
    low = lax.broadcasted_iota(jnp.int32, (8, 1), 0) < 4
    gains = jnp.sum(jnp.where(here, gain[...], 0.0), axis=1, keepdims=True)
    gains = jnp.where(low, gains, 1.0)
    pieces = []
    for which in range(2):
        folds[which].wait()
        short = mate[which][...] + fold_in[which][...]
        pieces += [short, pltpu.roll(short, 4, 0)]
    full = jnp.concatenate(pieces, axis=1)
    of_gain = (
        jnp.sum(weights[0][:, :512] * full[:, :512], axis=1, keepdims=True)
        + jnp.sum(weights[0][:, 512:] * full[:, 1536:2048], axis=1, keepdims=True)
        + jnp.sum(weights[1] * full[:, 1024:1280], axis=1, keepdims=True)
        + jnp.sum(weights[2] * full[:, 1280:1536], axis=1, keepdims=True)
    ) / gains
    out_ref[:, :TOTAL] = full
    out_ref[:, TOTAL:] = jnp.broadcast_to(of_gain, (8, 128))


def sum_over_devices(*operands):
    tall = pltpu.VMEM((2 * SEG, 1024), BF16)
    scratch = [tall] * 4 + [pltpu.VMEM((2 * SEG, 512), BF16), pltpu.VMEM((16, 2, 32, 256), F32)]
    scratch += [pltpu.VMEM((16, 2, 32, n), F32) for n in WIDTHS[:5]]
    scratch += [pltpu.VMEM((16, 32, n), F32) for n in WIDTHS]
    scratch += [pltpu.VMEM((2, 4, 4, 4, 8, n // 2), F32) for n in WIDTHS]
    for n in WIDTHS:
        for stage in range(3):
            tail = (4,) * (2 - stage) + (8, n // 2)
            lands = (3, 2) if stage else (6,)
            scratch += [pltpu.VMEM(lands + tail, F32), pltpu.VMEM((2,) + tail, F32)]
    scratch += [pltpu.VMEM((16, n), BF16) for n in (256, 256)]
    scratch += [pltpu.VMEM((8, n), F32) for n in (768, 640)] * 3
    scratch += [
        pltpu.SemaphoreType.DMA((11,)),
        pltpu.SemaphoreType.DMA((11,)),
        pltpu.SemaphoreType.DMA((18, 6)),
        pltpu.SemaphoreType.DMA((18, 6)),
        pltpu.SemaphoreType.DMA((2, 2)),
        pltpu.SemaphoreType.DMA((3,)),
    ]
    return pl.pallas_call(
        sum_kernel,
        out_shape=jax.ShapeDtypeStruct((8, TOTAL + 128), F32),
        in_specs=[VMEM_SPEC] * 25 + [pl.BlockSpec(memory_space=pl.ANY)] * 2,
        out_specs=VMEM_SPEC,
        scratch_shapes=scratch,
        compiler_params=pltpu.CompilerParams(
            collective_id=2, has_side_effects=True, vmem_limit_bytes=60 << 20
        ),
        name="sum_over_devices",
    )(*operands)


def finish_kernel(full, gq, go, gk, gv, gain, gate, memory):
    gq[:, :512] = full[:4, :512]
    gq[:, 512:] = full[:4, 1536:2048]
    go[:, :512] = full[:4, 512:1024]
    go[:, 512:] = full[:4, 2048:2560]
    gk[...] = full[:4, 1024:1280]
    gv[...] = full[:4, 1280:1536]
    memory[...] = full[:4, 2560:2688]
    for ref, start in ((gate, 2688), (gain, TOTAL)):
        rows = jnp.concatenate([full[:, start : start + 128], jnp.zeros((120, 128), F32)], axis=0)
        ref[...] = jnp.transpose(rows)[:1, :4]


WIDE = 1152


def joined(earlier, later):
    keep = later[:, 1024:]
    gain = jnp.concatenate([keep] * 9, axis=1)
    added = jnp.concatenate([later[:, :1024], jnp.zeros_like(keep)], axis=1)
    return gain * earlier + added


def identity_rows(rows):
    return jnp.concatenate(
        [jnp.zeros((rows, 1024), jnp.float32), jnp.ones((rows, 128), jnp.float32)], axis=1
    )


CHUNKS = 2
CORE_ROWS, X_ROWS = 32, 8


def scan_kernel(
    reverse, add_ref, keep_ref, out_ref, own, mate, pair, xs, zs, backs, down, up, far, send,
    receive,
):
    core, x, zl = lax.axis_index("c"), lax.axis_index("x"), lax.axis_index("zl")
    other = {"c": 1 - core}
    x_peers = [{"x": lax.rem(x + k, 4)} for k in (1, 2, 3)]
    z_peers = [{"zl": lax.rem(zl + k, 4)} for k in (1, 2, 3)]
    peers = [other] + x_peers + z_peers
    barrier = pltpu.get_barrier_semaphore()
    for device in peers:
        pl.semaphore_signal(barrier, inc=1, device_id=device, device_id_type=MESH)
    own[:, :1024] = add_ref[...]
    own[:, 1024:] = keep_ref[...]
    pl.semaphore_wait(barrier, len(peers))
    order = (3, 2, 1, 0) if reverse else (0, 1, 2, 3)
    leads = core == (1 if reverse else 0)
    all_copies = []

    def chunk_of(chunk):
        copies = []

        def push(source, target, device):
            n = len(copies)
            copy = remote(source, target, send.at[chunk, n], receive.at[chunk, n], device)
            copy.start()
            copies.append(copy)
            all_copies.append(copy)
            return copy

        def rows_of(start, count):
            return pl.ds(pl.multiple_of(start, count), count)

        mine = rows_of(chunk * 2 * CORE_ROWS + core * CORE_ROWS, CORE_ROWS)
        theirs = rows_of(chunk * 2 * CORE_ROWS + (1 - core) * CORE_ROWS, CORE_ROWS)
        at_x = [rows_of(lax.rem(x + k, 4) * X_ROWS, X_ROWS) for k in range(4)]
        started = push(own.at[theirs], mate.at[chunk], other)
        yield
        started.wait_recv()
        kept, got = own[mine], mate[chunk]
        earlier = jnp.where(leads, kept, got)
        pair[chunk] = joined(earlier, jnp.where(leads, got, kept))
        started = [
            push(pair.at[chunk, at_x[k]], xs.at[chunk, x], x_peers[k - 1]) for k in (2, 1, 3)
        ]
        xs[chunk, x] = pair[chunk, at_x[0]]
        yield
        for copy in started:
            copy.wait_recv()
        inside = {}
        running = None
        for k in order:
            inside[k] = running
            running = xs[chunk, k] if running is None else joined(running, xs[chunk, k])
        zs[chunk, zl] = running
        started = [
            push(zs.at[chunk, zl], zs.at[chunk, zl], z_peers[k - 1])
            for k in ((1, 2, 3) if reverse else (3, 2, 1))
        ]
        yield
        for copy in started:
            copy.wait_recv()
        before = identity_rows(X_ROWS)
        for k in order[:3]:
            passed = k > zl if reverse else k < zl
            before = jnp.where(passed, joined(before, zs[chunk, k]), before)
        for k in order:
            backs[chunk, k] = before if inside[k] is None else joined(before, inside[k])
        started = [
            push(backs.at[chunk, lax.rem(x + k, 4)], down.at[chunk, at_x[0]], x_peers[k - 1])
            for k in (2, 1, 3)
        ]
        down[chunk, at_x[0]] = backs[chunk, x]
        yield
        for copy in started:
            copy.wait_recv()
        lead = down[chunk]
        follow = joined(lead, earlier)
        up[chunk] = jnp.where(leads, follow, lead)
        started = push(up.at[chunk], far.at[chunk], other)
        out_ref[mine] = jnp.where(leads, lead, follow)
        yield
        started.wait_recv()
        out_ref[theirs] = far[chunk]

    running = [chunk_of(chunk) for chunk in range(CHUNKS)]
    for step in range(6):
        for steps in running:
            next(steps, None)
    for copy in all_copies:
        copy.wait_send()


def entering(keep, added, reverse):
    f32 = jnp.float32
    out = pl.pallas_call(
        functools.partial(scan_kernel, reverse),
        out_shape=jax.ShapeDtypeStruct((128, WIDE), f32),
        in_specs=[VMEM_SPEC] * 2,
        out_specs=VMEM_SPEC,
        scratch_shapes=[
            pltpu.VMEM((128, WIDE), f32),
            pltpu.VMEM((CHUNKS, CORE_ROWS, WIDE), f32),
            pltpu.VMEM((CHUNKS, CORE_ROWS, WIDE), f32),
            pltpu.VMEM((CHUNKS, 4, X_ROWS, WIDE), f32),
            pltpu.VMEM((CHUNKS, 4, X_ROWS, WIDE), f32),
            pltpu.VMEM((CHUNKS, 4, X_ROWS, WIDE), f32),
            pltpu.VMEM((CHUNKS, CORE_ROWS, WIDE), f32),
            pltpu.VMEM((CHUNKS, CORE_ROWS, WIDE), f32),
            pltpu.VMEM((CHUNKS, CORE_ROWS, WIDE), f32),
            pltpu.SemaphoreType.DMA((CHUNKS, 11)),
            pltpu.SemaphoreType.DMA((CHUNKS, 11)),
        ],
        compiler_params=pltpu.CompilerParams(
            collective_id=1 if reverse else 0, has_side_effects=True
        ),
        name="suffix" if reverse else "prefix",
    )(added, keep)
    return out


epsilon = 1e-05
score_scale = 0.125
GROUPS, SHARED, SEG = 4, 4, 128


def mul(a, b):
    return lax.dot_general(a, b, (((1,), (0,)), ((), ())), preferred_element_type=F32)


def mul_nt(a, b):
    return lax.dot_general(a, b, (((1,), (1,)), ((), ())), preferred_element_type=F32)


def mul_tn(a, b):
    return lax.dot_general(a, b, (((0,), (0,)), ((), ())), preferred_element_type=F32)


def inverse_of(rows):
    return lax.rsqrt(jnp.mean(rows * rows, axis=-1, keepdims=True) + epsilon)


def normalize(rows, gain):
    return (rows * inverse_of(rows) * gain).astype(BF16)


def normalize_back(rows, gain, d_normed):
    inverse = inverse_of(rows)
    scaled = d_normed * gain
    shared = jnp.mean(scaled * rows, axis=-1, keepdims=True)
    return inverse * scaled - rows * (inverse * inverse * inverse * shared)


def stacked(rows, group):
    start = group * SHARED * HEAD
    return jnp.concatenate(
        [rows[:, start + k * HEAD : start + (k + 1) * HEAD] for k in range(SHARED)], axis=0
    )


def side_by_side(rows):
    return jnp.concatenate([rows[k * SEG : (k + 1) * SEG] for k in range(SHARED)], axis=1)


def of_group(rows, group):
    return rows[:, group * HEAD : (group + 1) * HEAD]


def weights_of(queries, keys, allowed):
    scores = jnp.where(allowed, mul_nt(queries, keys), -1e30)
    raised = jnp.exp(scores - jnp.max(scores, axis=-1, keepdims=True))
    return raised / jnp.sum(raised, axis=-1, keepdims=True)


def attend_back(weights, rounded, queries, keys, values, d_context):
    d_values = mul_tn(rounded, d_context)
    d_weights = mul_nt(d_context, values).astype(BF16).astype(F32)
    pulled = jnp.sum(d_weights * weights, axis=-1, keepdims=True)
    d_scores = (weights * (d_weights - pulled)).astype(BF16)
    return mul(d_scores, keys).astype(BF16), mul_tn(d_scores, queries), d_values


def write_kernel(
    length_ref, x_ref, wq_ref, wk_ref, wv_ref, wo_ref, gain_ref, vector_ref, bias_ref, start_ref,
    q_ref, k_ref, v_ref, left_ref, sq_ref, p_ref, context_ref, written_ref, retain_ref,
    added_ref,
):
    length = length_ref[0, 0]
    gain = gain_ref[...]
    xn = normalize(x_ref[...].astype(F32), gain)
    sn = normalize(start_ref[...].astype(F32), gain)
    left = jnp.concatenate([xn, sn], axis=0)
    left_ref[...] = left
    both = (mul(left, wq_ref[...]) * score_scale).astype(BF16)
    q_ref[...] = both[:SEG]
    sq = both[SEG:]
    sq_ref[...] = sq
    keys = mul(xn, wk_ref[...]).astype(BF16)
    values = mul(xn, wv_ref[...]).astype(BF16)
    k_ref[...] = keys
    v_ref[...] = values
    allowed = lax.broadcasted_iota(jnp.int32, (SHARED * SEG, SEG), 1) < length
    contexts = []
    for group in range(GROUPS):
        weights = weights_of(stacked(sq, group), of_group(keys, group), allowed).astype(BF16)
        p_ref[group] = weights
        contexts.append(side_by_side(mul(weights, of_group(values, group)).astype(BF16)))
    context = jnp.concatenate(contexts, axis=1)
    context_ref[...] = context
    written = mul(context, wo_ref[...])
    written_ref[...] = written
    bias = jnp.transpose(jnp.broadcast_to(bias_ref[...], (128, 128)))[:, :1]
    logits = jnp.sum(written * vector_ref[...], axis=-1, keepdims=True) + bias
    retain = jax.nn.sigmoid(logits)
    retain_ref[...] = jnp.broadcast_to(retain, (SEG, 128))
    added_ref[...] = (1.0 - retain) * written


def read_kernel(
    length_ref, x_ref, cot_ref, wk_ref, wv_ref, wo_ref, gain_ref, start_ref, scan_ref,
    q_ref, k_ref, v_ref,
    out_ref, memory_ref, mn_ref, context_ref, dr_ref, dq_ref, dk_ref, dv_ref, dmk_ref, dmv_ref,
    r_ref,
):
    length = length_ref[0, 0]
    gain = gain_ref[...]
    memory = scan_ref[:, 1024:1025] * start_ref[...].astype(F32) + scan_ref[:, :1024]
    memory_ref[...] = memory
    mn = normalize(memory, gain)
    mn_ref[...] = mn
    keys = jnp.concatenate([mul(mn, wk_ref[...]).astype(BF16), k_ref[...]], axis=0)
    values = jnp.concatenate([mul(mn, wv_ref[...]).astype(BF16), v_ref[...]], axis=0)
    valid = lax.broadcasted_iota(jnp.int32, (SEG, 1024), 0) < length
    d_result = jnp.where(valid, cot_ref[...].astype(F32), 0.0).astype(BF16)
    dr_ref[...] = d_result
    d_context = mul_nt(d_result, wo_ref[...]).astype(BF16)
    shape = (SHARED * SEG, 2 * SEG)
    place = lax.broadcasted_iota(jnp.int32, shape, 1) - SEG
    row = lax.rem(lax.broadcasted_iota(jnp.int32, shape, 0), SEG)
    allowed = (place < 0) | ((place <= row) & (place < length))
    queries = q_ref[...]
    contexts, d_queries, d_keys, d_values = [], [], [], []
    for group in range(GROUPS):
        q, k, v = stacked(queries, group), of_group(keys, group), of_group(values, group)
        weights = weights_of(q, k, allowed)
        rounded = weights.astype(BF16)
        contexts.append(side_by_side(mul(rounded, v).astype(BF16)))
        dq, dk, dv = attend_back(weights, rounded, q, k, v, stacked(d_context, group))
        d_queries.append(side_by_side(dq))
        d_keys.append(dk.astype(BF16))
        d_values.append(dv.astype(BF16))
    context = jnp.concatenate(contexts, axis=1)
    context_ref[...] = context
    out_ref[...] = (x_ref[...].astype(F32) + mul(context, wo_ref[...])).astype(BF16)
    dq_ref[...] = jnp.concatenate(d_queries, axis=1)
    d_key = jnp.concatenate(d_keys, axis=1)
    d_value = jnp.concatenate(d_values, axis=1)
    dmk_ref[...] = d_key[:SEG]
    dmv_ref[...] = d_value[:SEG]
    dk_ref[...] = d_key[SEG:]
    dv_ref[...] = d_value[SEG:]
    d_mn = mul_nt(d_key[:SEG], wk_ref[...]) + mul_nt(d_value[:SEG], wv_ref[...])
    r_ref[...] = normalize_back(memory, gain, d_mn.astype(BF16).astype(F32))


def local_kernel(kernel, shapes, operands, name):
    smem = pl.BlockSpec(memory_space=pltpu.SMEM)
    return pl.pallas_call(
        kernel,
        out_shape=[jax.ShapeDtypeStruct(shape, dtype) for shape, dtype in shapes],
        in_specs=[smem if a.dtype == jnp.int32 else VMEM_SPEC for a in operands],
        out_specs=[VMEM_SPEC] * len(shapes),
        compiler_params=pltpu.CompilerParams(vmem_limit_bytes=60 << 20),
        name=name,
    )(*operands)


def per_device(
    segments,
    lengths,
    query_weight,
    key_weight,
    value_weight,
    out_weight,
    norm_gain,
    gate_vector,
    gate_bias,
    memory_init,
    cotangent,
):
    segment, cot = segments[0, 0], cotangent[0, 0]
    gain, vector, bias = norm_gain[None], gate_vector[None], gate_bias[None]
    wide, narrow = ((SEG, 1024), BF16), ((SEG, 256), BF16)
    full, double = ((SEG, 1024), F32), ((2 * SEG, 1024), BF16)
    q, k, v, left, sq, p, cw, written, retain, added = local_kernel(
        write_kernel,
        [wide, narrow, narrow, double, wide, ((GROUPS, SHARED * SEG, SEG), BF16), wide, full,
         ((SEG, 128), F32), full],
        (lengths, segment, query_weight, key_weight, value_weight, out_weight, gain, vector, bias,
         memory_init),
        "write_forward",
    )
    scan = entering(retain, added, False)
    output, memory, mn, cr, dr, dq, dk, dv, dmk, dmv, r = local_kernel(
        read_kernel,
        [wide, full, wide, wide, wide, wide, narrow, narrow, narrow, narrow, full],
        (lengths, segment, cot, key_weight, value_weight, out_weight, gain, memory_init, scan, q,
         k, v),
        "read_both",
    )
    later = entering(retain, r, True)
    summed = sum_over_devices(
        later, memory, written, retain, vector, query_weight, out_weight, gain, memory_init, scan,
        r, p, sq, k, v, left, mn, cr, cw, dr, dq, dk, dv, dmk, dmv, key_weight, value_weight,
    )
    grad_query, grad_out, grad_key, grad_value, grad_gain, grad_gate, grad_memory = local_kernel(
        finish_kernel,
        [((4, n), F32) for n in (1024, 1024, 256, 256)]
        + [((1, 4), F32), ((1, 4), F32), ((4, 128), F32)],
        (summed,),
        "finish",
    )
    grad_gain, grad_gate, grad_memory = grad_gain[0], grad_gate[0], grad_memory.T
    return (
        output[None, None],
        grad_query,
        grad_key,
        grad_value,
        grad_out,
        grad_gain,
        grad_gate,
        grad_memory,
    )


def solution(mesh):
    split = Mesh(mesh.devices.reshape(4, 4, 2, 2, 4), AXES)
    rows = P(("zh", "y"), ("zl", "x", "c"), None, None)
    return jax.shard_map(
        per_device,
        mesh=split,
        in_specs=(rows, P(("zh", "y"), ("zl", "x", "c"))) + (P(),) * 8 + (rows,),
        out_specs=(
            rows,
            P(AXES, None),
            P(AXES, None),
            P(AXES, None),
            P(AXES, None),
            P(AXES),
            P(AXES),
            P(None, AXES),
        ),
        check_vma=False,
    )
```

```python
import functools

import jax
import jax.numpy as jnp
from jax import lax
from jax.experimental import pallas as pl
from jax.experimental.pallas import tpu as pltpu
from jax.sharding import Mesh
from jax.sharding import PartitionSpec as P

HEAD = 64
F32, BF16 = jnp.float32, jnp.bfloat16
AXES = ("zl", "x", "c", "zh", "y")
MESH = pl.DeviceIdType.MESH
VMEM_SPEC = pl.BlockSpec(memory_space=pltpu.VMEM)


def z_shift(step):
    place = lax.rem(lax.axis_index("zh") * 4 + lax.axis_index("zl") + step, 8)
    return {"zh": lax.div(place, 4), "zl": lax.rem(place, 4)}


def shift(axis, step):
    if axis == "z":
        return z_shift(step % 8)
    return {axis: lax.rem(lax.axis_index(axis) + step % 4, 4)}


def place_of(axis):
    return lax.axis_index("zl" if axis == "z" else axis)


def remote(source, target, send, receive, device):
    return pltpu.make_async_remote_copy(
        src_ref=source,
        dst_ref=target,
        send_sem=send,
        recv_sem=receive,
        device_id=device,
        device_id_type=MESH,
    )


class Ring:
    def __init__(self, axis, work, landing, out, send, receive):
        self.work, self.landing, self.out = work, landing, out
        self.send, self.receive = send, receive
        self.me = place_of(axis)
        self.up, self.down = shift(axis, 1), shift(axis, -1)
        self.copies = []

    def at(self, step):
        return lax.rem(self.me + step, 4)

    def push(self, half, step, device):
        slot = len(self.copies)
        copy = remote(
            self.work.at[half, self.at(step)],
            self.landing.at[slot],
            self.send.at[slot],
            self.receive.at[slot],
            device,
        )
        copy.start()
        self.copies.append(copy)

    def first(self):
        self.push(0, 2, self.up)
        self.push(1, 2, self.down)
        self.push(1, 1, self.up)
        self.push(0, 3, self.down)

    def second(self):
        for half, step, device in ((0, 1, self.up), (1, 3, self.down)):
            self.copies[half].wait_recv()
            self.work[half, self.at(step)] += self.landing[half]
            self.push(half, step, device)

    def finish(self):
        for slot in range(2, 6):
            self.copies[slot].wait_recv()
        self.out[0] = self.work[0, self.me] + self.landing[3] + self.landing[4]
        self.out[1] = self.work[1, self.me] + self.landing[2] + self.landing[5]

    def drain(self):
        for copy in self.copies:
            copy.wait_send()


class Direct:
    def __init__(self, axis, work, landing, out, send, receive):
        self.work, self.landing, self.out = work, landing, out
        self.send, self.receive = send, receive
        self.me = place_of(axis)
        self.steps = ((2, shift(axis, 2)), (1, shift(axis, 1)), (3, shift(axis, -1)))
        self.copies = []

    def first(self):
        for slot, (step, device) in enumerate(self.steps):
            copy = remote(
                self.work.at[:, lax.rem(self.me + step, 4)],
                self.landing.at[slot],
                self.send.at[slot],
                self.receive.at[slot],
                device,
            )
            copy.start()
            self.copies.append(copy)

    def second(self):
        pass

    def finish(self):
        for copy in self.copies:
            copy.wait_recv()
        self.out[...] = (
            self.work[:, self.me] + self.landing[0] + self.landing[1] + self.landing[2]
        )

    def drain(self):
        for copy in self.copies:
            copy.wait_send()


ORDERS = (
    ("y", "z", "x"), ("y", "z", "x"), ("z", "x", "y"),
    ("x", "y", "z"), ("x", "y", "z"), ("z", "x", "y"),
)
WIDTHS = (512, 512, 512, 512, 512, 256)
TOTAL = 2816


def sum_kernel(*refs):
    (
        later_ref, memory_ref, written_ref, retain_ref, vector_ref, wq_ref, wo_ref, gain,
        start_ref, scan_ref, r_ref, p_ref, sq_ref, k_ref, v_ref, left, mn_ref,
        cr_ref, cw_ref, dr_ref, dq_ref, dk_ref, dv_ref, dmk_ref, dmv_ref, wk, wv,
    ) = refs[:27]
    out_ref, refs = refs[27], refs[28:]
    right, context, d_out, normed, pair, rest, *refs = refs
    products, refs = refs[:5], refs[5:]
    landed, refs = refs[:6], refs[6:]
    works, refs = refs[:6], refs[6:]
    rings_of, refs = refs[:36], refs[36:]
    rows_of, refs = refs[:2], refs[2:]
    sent, mate, fold_in, refs = refs[:2], refs[2:4], refs[4:6], refs[6:]
    core_send, core_receive, ring_send, ring_receive, fold_sems, row_sems = refs
    core = lax.axis_index("c")
    other = {"c": 1 - core}
    far = z_shift(4)
    place = lax.axis_index(AXES)
    base = pl.ds(pl.multiple_of(lax.div(place, 4) * 16, 16), 16)
    row_copies = [
        pltpu.make_async_copy(w.at[base], rows, row_sems.at[k])
        for k, (w, rows) in enumerate(zip((wk, wv), rows_of))
    ]
    for copy in row_copies:
        copy.start()
    peers = [other, far, shift("x", 2), shift("y", 2), shift("z", 2), shift("z", -2)]
    peers += [shift(axis, step) for axis in ("x", "y", "z") for step in (1, -1)]
    barrier = pltpu.get_barrier_semaphore()
    for device in peers:
        pl.semaphore_signal(barrier, inc=1, device_id=device, device_id_type=MESH)
    core_copies = []
    core_of = {}

    def push_core(part, source, target):
        n = len(core_copies)
        copy = remote(source, target, core_send.at[n], core_receive.at[n], other)
        copy.start()
        core_copies.append(copy)
        core_of.setdefault(part, []).append(copy)

    def product_and_push(part):
        factor, other_factor, start = (
            (left, right, 0),
            (context, d_out, 0),
            (normed, pair, 0),
            (left, right, 512),
            (context, d_out, 512),
        )[part]
        for block in range(4):
            value = mul_tn(
                factor[:, block * 256 : block * 256 + 256], other_factor[:, start : start + 512]
            )
            products[part][block * 4 : block * 4 + 4] = value.reshape(4, 2, 32, 512)
            if not core_copies and block == 0:
                pl.semaphore_wait(barrier, len(peers))
            if block % 2 == 1:
                blocks = pl.ds((block - 1) * 4, 8)
                push_core(part, products[part].at[blocks, 1 - core], landed[part].at[blocks])

    sources = tuple(products) + (rest,)

    def build_part(part):
        order, work = ORDERS[part], works[part]
        half_width = WIDTHS[part] // 2

        def build(zl, carry):
            for x in range(4):
                block = zl * 4 + x
                for col in range(0, WIDTHS[part], 128):
                    cols = pl.ds(col, 128)
                    half = col // half_width
                    to = pl.ds(col % half_width, 128)
                    rows = sources[part][block, core, :, cols] + landed[part][block, :, cols]
                    low = lax.broadcasted_iota(jnp.int32, (8, 128), 0) < 4
                    for pair_at in range(2):
                        a = rows[pair_at * 8 : pair_at * 8 + 8]
                        b = rows[16 + pair_at * 8 : 24 + pair_at * 8]
                        tiles = (
                            jnp.where(low, a, pltpu.roll(b, 4, 0)),
                            jnp.where(low, pltpu.roll(a, 4, 0), b),
                        )
                        for bit in range(2):
                            where = {"z": zl, "x": x, "y": pair_at * 2 + bit}
                            index = (half,) + tuple(where[axis] for axis in order)
                            work[index + (slice(None), to)] = tiles[bit]
            return carry

        lax.fori_loop(0, 4, build, 0)

    rings = {}

    def begin(part):
        for copy in core_of[part]:
            copy.wait_recv()
        build_part(part)
        stages = []
        for stage in range(3):
            n = part * 3 + stage
            stages.append(
                (Direct if stage else Ring)(
                    ORDERS[part][stage],
                    works[part] if stage == 0 else rings_of[2 * (n - 1) + 1],
                    rings_of[2 * n],
                    rings_of[2 * n + 1],
                    ring_send.at[n],
                    ring_receive.at[n],
                )
            )
        rings[part] = stages
        stages[0].first()

    early, late = (1, 4, 2), (0, 3, 5)

    def second(parts, stage):
        for part in parts:
            rings[part][stage].second()

    def finish(parts, stage):
        for part in parts:
            rings[part][stage].finish()
            if stage < 2:
                rings[part][stage + 1].first()

    high = lax.axis_index("zh")
    folds = []

    def fold(parts, which):
        total = jnp.concatenate(
            [rings_of[2 * (part * 3 + 2) + 1][half] for part in parts for half in range(2)],
            axis=1,
        )
        turned = pltpu.roll(total, 4, 0)
        middle = total.shape[1] // 2
        top = lax.broadcasted_iota(jnp.int32, (8, middle), 0) < 4
        straight = jnp.where(top, total[:, :middle], turned[:, middle:])
        crossed = jnp.where(top, turned[:, :middle], total[:, middle:])
        sent[which][...] = jnp.where(high == 1, straight, crossed)
        mate[which][...] = jnp.where(high == 0, straight, crossed)
        copy = remote(
            sent[which], fold_in[which], fold_sems.at[which, 0], fold_sems.at[which, 1], far
        )
        copy.start()
        folds.append(copy)

    later = later_ref[:, :1024]
    written = written_ref[...]
    retain = retain_ref[:, :1]
    d_retain = jnp.sum(later * (memory_ref[...] - written), axis=-1, keepdims=True)
    d_logit = d_retain * retain * (1.0 - retain)
    gate = jnp.sum(written * d_logit, axis=0, keepdims=True)
    d_written = ((1.0 - retain) * later + d_logit * vector_ref[...]).astype(BF16)
    context[:SEG] = cr_ref[...]
    context[SEG:] = cw_ref[...]
    d_out[:SEG] = dr_ref[...]
    d_out[SEG:] = d_written
    product_and_push(1)
    product_and_push(4)
    begin(1)
    begin(4)
    d_context = mul_nt(d_written, wo_ref[...]).astype(BF16)
    slots, keys, values = sq_ref[...], k_ref[...], v_ref[...]
    d_slots, d_keys, d_values = [], [], []
    for group in range(GROUPS):
        rounded = p_ref[group]
        dq, dk, dv = attend_back(
            rounded.astype(F32), rounded, stacked(slots, group), of_group(keys, group),
            of_group(values, group), stacked(d_context, group),
        )
        d_slots.append(side_by_side(dq))
        d_keys.append(dk.astype(BF16))
        d_values.append(dv.astype(BF16))

    def added(one, two):
        return (one.astype(F32) + two.astype(F32)).astype(BF16)

    scale = jnp.asarray(score_scale, BF16)
    d_slot = jnp.concatenate(d_slots, axis=1) * scale
    pair[:SEG, :256] = added(dk_ref[...], jnp.concatenate(d_keys, axis=1))
    pair[:SEG, 256:] = added(dv_ref[...], jnp.concatenate(d_values, axis=1))
    pair[SEG:, :256] = dmk_ref[...]
    pair[SEG:, 256:] = dmv_ref[...]
    normed[:SEG] = left[:SEG]
    normed[SEG:] = mn_ref[...]
    product_and_push(2)
    right[:SEG] = dq_ref[...] * scale
    right[SEG:] = d_slot
    product_and_push(0)
    begin(2)
    second((1, 4), 0)
    product_and_push(3)
    begin(0)
    begin(3)
    d_sn = mul_nt(d_slot, wq_ref[...]).astype(BF16).astype(F32)
    start = start_ref[...].astype(F32)
    total = normalize_back(start, gain[...], d_sn) + scan_ref[:, 1024:1025] * r_ref[...]
    gates = jnp.broadcast_to(gate, (128, 1024))
    for block in range(8):
        rows = slice(block * 128, block * 128 + 128)
        blocks = slice(block * 2, block * 2 + 2)
        rest[blocks, :, :, :128] = jnp.transpose(total[:, rows]).reshape(2, 2, 32, 128)
        rest[blocks, :, :, 128:] = jnp.transpose(gates[:, rows]).reshape(2, 2, 32, 128)
    push_core(5, rest.at[:, 1 - core], landed[5])
    second((2,), 0)
    begin(5)
    finish((1, 4), 0)
    second((0, 3), 0)
    finish((2,), 0)
    second((5,), 0)
    finish((1, 4), 1)
    finish((0, 3), 0)
    finish((2,), 1)
    finish((5,), 0)
    finish(early, 2)
    fold(early, 0)
    finish(late, 1)
    finish(late, 2)
    fold(late, 1)
    for copy in core_copies:
        copy.wait_send()
    for stages in rings.values():
        for ring in stages:
            ring.drain()
    for copy in row_copies:
        copy.wait()
    part_of_16 = lax.rem(place, 4)
    weights = []
    for loaded in (wq_ref[base], rows_of[0][...], rows_of[1][...]):
        loaded = loaded.astype(F32)
        tile = jnp.where(part_of_16 >= 2, loaded[8:], loaded[:8])
        weights.append(jnp.where(lax.rem(place, 2) == 1, pltpu.roll(tile, 4, 0), tile))
    spot = place * 4 + lax.broadcasted_iota(jnp.int32, (8, 1024), 0)
    here = lax.broadcasted_iota(jnp.int32, (8, 1024), 1) == spot
    low = lax.broadcasted_iota(jnp.int32, (8, 1), 0) < 4
    gains = jnp.sum(jnp.where(here, gain[...], 0.0), axis=1, keepdims=True)
    gains = jnp.where(low, gains, 1.0)
    pieces = []
    for which in range(2):
        folds[which].wait()
        short = mate[which][...] + fold_in[which][...]
        pieces += [short, pltpu.roll(short, 4, 0)]
    full = jnp.concatenate(pieces, axis=1)
    of_gain = (
        jnp.sum(weights[0] * full[:, 1536:2560], axis=1, keepdims=True)
        + jnp.sum(weights[1] * full[:, 1024:1280], axis=1, keepdims=True)
        + jnp.sum(weights[2] * full[:, 1280:1536], axis=1, keepdims=True)
    ) / gains
    out_ref[:, :TOTAL] = full
    out_ref[:, TOTAL:] = jnp.broadcast_to(of_gain, (8, 128))


def sum_over_devices(*operands):
    tall = pltpu.VMEM((2 * SEG, 1024), BF16)
    scratch = [tall] * 4 + [pltpu.VMEM((2 * SEG, 512), BF16), pltpu.VMEM((16, 2, 32, 256), F32)]
    scratch += [pltpu.VMEM((16, 2, 32, n), F32) for n in WIDTHS[:5]]
    scratch += [pltpu.VMEM((16, 32, n), F32) for n in WIDTHS]
    scratch += [pltpu.VMEM((2, 4, 4, 4, 8, n // 2), F32) for n in WIDTHS]
    for n in WIDTHS:
        for stage in range(3):
            tail = (4,) * (2 - stage) + (8, n // 2)
            lands = (3, 2) if stage else (6,)
            scratch += [pltpu.VMEM(lands + tail, F32), pltpu.VMEM((2,) + tail, F32)]
    scratch += [pltpu.VMEM((16, n), BF16) for n in (256, 256)]
    scratch += [pltpu.VMEM((8, n), F32) for n in (768, 640)] * 3
    scratch += [
        pltpu.SemaphoreType.DMA((11,)),
        pltpu.SemaphoreType.DMA((11,)),
        pltpu.SemaphoreType.DMA((18, 6)),
        pltpu.SemaphoreType.DMA((18, 6)),
        pltpu.SemaphoreType.DMA((2, 2)),
        pltpu.SemaphoreType.DMA((3,)),
    ]
    return pl.pallas_call(
        sum_kernel,
        out_shape=jax.ShapeDtypeStruct((8, TOTAL + 128), F32),
        in_specs=[VMEM_SPEC] * 25 + [pl.BlockSpec(memory_space=pl.ANY)] * 2,
        out_specs=VMEM_SPEC,
        scratch_shapes=scratch,
        compiler_params=pltpu.CompilerParams(
            collective_id=2, has_side_effects=True, vmem_limit_bytes=60 << 20
        ),
        name="sum_over_devices",
    )(*operands)


def finish_kernel(full, gq, go, gk, gv, gain, gate, memory):
    gq[...] = full[:4, 1536:2560]
    go[...] = full[:4, :1024]
    gk[...] = full[:4, 1024:1280]
    gv[...] = full[:4, 1280:1536]
    memory[...] = full[:4, 2560:2688]
    for ref, start in ((gate, 2688), (gain, TOTAL)):
        rows = jnp.concatenate([full[:, start : start + 128], jnp.zeros((120, 128), F32)], axis=0)
        ref[...] = jnp.transpose(rows)[:1, :4]


WIDE = 1152


def joined(earlier, later):
    keep = later[:, 1024:]
    gain = jnp.concatenate([keep] * 9, axis=1)
    added = jnp.concatenate([later[:, :1024], jnp.zeros_like(keep)], axis=1)
    return gain * earlier + added


def identity_rows(rows):
    return jnp.concatenate(
        [jnp.zeros((rows, 1024), jnp.float32), jnp.ones((rows, 128), jnp.float32)], axis=1
    )


CHUNKS = 2
CORE_ROWS, X_ROWS = 32, 8


def scan_kernel(
    reverse, add_ref, keep_ref, out_ref, own, mate, pair, xs, zs, backs, down, up, far, send,
    receive,
):
    core, x, zl = lax.axis_index("c"), lax.axis_index("x"), lax.axis_index("zl")
    other = {"c": 1 - core}
    x_peers = [{"x": lax.rem(x + k, 4)} for k in (1, 2, 3)]
    z_peers = [{"zl": lax.rem(zl + k, 4)} for k in (1, 2, 3)]
    peers = [other] + x_peers + z_peers
    barrier = pltpu.get_barrier_semaphore()
    for device in peers:
        pl.semaphore_signal(barrier, inc=1, device_id=device, device_id_type=MESH)
    own[:, :1024] = add_ref[...]
    own[:, 1024:] = keep_ref[...]
    pl.semaphore_wait(barrier, len(peers))
    order = (3, 2, 1, 0) if reverse else (0, 1, 2, 3)
    leads = core == (1 if reverse else 0)
    all_copies = []

    def chunk_of(chunk):
        copies = []

        def push(source, target, device):
            n = len(copies)
            copy = remote(source, target, send.at[chunk, n], receive.at[chunk, n], device)
            copy.start()
            copies.append(copy)
            all_copies.append(copy)
            return copy

        def rows_of(start, count):
            return pl.ds(pl.multiple_of(start, count), count)

        mine = rows_of(chunk * 2 * CORE_ROWS + core * CORE_ROWS, CORE_ROWS)
        theirs = rows_of(chunk * 2 * CORE_ROWS + (1 - core) * CORE_ROWS, CORE_ROWS)
        at_x = [rows_of(lax.rem(x + k, 4) * X_ROWS, X_ROWS) for k in range(4)]
        started = push(own.at[theirs], mate.at[chunk], other)
        yield
        started.wait_recv()
        kept, got = own[mine], mate[chunk]
        earlier = jnp.where(leads, kept, got)
        pair[chunk] = joined(earlier, jnp.where(leads, got, kept))
        started = [
            push(pair.at[chunk, at_x[k]], xs.at[chunk, x], x_peers[k - 1]) for k in (2, 1, 3)
        ]
        xs[chunk, x] = pair[chunk, at_x[0]]
        yield
        for copy in started:
            copy.wait_recv()
        inside = {}
        running = None
        for k in order:
            inside[k] = running
            running = xs[chunk, k] if running is None else joined(running, xs[chunk, k])
        zs[chunk, zl] = running
        started = [
            push(zs.at[chunk, zl], zs.at[chunk, zl], z_peers[k - 1])
            for k in ((1, 2, 3) if reverse else (3, 2, 1))
        ]
        yield
        for copy in started:
            copy.wait_recv()
        before = identity_rows(X_ROWS)
        for k in order[:3]:
            passed = k > zl if reverse else k < zl
            before = jnp.where(passed, joined(before, zs[chunk, k]), before)
        for k in order:
            backs[chunk, k] = before if inside[k] is None else joined(before, inside[k])
        started = [
            push(backs.at[chunk, lax.rem(x + k, 4)], down.at[chunk, at_x[0]], x_peers[k - 1])
            for k in (2, 1, 3)
        ]
        down[chunk, at_x[0]] = backs[chunk, x]
        yield
        for copy in started:
            copy.wait_recv()
        lead = down[chunk]
        follow = joined(lead, earlier)
        up[chunk] = jnp.where(leads, follow, lead)
        started = push(up.at[chunk], far.at[chunk], other)
        out_ref[mine] = jnp.where(leads, lead, follow)
        yield
        started.wait_recv()
        out_ref[theirs] = far[chunk]

    running = [chunk_of(chunk) for chunk in range(CHUNKS)]
    for step in range(6):
        for steps in running:
            next(steps, None)
    for copy in all_copies:
        copy.wait_send()


def entering(keep, added, reverse):
    f32 = jnp.float32
    out = pl.pallas_call(
        functools.partial(scan_kernel, reverse),
        out_shape=jax.ShapeDtypeStruct((128, WIDE), f32),
        in_specs=[VMEM_SPEC] * 2,
        out_specs=VMEM_SPEC,
        scratch_shapes=[
            pltpu.VMEM((128, WIDE), f32),
            pltpu.VMEM((CHUNKS, CORE_ROWS, WIDE), f32),
            pltpu.VMEM((CHUNKS, CORE_ROWS, WIDE), f32),
            pltpu.VMEM((CHUNKS, 4, X_ROWS, WIDE), f32),
            pltpu.VMEM((CHUNKS, 4, X_ROWS, WIDE), f32),
            pltpu.VMEM((CHUNKS, 4, X_ROWS, WIDE), f32),
            pltpu.VMEM((CHUNKS, CORE_ROWS, WIDE), f32),
            pltpu.VMEM((CHUNKS, CORE_ROWS, WIDE), f32),
            pltpu.VMEM((CHUNKS, CORE_ROWS, WIDE), f32),
            pltpu.SemaphoreType.DMA((CHUNKS, 11)),
            pltpu.SemaphoreType.DMA((CHUNKS, 11)),
        ],
        compiler_params=pltpu.CompilerParams(
            collective_id=1 if reverse else 0, has_side_effects=True
        ),
        name="suffix" if reverse else "prefix",
    )(added, keep)
    return out


epsilon = 1e-05
score_scale = 0.125
GROUPS, SHARED, SEG = 4, 4, 128


def mul(a, b):
    return lax.dot_general(a, b, (((1,), (0,)), ((), ())), preferred_element_type=F32)


def mul_nt(a, b):
    return lax.dot_general(a, b, (((1,), (1,)), ((), ())), preferred_element_type=F32)


def mul_tn(a, b):
    return lax.dot_general(a, b, (((0,), (0,)), ((), ())), preferred_element_type=F32)


def inverse_of(rows):
    return lax.rsqrt(jnp.mean(rows * rows, axis=-1, keepdims=True) + epsilon)


def normalize(rows, gain):
    return (rows * inverse_of(rows) * gain).astype(BF16)


def normalize_back(rows, gain, d_normed):
    inverse = inverse_of(rows)
    scaled = d_normed * gain
    shared = jnp.mean(scaled * rows, axis=-1, keepdims=True)
    return inverse * scaled - rows * (inverse * inverse * inverse * shared)


def stacked(rows, group):
    start = group * SHARED * HEAD
    return jnp.concatenate(
        [rows[:, start + k * HEAD : start + (k + 1) * HEAD] for k in range(SHARED)], axis=0
    )


def side_by_side(rows):
    return jnp.concatenate([rows[k * SEG : (k + 1) * SEG] for k in range(SHARED)], axis=1)


def of_group(rows, group):
    return rows[:, group * HEAD : (group + 1) * HEAD]


def weights_of(queries, keys, allowed):
    scores = jnp.where(allowed, mul_nt(queries, keys), -1e30)
    raised = jnp.exp(scores - jnp.max(scores, axis=-1, keepdims=True))
    return raised / jnp.sum(raised, axis=-1, keepdims=True)


def attend_back(weights, rounded, queries, keys, values, d_context):
    d_values = mul_tn(rounded, d_context)
    d_weights = mul_nt(d_context, values).astype(BF16).astype(F32)
    pulled = jnp.sum(d_weights * weights, axis=-1, keepdims=True)
    d_scores = (weights * (d_weights - pulled)).astype(BF16)
    return mul(d_scores, keys).astype(BF16), mul_tn(d_scores, queries), d_values


def write_kernel(
    length_ref, x_ref, wq_ref, wk_ref, wv_ref, wo_ref, gain_ref, vector_ref, bias_ref, start_ref,
    q_ref, k_ref, v_ref, left_ref, sq_ref, p_ref, context_ref, written_ref, retain_ref,
    added_ref,
):
    length = length_ref[0, 0]
    gain = gain_ref[...]
    xn = normalize(x_ref[...].astype(F32), gain)
    sn = normalize(start_ref[...].astype(F32), gain)
    left = jnp.concatenate([xn, sn], axis=0)
    left_ref[...] = left
    both = (mul(left, wq_ref[...]) * score_scale).astype(BF16)
    q_ref[...] = both[:SEG]
    sq = both[SEG:]
    sq_ref[...] = sq
    keys = mul(xn, wk_ref[...]).astype(BF16)
    values = mul(xn, wv_ref[...]).astype(BF16)
    k_ref[...] = keys
    v_ref[...] = values
    allowed = lax.broadcasted_iota(jnp.int32, (SHARED * SEG, SEG), 1) < length
    contexts = []
    for group in range(GROUPS):
        weights = weights_of(stacked(sq, group), of_group(keys, group), allowed).astype(BF16)
        p_ref[group] = weights
        contexts.append(side_by_side(mul(weights, of_group(values, group)).astype(BF16)))
    context = jnp.concatenate(contexts, axis=1)
    context_ref[...] = context
    written = mul(context, wo_ref[...])
    written_ref[...] = written
    bias = jnp.transpose(jnp.broadcast_to(bias_ref[...], (128, 128)))[:, :1]
    logits = jnp.sum(written * vector_ref[...], axis=-1, keepdims=True) + bias
    retain = jax.nn.sigmoid(logits)
    retain_ref[...] = jnp.broadcast_to(retain, (SEG, 128))
    added_ref[...] = (1.0 - retain) * written


def read_kernel(
    length_ref, x_ref, cot_ref, wk_ref, wv_ref, wo_ref, gain_ref, start_ref, scan_ref,
    q_ref, k_ref, v_ref,
    out_ref, memory_ref, mn_ref, context_ref, dr_ref, dq_ref, dk_ref, dv_ref, dmk_ref, dmv_ref,
    r_ref,
):
    length = length_ref[0, 0]
    gain = gain_ref[...]
    memory = scan_ref[:, 1024:1025] * start_ref[...].astype(F32) + scan_ref[:, :1024]
    memory_ref[...] = memory
    mn = normalize(memory, gain)
    mn_ref[...] = mn
    keys = jnp.concatenate([mul(mn, wk_ref[...]).astype(BF16), k_ref[...]], axis=0)
    values = jnp.concatenate([mul(mn, wv_ref[...]).astype(BF16), v_ref[...]], axis=0)
    valid = lax.broadcasted_iota(jnp.int32, (SEG, 1024), 0) < length
    d_result = jnp.where(valid, cot_ref[...].astype(F32), 0.0).astype(BF16)
    dr_ref[...] = d_result
    d_context = mul_nt(d_result, wo_ref[...]).astype(BF16)
    shape = (SHARED * SEG, 2 * SEG)
    place = lax.broadcasted_iota(jnp.int32, shape, 1) - SEG
    row = lax.rem(lax.broadcasted_iota(jnp.int32, shape, 0), SEG)
    allowed = (place < 0) | ((place <= row) & (place < length))
    queries = q_ref[...]
    contexts, d_queries, d_keys, d_values = [], [], [], []
    for group in range(GROUPS):
        q, k, v = stacked(queries, group), of_group(keys, group), of_group(values, group)
        weights = weights_of(q, k, allowed)
        rounded = weights.astype(BF16)
        contexts.append(side_by_side(mul(rounded, v).astype(BF16)))
        dq, dk, dv = attend_back(weights, rounded, q, k, v, stacked(d_context, group))
        d_queries.append(side_by_side(dq))
        d_keys.append(dk.astype(BF16))
        d_values.append(dv.astype(BF16))
    context = jnp.concatenate(contexts, axis=1)
    context_ref[...] = context
    out_ref[...] = (x_ref[...].astype(F32) + mul(context, wo_ref[...])).astype(BF16)
    dq_ref[...] = jnp.concatenate(d_queries, axis=1)
    d_key = jnp.concatenate(d_keys, axis=1)
    d_value = jnp.concatenate(d_values, axis=1)
    dmk_ref[...] = d_key[:SEG]
    dmv_ref[...] = d_value[:SEG]
    dk_ref[...] = d_key[SEG:]
    dv_ref[...] = d_value[SEG:]
    d_mn = mul_nt(d_key[:SEG], wk_ref[...]) + mul_nt(d_value[:SEG], wv_ref[...])
    r_ref[...] = normalize_back(memory, gain, d_mn.astype(BF16).astype(F32))


def local_kernel(kernel, shapes, operands, name):
    smem = pl.BlockSpec(memory_space=pltpu.SMEM)
    return pl.pallas_call(
        kernel,
        out_shape=[jax.ShapeDtypeStruct(shape, dtype) for shape, dtype in shapes],
        in_specs=[smem if a.dtype == jnp.int32 else VMEM_SPEC for a in operands],
        out_specs=[VMEM_SPEC] * len(shapes),
        compiler_params=pltpu.CompilerParams(vmem_limit_bytes=60 << 20),
        name=name,
    )(*operands)


def per_device(
    segments,
    lengths,
    query_weight,
    key_weight,
    value_weight,
    out_weight,
    norm_gain,
    gate_vector,
    gate_bias,
    memory_init,
    cotangent,
):
    segment, cot = segments[0, 0], cotangent[0, 0]
    gain, vector, bias = norm_gain[None], gate_vector[None], gate_bias[None]
    wide, narrow = ((SEG, 1024), BF16), ((SEG, 256), BF16)
    full, double = ((SEG, 1024), F32), ((2 * SEG, 1024), BF16)
    q, k, v, left, sq, p, cw, written, retain, added = local_kernel(
        write_kernel,
        [wide, narrow, narrow, double, wide, ((GROUPS, SHARED * SEG, SEG), BF16), wide, full,
         ((SEG, 128), F32), full],
        (lengths, segment, query_weight, key_weight, value_weight, out_weight, gain, vector, bias,
         memory_init),
        "write_forward",
    )
    scan = entering(retain, added, False)
    output, memory, mn, cr, dr, dq, dk, dv, dmk, dmv, r = local_kernel(
        read_kernel,
        [wide, full, wide, wide, wide, wide, narrow, narrow, narrow, narrow, full],
        (lengths, segment, cot, key_weight, value_weight, out_weight, gain, memory_init, scan, q,
         k, v),
        "read_both",
    )
    later = entering(retain, r, True)
    summed = sum_over_devices(
        later, memory, written, retain, vector, query_weight, out_weight, gain, memory_init, scan,
        r, p, sq, k, v, left, mn, cr, cw, dr, dq, dk, dv, dmk, dmv, key_weight, value_weight,
    )
    grad_query, grad_out, grad_key, grad_value, grad_gain, grad_gate, grad_memory = local_kernel(
        finish_kernel,
        [((4, n), F32) for n in (1024, 1024, 256, 256)]
        + [((1, 4), F32), ((1, 4), F32), ((4, 128), F32)],
        (summed,),
        "finish",
    )
    grad_gain, grad_gate, grad_memory = grad_gain[0], grad_gate[0], grad_memory.T
    return (
        output[None, None],
        grad_query,
        grad_key,
        grad_value,
        grad_out,
        grad_gain,
        grad_gate,
        grad_memory,
    )


def solution(mesh):
    split = Mesh(mesh.devices.reshape(4, 4, 2, 2, 4), AXES)
    rows = P(("zh", "y"), ("zl", "x", "c"), None, None)
    return jax.shard_map(
        per_device,
        mesh=split,
        in_specs=(rows, P(("zh", "y"), ("zl", "x", "c"))) + (P(),) * 8 + (rows,),
        out_specs=(
            rows,
            P(AXES, None),
            P(AXES, None),
            P(AXES, None),
            P(AXES, None),
            P(AXES),
            P(AXES),
            P(None, AXES),
        ),
        check_vma=False,
    )
```

```python
import functools

import jax
import jax.numpy as jnp
from jax import lax
from jax.experimental import pallas as pl
from jax.experimental.pallas import tpu as pltpu
from jax.sharding import Mesh
from jax.sharding import PartitionSpec as P

HEAD = 64
F32, BF16 = jnp.float32, jnp.bfloat16
AXES = ("zl", "x", "c", "zh", "y")
MESH = pl.DeviceIdType.MESH
VMEM_SPEC = pl.BlockSpec(memory_space=pltpu.VMEM)


def z_shift(step):
    place = lax.rem(lax.axis_index("zh") * 4 + lax.axis_index("zl") + step, 8)
    return {"zh": lax.div(place, 4), "zl": lax.rem(place, 4)}


def shift(axis, step):
    if axis == "z":
        return z_shift(step % 8)
    return {axis: lax.rem(lax.axis_index(axis) + step % 4, 4)}


def place_of(axis):
    return lax.axis_index("zl" if axis == "z" else axis)


def remote(source, target, send, receive, device):
    return pltpu.make_async_remote_copy(
        src_ref=source,
        dst_ref=target,
        send_sem=send,
        recv_sem=receive,
        device_id=device,
        device_id_type=MESH,
    )


class Ring:
    def __init__(self, axis, work, landing, out, send, receive):
        self.work, self.landing, self.out = work, landing, out
        self.send, self.receive = send, receive
        self.me = place_of(axis)
        self.up, self.down = shift(axis, 1), shift(axis, -1)
        self.copies = []

    def at(self, step):
        return lax.rem(self.me + step, 4)

    def push(self, half, step, device):
        slot = len(self.copies)
        copy = remote(
            self.work.at[half, self.at(step)],
            self.landing.at[slot],
            self.send.at[slot],
            self.receive.at[slot],
            device,
        )
        copy.start()
        self.copies.append(copy)

    def first(self):
        self.push(0, 2, self.up)
        self.push(1, 2, self.down)
        self.push(1, 1, self.up)
        self.push(0, 3, self.down)

    def second(self):
        for half, step, device in ((0, 1, self.up), (1, 3, self.down)):
            self.copies[half].wait_recv()
            self.work[half, self.at(step)] += self.landing[half]
            self.push(half, step, device)

    def finish(self):
        for slot in range(2, 6):
            self.copies[slot].wait_recv()
        self.out[0] = self.work[0, self.me] + self.landing[3] + self.landing[4]
        self.out[1] = self.work[1, self.me] + self.landing[2] + self.landing[5]

    def drain(self):
        for copy in self.copies:
            copy.wait_send()


class Direct:
    def __init__(self, axis, work, landing, out, send, receive):
        self.work, self.landing, self.out = work, landing, out
        self.send, self.receive = send, receive
        self.me = place_of(axis)
        self.steps = ((2, shift(axis, 2)), (1, shift(axis, 1)), (3, shift(axis, -1)))
        self.copies = []

    def first(self):
        for slot, (step, device) in enumerate(self.steps):
            copy = remote(
                self.work.at[:, lax.rem(self.me + step, 4)],
                self.landing.at[slot],
                self.send.at[slot],
                self.receive.at[slot],
                device,
            )
            copy.start()
            self.copies.append(copy)

    def second(self):
        pass

    def finish(self):
        for copy in self.copies:
            copy.wait_recv()
        self.out[...] = (
            self.work[:, self.me] + self.landing[0] + self.landing[1] + self.landing[2]
        )

    def drain(self):
        for copy in self.copies:
            copy.wait_send()


ORDERS = (
    ("y", "z", "x"), ("y", "z", "x"), ("z", "x", "y"),
    ("x", "y", "z"), ("x", "z", "y"), ("z", "x", "y"),
)
WIDTHS = (512, 512, 512, 512, 512, 256)
TOTAL = 2816


def sum_kernel(*refs):
    (
        later_ref, memory_ref, written_ref, retain_ref, vector_ref, gain,
        start_ref, scan_ref, r_ref, p_ref, sq_ref, k_ref, v_ref, left, mn_ref,
        cr_ref, cw_ref, dr_ref, dq_ref, dk_ref, dv_ref, dmk_ref, dmv_ref, wk, wv, wo, wq,
    ) = refs[:27]
    out_ref, refs = refs[27], refs[28:]
    wo_ref, wq_ref, right, context, d_out, normed, pair, rest, *refs = refs
    products, refs = refs[:5], refs[5:]
    landed, refs = refs[:6], refs[6:]
    works, refs = refs[:6], refs[6:]
    rings_of, refs = refs[:36], refs[36:]
    rows_of, refs = refs[:2], refs[2:]
    sent, mate, fold_in, refs = refs[:2], refs[2:4], refs[4:6], refs[6:]
    core_send, core_receive, ring_send, ring_receive, fold_sems, row_sems = refs
    core = lax.axis_index("c")
    other = {"c": 1 - core}
    far = z_shift(4)
    place = lax.axis_index(AXES)
    base = pl.ds(pl.multiple_of(lax.div(place, 4) * 16, 16), 16)
    row_copies = [
        pltpu.make_async_copy(w.at[base], rows, row_sems.at[k])
        for k, (w, rows) in enumerate(zip((wk, wv), rows_of))
    ]
    whole_copies = [
        pltpu.make_async_copy(wo, wo_ref, row_sems.at[2]),
        pltpu.make_async_copy(wq, wq_ref, row_sems.at[3]),
    ]
    for copy in whole_copies + row_copies:
        copy.start()
    peers = [other, far, shift("x", 2), shift("y", 2), shift("z", 2), shift("z", -2)]
    peers += [shift(axis, step) for axis in ("x", "y", "z") for step in (1, -1)]
    barrier = pltpu.get_barrier_semaphore()
    for device in peers:
        pl.semaphore_signal(barrier, inc=1, device_id=device, device_id_type=MESH)
    core_copies = []
    core_of = {}

    def push_core(part, source, target):
        n = len(core_copies)
        copy = remote(source, target, core_send.at[n], core_receive.at[n], other)
        copy.start()
        core_copies.append(copy)
        core_of.setdefault(part, []).append(copy)

    def product_and_push(part):
        factor, other_factor, start = (
            (left, right, 0),
            (context, d_out, 0),
            (normed, pair, 0),
            (left, right, 512),
            (context, d_out, 512),
        )[part]
        for block in range(4):
            value = mul_tn(
                factor[:, block * 256 : block * 256 + 256], other_factor[:, start : start + 512]
            )
            products[part][block * 4 : block * 4 + 4] = value.reshape(4, 2, 32, 512)
            if not core_copies and block == 0:
                pl.semaphore_wait(barrier, len(peers))
            if block % 2 == 1:
                blocks = pl.ds((block - 1) * 4, 8)
                push_core(part, products[part].at[blocks, 1 - core], landed[part].at[blocks])

    sources = tuple(products) + (rest,)

    def build_part(part):
        order, work = ORDERS[part], works[part]
        half_width = WIDTHS[part] // 2

        def build(zl, carry):
            for x in range(4):
                block = zl * 4 + x
                for col in range(0, WIDTHS[part], 128):
                    cols = pl.ds(col, 128)
                    half = col // half_width
                    to = pl.ds(col % half_width, 128)
                    rows = sources[part][block, core, :, cols] + landed[part][block, :, cols]
                    low = lax.broadcasted_iota(jnp.int32, (8, 128), 0) < 4
                    for pair_at in range(2):
                        a = rows[pair_at * 8 : pair_at * 8 + 8]
                        b = rows[16 + pair_at * 8 : 24 + pair_at * 8]
                        tiles = (
                            jnp.where(low, a, pltpu.roll(b, 4, 0)),
                            jnp.where(low, pltpu.roll(a, 4, 0), b),
                        )
                        for bit in range(2):
                            where = {"z": zl, "x": x, "y": pair_at * 2 + bit}
                            index = (half,) + tuple(where[axis] for axis in order)
                            work[index + (slice(None), to)] = tiles[bit]
            return carry

        lax.fori_loop(0, 4, build, 0)

    rings = {}

    def begin(part):
        for copy in core_of[part]:
            copy.wait_recv()
        build_part(part)
        stages = []
        for stage in range(3):
            n = part * 3 + stage
            stages.append(
                (Direct if stage else Ring)(
                    ORDERS[part][stage],
                    works[part] if stage == 0 else rings_of[2 * (n - 1) + 1],
                    rings_of[2 * n],
                    rings_of[2 * n + 1],
                    ring_send.at[n],
                    ring_receive.at[n],
                )
            )
        rings[part] = stages
        stages[0].first()

    early, late = (1, 4, 2), (0, 3, 5)

    def second(parts, stage):
        for part in parts:
            rings[part][stage].second()

    def finish(parts, stage):
        for part in parts:
            rings[part][stage].finish()
            if stage < 2:
                rings[part][stage + 1].first()

    high = lax.axis_index("zh")
    folds = []

    def fold(parts, which):
        total = jnp.concatenate(
            [rings_of[2 * (part * 3 + 2) + 1][half] for part in parts for half in range(2)],
            axis=1,
        )
        turned = pltpu.roll(total, 4, 0)
        middle = total.shape[1] // 2
        top = lax.broadcasted_iota(jnp.int32, (8, middle), 0) < 4
        straight = jnp.where(top, total[:, :middle], turned[:, middle:])
        crossed = jnp.where(top, turned[:, :middle], total[:, middle:])
        sent[which][...] = jnp.where(high == 1, straight, crossed)
        mate[which][...] = jnp.where(high == 0, straight, crossed)
        copy = remote(
            sent[which], fold_in[which], fold_sems.at[which, 0], fold_sems.at[which, 1], far
        )
        copy.start()
        folds.append(copy)

    later = later_ref[:, :1024]
    written = written_ref[...]
    retain = retain_ref[:, :1]
    d_retain = jnp.sum(later * (memory_ref[...] - written), axis=-1, keepdims=True)
    d_logit = d_retain * retain * (1.0 - retain)
    gate = jnp.sum(written * d_logit, axis=0, keepdims=True)
    d_written = ((1.0 - retain) * later + d_logit * vector_ref[...]).astype(BF16)
    context[:SEG] = cr_ref[...]
    context[SEG:] = cw_ref[...]
    d_out[:SEG] = dr_ref[...]
    d_out[SEG:] = d_written
    product_and_push(1)
    product_and_push(4)
    begin(1)
    begin(4)
    whole_copies[0].wait()
    d_context = mul_nt(d_written, wo_ref[...]).astype(BF16)
    slots, keys, values = sq_ref[...], k_ref[...], v_ref[...]
    d_slots, d_keys, d_values = [], [], []
    for group in range(GROUPS):
        rounded = p_ref[group]
        dq, dk, dv = attend_back(
            rounded.astype(F32), rounded, stacked(slots, group), of_group(keys, group),
            of_group(values, group), stacked(d_context, group),
        )
        d_slots.append(side_by_side(dq))
        d_keys.append(dk.astype(BF16))
        d_values.append(dv.astype(BF16))

    def added(one, two):
        return (one.astype(F32) + two.astype(F32)).astype(BF16)

    scale = jnp.asarray(score_scale, BF16)
    d_slot = jnp.concatenate(d_slots, axis=1) * scale
    pair[:SEG, :256] = added(dk_ref[...], jnp.concatenate(d_keys, axis=1))
    pair[:SEG, 256:] = added(dv_ref[...], jnp.concatenate(d_values, axis=1))
    pair[SEG:, :256] = dmk_ref[...]
    pair[SEG:, 256:] = dmv_ref[...]
    normed[:SEG] = left[:SEG]
    normed[SEG:] = mn_ref[...]
    product_and_push(2)
    right[:SEG] = dq_ref[...] * scale
    right[SEG:] = d_slot
    product_and_push(0)
    begin(2)
    second((1, 4), 0)
    product_and_push(3)
    begin(0)
    begin(3)
    whole_copies[1].wait()
    d_sn = mul_nt(d_slot, wq_ref[...]).astype(BF16).astype(F32)
    start = start_ref[...].astype(F32)
    total = normalize_back(start, gain[...], d_sn) + scan_ref[:, 1024:1025] * r_ref[...]
    gates = jnp.broadcast_to(gate, (128, 1024))
    for block in range(8):
        rows = slice(block * 128, block * 128 + 128)
        blocks = slice(block * 2, block * 2 + 2)
        rest[blocks, :, :, :128] = jnp.transpose(total[:, rows]).reshape(2, 2, 32, 128)
        rest[blocks, :, :, 128:] = jnp.transpose(gates[:, rows]).reshape(2, 2, 32, 128)
    push_core(5, rest.at[:, 1 - core], landed[5])
    second((2,), 0)
    begin(5)
    finish((1, 4), 0)
    second((0, 3), 0)
    finish((2,), 0)
    second((5,), 0)
    finish((1, 4), 1)
    finish((0, 3), 0)
    finish((2,), 1)
    finish((5,), 0)
    finish(early, 2)
    fold(early, 0)
    finish(late, 1)
    finish(late, 2)
    fold(late, 1)
    for copy in core_copies:
        copy.wait_send()
    for stages in rings.values():
        for ring in stages:
            ring.drain()
    for copy in row_copies:
        copy.wait()
    part_of_16 = lax.rem(place, 4)
    weights = []
    for loaded in (wq_ref[base], rows_of[0][...], rows_of[1][...]):
        loaded = loaded.astype(F32)
        tile = jnp.where(part_of_16 >= 2, loaded[8:], loaded[:8])
        weights.append(jnp.where(lax.rem(place, 2) == 1, pltpu.roll(tile, 4, 0), tile))
    spot = place * 4 + lax.broadcasted_iota(jnp.int32, (8, 1024), 0)
    here = lax.broadcasted_iota(jnp.int32, (8, 1024), 1) == spot
    low = lax.broadcasted_iota(jnp.int32, (8, 1), 0) < 4
    gains = jnp.sum(jnp.where(here, gain[...], 0.0), axis=1, keepdims=True)
    gains = jnp.where(low, gains, 1.0)
    pieces = []
    for which in range(2):
        folds[which].wait()
        short = mate[which][...] + fold_in[which][...]
        pieces += [short, pltpu.roll(short, 4, 0)]
    full = jnp.concatenate(pieces, axis=1)
    of_gain = (
        jnp.sum(weights[0] * full[:, 1536:2560], axis=1, keepdims=True)
        + jnp.sum(weights[1] * full[:, 1024:1280], axis=1, keepdims=True)
        + jnp.sum(weights[2] * full[:, 1280:1536], axis=1, keepdims=True)
    ) / gains
    out_ref[:, :TOTAL] = full
    out_ref[:, TOTAL:] = jnp.broadcast_to(of_gain, (8, 128))


def sum_over_devices(*operands):
    tall = pltpu.VMEM((2 * SEG, 1024), BF16)
    scratch = [pltpu.VMEM((1024, 1024), BF16)] * 2 + [tall] * 4 + [pltpu.VMEM((2 * SEG, 512), BF16), pltpu.VMEM((16, 2, 32, 256), F32)]
    scratch += [pltpu.VMEM((16, 2, 32, n), F32) for n in WIDTHS[:5]]
    scratch += [pltpu.VMEM((16, 32, n), F32) for n in WIDTHS]
    scratch += [pltpu.VMEM((2, 4, 4, 4, 8, n // 2), F32) for n in WIDTHS]
    for n in WIDTHS:
        for stage in range(3):
            tail = (4,) * (2 - stage) + (8, n // 2)
            lands = (3, 2) if stage else (6,)
            scratch += [pltpu.VMEM(lands + tail, F32), pltpu.VMEM((2,) + tail, F32)]
    scratch += [pltpu.VMEM((16, n), BF16) for n in (256, 256)]
    scratch += [pltpu.VMEM((8, n), F32) for n in (768, 640)] * 3
    scratch += [
        pltpu.SemaphoreType.DMA((11,)),
        pltpu.SemaphoreType.DMA((11,)),
        pltpu.SemaphoreType.DMA((18, 6)),
        pltpu.SemaphoreType.DMA((18, 6)),
        pltpu.SemaphoreType.DMA((2, 2)),
        pltpu.SemaphoreType.DMA((4,)),
    ]
    return pl.pallas_call(
        sum_kernel,
        out_shape=jax.ShapeDtypeStruct((8, TOTAL + 128), F32),
        in_specs=[VMEM_SPEC] * 23 + [pl.BlockSpec(memory_space=pl.ANY)] * 4,
        out_specs=VMEM_SPEC,
        scratch_shapes=scratch,
        compiler_params=pltpu.CompilerParams(
            collective_id=2, has_side_effects=True, vmem_limit_bytes=60 << 20
        ),
        name="sum_over_devices",
    )(*operands)


def finish_kernel(full, gq, go, gk, gv, gain, gate, memory):
    gq[...] = full[:4, 1536:2560]
    go[...] = full[:4, :1024]
    gk[...] = full[:4, 1024:1280]
    gv[...] = full[:4, 1280:1536]
    memory[...] = full[:4, 2560:2688]
    for ref, start in ((gate, 2688), (gain, TOTAL)):
        rows = jnp.concatenate([full[:, start : start + 128], jnp.zeros((120, 128), F32)], axis=0)
        ref[...] = jnp.transpose(rows)[:1, :4]


WIDE = 1152


def joined(earlier, later):
    keep = later[:, 1024:]
    gain = jnp.concatenate([keep] * 9, axis=1)
    added = jnp.concatenate([later[:, :1024], jnp.zeros_like(keep)], axis=1)
    return gain * earlier + added


def identity_rows(rows):
    return jnp.concatenate(
        [jnp.zeros((rows, 1024), jnp.float32), jnp.ones((rows, 128), jnp.float32)], axis=1
    )


CHUNKS = 2
CORE_ROWS, X_ROWS = 32, 8


def scan_kernel(
    reverse, add_ref, keep_ref, out_ref, own, mate, pair, xs, zs, backs, down, up, far, send,
    receive,
):
    core, x, zl = lax.axis_index("c"), lax.axis_index("x"), lax.axis_index("zl")
    other = {"c": 1 - core}
    x_peers = [{"x": lax.rem(x + k, 4)} for k in (1, 2, 3)]
    z_peers = [{"zl": lax.rem(zl + k, 4)} for k in (1, 2, 3)]
    peers = [other] + x_peers + z_peers
    barrier = pltpu.get_barrier_semaphore()
    for device in peers:
        pl.semaphore_signal(barrier, inc=1, device_id=device, device_id_type=MESH)
    own[:, :1024] = add_ref[...]
    own[:, 1024:] = keep_ref[...]
    pl.semaphore_wait(barrier, len(peers))
    order = (3, 2, 1, 0) if reverse else (0, 1, 2, 3)
    leads = core == (1 if reverse else 0)
    all_copies = []

    def chunk_of(chunk):
        copies = []

        def push(source, target, device):
            n = len(copies)
            copy = remote(source, target, send.at[chunk, n], receive.at[chunk, n], device)
            copy.start()
            copies.append(copy)
            all_copies.append(copy)
            return copy

        def rows_of(start, count):
            return pl.ds(pl.multiple_of(start, count), count)

        mine = rows_of(chunk * 2 * CORE_ROWS + core * CORE_ROWS, CORE_ROWS)
        theirs = rows_of(chunk * 2 * CORE_ROWS + (1 - core) * CORE_ROWS, CORE_ROWS)
        at_x = [rows_of(lax.rem(x + k, 4) * X_ROWS, X_ROWS) for k in range(4)]
        started = push(own.at[theirs], mate.at[chunk], other)
        yield
        started.wait_recv()
        kept, got = own[mine], mate[chunk]
        earlier = jnp.where(leads, kept, got)
        pair[chunk] = joined(earlier, jnp.where(leads, got, kept))
        started = [
            push(pair.at[chunk, at_x[k]], xs.at[chunk, x], x_peers[k - 1]) for k in (2, 1, 3)
        ]
        xs[chunk, x] = pair[chunk, at_x[0]]
        yield
        for copy in started:
            copy.wait_recv()
        inside = {}
        running = None
        for k in order:
            inside[k] = running
            running = xs[chunk, k] if running is None else joined(running, xs[chunk, k])
        zs[chunk, zl] = running
        started = [
            push(zs.at[chunk, zl], zs.at[chunk, zl], z_peers[k - 1])
            for k in ((1, 2, 3) if reverse else (3, 2, 1))
        ]
        yield
        for copy in started:
            copy.wait_recv()
        before = identity_rows(X_ROWS)
        for k in order[:3]:
            passed = k > zl if reverse else k < zl
            before = jnp.where(passed, joined(before, zs[chunk, k]), before)
        for k in order:
            backs[chunk, k] = before if inside[k] is None else joined(before, inside[k])
        started = [
            push(backs.at[chunk, lax.rem(x + k, 4)], down.at[chunk, at_x[0]], x_peers[k - 1])
            for k in (2, 1, 3)
        ]
        down[chunk, at_x[0]] = backs[chunk, x]
        yield
        for copy in started:
            copy.wait_recv()
        lead = down[chunk]
        follow = joined(lead, earlier)
        up[chunk] = jnp.where(leads, follow, lead)
        started = push(up.at[chunk], far.at[chunk], other)
        out_ref[mine] = jnp.where(leads, lead, follow)
        yield
        started.wait_recv()
        out_ref[theirs] = far[chunk]

    running = [chunk_of(chunk) for chunk in range(CHUNKS)]
    for step in range(6):
        for steps in running:
            next(steps, None)
    for copy in all_copies:
        copy.wait_send()


def entering(keep, added, reverse):
    f32 = jnp.float32
    out = pl.pallas_call(
        functools.partial(scan_kernel, reverse),
        out_shape=jax.ShapeDtypeStruct((128, WIDE), f32),
        in_specs=[VMEM_SPEC] * 2,
        out_specs=VMEM_SPEC,
        scratch_shapes=[
            pltpu.VMEM((128, WIDE), f32),
            pltpu.VMEM((CHUNKS, CORE_ROWS, WIDE), f32),
            pltpu.VMEM((CHUNKS, CORE_ROWS, WIDE), f32),
            pltpu.VMEM((CHUNKS, 4, X_ROWS, WIDE), f32),
            pltpu.VMEM((CHUNKS, 4, X_ROWS, WIDE), f32),
            pltpu.VMEM((CHUNKS, 4, X_ROWS, WIDE), f32),
            pltpu.VMEM((CHUNKS, CORE_ROWS, WIDE), f32),
            pltpu.VMEM((CHUNKS, CORE_ROWS, WIDE), f32),
            pltpu.VMEM((CHUNKS, CORE_ROWS, WIDE), f32),
            pltpu.SemaphoreType.DMA((CHUNKS, 11)),
            pltpu.SemaphoreType.DMA((CHUNKS, 11)),
        ],
        compiler_params=pltpu.CompilerParams(
            collective_id=1 if reverse else 0, has_side_effects=True
        ),
        name="suffix" if reverse else "prefix",
    )(added, keep)
    return out


epsilon = 1e-05
score_scale = 0.125
GROUPS, SHARED, SEG = 4, 4, 128


def mul(a, b):
    return lax.dot_general(a, b, (((1,), (0,)), ((), ())), preferred_element_type=F32)


def mul_nt(a, b):
    return lax.dot_general(a, b, (((1,), (1,)), ((), ())), preferred_element_type=F32)


def mul_tn(a, b):
    return lax.dot_general(a, b, (((0,), (0,)), ((), ())), preferred_element_type=F32)


def inverse_of(rows):
    return lax.rsqrt(jnp.mean(rows * rows, axis=-1, keepdims=True) + epsilon)


def normalize(rows, gain):
    return (rows * inverse_of(rows) * gain).astype(BF16)


def normalize_back(rows, gain, d_normed):
    inverse = inverse_of(rows)
    scaled = d_normed * gain
    shared = jnp.mean(scaled * rows, axis=-1, keepdims=True)
    return inverse * scaled - rows * (inverse * inverse * inverse * shared)


def stacked(rows, group):
    start = group * SHARED * HEAD
    return jnp.concatenate(
        [rows[:, start + k * HEAD : start + (k + 1) * HEAD] for k in range(SHARED)], axis=0
    )


def side_by_side(rows):
    return jnp.concatenate([rows[k * SEG : (k + 1) * SEG] for k in range(SHARED)], axis=1)


def of_group(rows, group):
    return rows[:, group * HEAD : (group + 1) * HEAD]


def weights_of(queries, keys, allowed):
    scores = jnp.where(allowed, mul_nt(queries, keys), -1e30)
    raised = jnp.exp(scores - jnp.max(scores, axis=-1, keepdims=True))
    return raised / jnp.sum(raised, axis=-1, keepdims=True)


def attend_back(weights, rounded, queries, keys, values, d_context):
    d_values = mul_tn(rounded, d_context)
    d_weights = mul_nt(d_context, values).astype(BF16).astype(F32)
    pulled = jnp.sum(d_weights * weights, axis=-1, keepdims=True)
    d_scores = (weights * (d_weights - pulled)).astype(BF16)
    return mul(d_scores, keys).astype(BF16), mul_tn(d_scores, queries), d_values


def write_kernel(
    length_ref, x_ref, wq_ref, wk_ref, wv_ref, wo_ref, gain_ref, vector_ref, bias_ref, start_ref,
    q_ref, k_ref, v_ref, left_ref, sq_ref, p_ref, context_ref, written_ref, retain_ref,
    added_ref,
):
    length = length_ref[0, 0]
    gain = gain_ref[...]
    xn = normalize(x_ref[...].astype(F32), gain)
    sn = normalize(start_ref[...].astype(F32), gain)
    left = jnp.concatenate([xn, sn], axis=0)
    left_ref[...] = left
    both = (mul(left, wq_ref[...]) * score_scale).astype(BF16)
    q_ref[...] = both[:SEG]
    sq = both[SEG:]
    sq_ref[...] = sq
    keys = mul(xn, wk_ref[...]).astype(BF16)
    values = mul(xn, wv_ref[...]).astype(BF16)
    k_ref[...] = keys
    v_ref[...] = values
    allowed = lax.broadcasted_iota(jnp.int32, (SHARED * SEG, SEG), 1) < length
    contexts = []
    for group in range(GROUPS):
        weights = weights_of(stacked(sq, group), of_group(keys, group), allowed).astype(BF16)
        p_ref[group] = weights
        contexts.append(side_by_side(mul(weights, of_group(values, group)).astype(BF16)))
    context = jnp.concatenate(contexts, axis=1)
    context_ref[...] = context
    written = mul(context, wo_ref[...])
    written_ref[...] = written
    bias = jnp.transpose(jnp.broadcast_to(bias_ref[...], (128, 128)))[:, :1]
    logits = jnp.sum(written * vector_ref[...], axis=-1, keepdims=True) + bias
    retain = jax.nn.sigmoid(logits)
    retain_ref[...] = jnp.broadcast_to(retain, (SEG, 128))
    added_ref[...] = (1.0 - retain) * written


def read_kernel(
    length_ref, x_ref, cot_ref, wk_ref, wv_ref, wo_ref, gain_ref, start_ref, scan_ref,
    q_ref, k_ref, v_ref,
    out_ref, memory_ref, mn_ref, context_ref, dr_ref, dq_ref, dk_ref, dv_ref, dmk_ref, dmv_ref,
    r_ref,
):
    length = length_ref[0, 0]
    gain = gain_ref[...]
    memory = scan_ref[:, 1024:1025] * start_ref[...].astype(F32) + scan_ref[:, :1024]
    memory_ref[...] = memory
    mn = normalize(memory, gain)
    mn_ref[...] = mn
    keys = jnp.concatenate([mul(mn, wk_ref[...]).astype(BF16), k_ref[...]], axis=0)
    values = jnp.concatenate([mul(mn, wv_ref[...]).astype(BF16), v_ref[...]], axis=0)
    valid = lax.broadcasted_iota(jnp.int32, (SEG, 1024), 0) < length
    d_result = jnp.where(valid, cot_ref[...].astype(F32), 0.0).astype(BF16)
    dr_ref[...] = d_result
    d_context = mul_nt(d_result, wo_ref[...]).astype(BF16)
    shape = (SHARED * SEG, 2 * SEG)
    place = lax.broadcasted_iota(jnp.int32, shape, 1) - SEG
    row = lax.rem(lax.broadcasted_iota(jnp.int32, shape, 0), SEG)
    allowed = (place < 0) | ((place <= row) & (place < length))
    queries = q_ref[...]
    contexts, d_queries, d_keys, d_values = [], [], [], []
    for group in range(GROUPS):
        q, k, v = stacked(queries, group), of_group(keys, group), of_group(values, group)
        weights = weights_of(q, k, allowed)
        rounded = weights.astype(BF16)
        contexts.append(side_by_side(mul(rounded, v).astype(BF16)))
        dq, dk, dv = attend_back(weights, rounded, q, k, v, stacked(d_context, group))
        d_queries.append(side_by_side(dq))
        d_keys.append(dk.astype(BF16))
        d_values.append(dv.astype(BF16))
    context = jnp.concatenate(contexts, axis=1)
    context_ref[...] = context
    out_ref[...] = (x_ref[...].astype(F32) + mul(context, wo_ref[...])).astype(BF16)
    dq_ref[...] = jnp.concatenate(d_queries, axis=1)
    d_key = jnp.concatenate(d_keys, axis=1)
    d_value = jnp.concatenate(d_values, axis=1)
    dmk_ref[...] = d_key[:SEG]
    dmv_ref[...] = d_value[:SEG]
    dk_ref[...] = d_key[SEG:]
    dv_ref[...] = d_value[SEG:]
    d_mn = mul_nt(d_key[:SEG], wk_ref[...]) + mul_nt(d_value[:SEG], wv_ref[...])
    r_ref[...] = normalize_back(memory, gain, d_mn.astype(BF16).astype(F32))


def local_kernel(kernel, shapes, operands, name):
    smem = pl.BlockSpec(memory_space=pltpu.SMEM)
    return pl.pallas_call(
        kernel,
        out_shape=[jax.ShapeDtypeStruct(shape, dtype) for shape, dtype in shapes],
        in_specs=[smem if a.dtype == jnp.int32 else VMEM_SPEC for a in operands],
        out_specs=[VMEM_SPEC] * len(shapes),
        compiler_params=pltpu.CompilerParams(vmem_limit_bytes=60 << 20),
        name=name,
    )(*operands)


def per_device(
    segments,
    lengths,
    query_weight,
    key_weight,
    value_weight,
    out_weight,
    norm_gain,
    gate_vector,
    gate_bias,
    memory_init,
    cotangent,
):
    segment, cot = segments[0, 0], cotangent[0, 0]
    gain, vector, bias = norm_gain[None], gate_vector[None], gate_bias[None]
    wide, narrow = ((SEG, 1024), BF16), ((SEG, 256), BF16)
    full, double = ((SEG, 1024), F32), ((2 * SEG, 1024), BF16)
    q, k, v, left, sq, p, cw, written, retain, added = local_kernel(
        write_kernel,
        [wide, narrow, narrow, double, wide, ((GROUPS, SHARED * SEG, SEG), BF16), wide, full,
         ((SEG, 128), F32), full],
        (lengths, segment, query_weight, key_weight, value_weight, out_weight, gain, vector, bias,
         memory_init),
        "write_forward",
    )
    scan = entering(retain, added, False)
    output, memory, mn, cr, dr, dq, dk, dv, dmk, dmv, r = local_kernel(
        read_kernel,
        [wide, full, wide, wide, wide, wide, narrow, narrow, narrow, narrow, full],
        (lengths, segment, cot, key_weight, value_weight, out_weight, gain, memory_init, scan, q,
         k, v),
        "read_both",
    )
    later = entering(retain, r, True)
    summed = sum_over_devices(
        later, memory, written, retain, vector, gain, memory_init, scan, r, p, sq, k, v, left, mn,
        cr, cw, dr, dq, dk, dv, dmk, dmv, key_weight, value_weight, out_weight, query_weight,
    )
    grad_query, grad_out, grad_key, grad_value, grad_gain, grad_gate, grad_memory = local_kernel(
        finish_kernel,
        [((4, n), F32) for n in (1024, 1024, 256, 256)]
        + [((1, 4), F32), ((1, 4), F32), ((4, 128), F32)],
        (summed,),
        "finish",
    )
    grad_gain, grad_gate, grad_memory = grad_gain[0], grad_gate[0], grad_memory.T
    return (
        output[None, None],
        grad_query,
        grad_key,
        grad_value,
        grad_out,
        grad_gain,
        grad_gate,
        grad_memory,
    )


def solution(mesh):
    split = Mesh(mesh.devices.reshape(4, 4, 2, 2, 4), AXES)
    rows = P(("zh", "y"), ("zl", "x", "c"), None, None)
    return jax.shard_map(
        per_device,
        mesh=split,
        in_specs=(rows, P(("zh", "y"), ("zl", "x", "c"))) + (P(),) * 8 + (rows,),
        out_specs=(
            rows,
            P(AXES, None),
            P(AXES, None),
            P(AXES, None),
            P(AXES, None),
            P(AXES),
            P(AXES),
            P(None, AXES),
        ),
        check_vma=False,
    )
```
